128 devices in a mesh: leaf: 4 (over y), row: 8 (over z, core), col: 4 (over x).
Axes of the slice: x: 4, y: 4, z: 4, core: 2. Of those that a mesh axis runs over, the one named last changes fastest.
Arguments:
- sigma_top: float32 [1024, 1024], P(('leaf', 'row'), 'col')
- panels: float32 [4, 7, 1024, 512], P('leaf', None, 'row', 'col'), may hold values from -0.1875 to 0.1875
- inverse_diag: float32 [4, 7, 512, 512], P('leaf', None, 'col')
- slot_lists: int32 [4, 6, 8], P('leaf'), may hold values from -1 to 11, as said below
- parent_links: int32 [4, 4], P('leaf'), may hold values from 1 to 2
Outputs:
- ancestor_block: float32 [4, 7, 1024, 512], P('leaf', None, 'row', 'col')
- diagonal_block: float32 [4, 7, 512, 512], P('leaf', None, None, 'col')
The draws below stay inside these ranges and needn't reach their ends.
Inputs may be any that keep to these rules, and one draw needn't show every extreme that they name: `slot_lists`: in every row, entries 0 to 3 are 8 to 11 in order (the parent's own tiles); then come 1 to 3 distinct parent ancestor slots, below 8 for supernodes 1 and 2 and below 4 for supernodes 3 to 6; the rest are -1, so every row has padding. `parent_links`: each supernode 3 to 6 has supernode 1 or 2 as its parent. `sigma_top`: symmetric.
All inputs are finite; a program needn't handle non-finite values.
Results may differ from the reference program's by a relative error of at most 0.0001.
Values sent between devices are 32-bit elements; how exact they have to be, the bound alone decides.
A program may use at most 128 MiB of HBM per device.

```python
import jax
import jax.numpy as jnp
from jax import lax

TILE = 128
NA = 8
NJ = 4
NODES = 7
SEC = 4


def draw_sigma_top(key, part):
    order = NA * TILE
    key_noise, key_diag = jax.random.split(key, 2)
    random_part = jax.random.normal(key_noise, (order, order), jnp.float32)
    symmetric = (random_part + random_part.T) * (0.35 / jnp.sqrt(2.0 * order))
    positions = jnp.arange(order)
    identity = (positions[:, None] == positions[None, :]).astype(jnp.float32)
    diagonal_values = jax.random.uniform(key_diag, (order,), jnp.float32, 0.8, 1.3)
    matrix = symmetric + identity * diagonal_values[:, None]
    return matrix


def draw_inverse_diag(key, part):
    order = NJ * TILE
    key_noise, key_diag = jax.random.split(key, 2)
    positions = jnp.arange(order)
    strictly_lower = (positions[:, None] > positions[None, :]).astype(jnp.float32)
    identity = (positions[:, None] == positions[None, :]).astype(jnp.float32)
    off_part = jax.random.normal(key_noise, (SEC, NODES, order, order), jnp.float32) * (0.4 / jnp.sqrt(1.0 * order))
    diagonal_values = jax.random.uniform(key_diag, (SEC, NODES, order), jnp.float32, 0.7, 1.3)
    return off_part * strictly_lower + identity * diagonal_values[..., None]


def draw_slot_lists(key, part):
    key_count, key_score = jax.random.split(key, 2)
    rows_total = NODES - 1
    head_part = jnp.broadcast_to(NA + jnp.arange(NJ, dtype=jnp.int32), (SEC, rows_total, NJ))
    counts = jax.random.randint(key_count, (SEC, rows_total), 1, NA - NJ, dtype=jnp.int32)
    scores = jax.random.randint(key_score, (SEC, rows_total, NA), 0, 2 ** 20, dtype=jnp.int32)
    candidates = jnp.arange(NA, dtype=jnp.int32)
    limits = jnp.where(jnp.arange(rows_total) < 2, NA, NJ).astype(jnp.int32)
    outside = (candidates[None, None, :] >= limits[None, :, None]).astype(jnp.int32)
    sort_keys = outside * 2 ** 26 + scores * NA + candidates[None, None, :]
    ordering = jnp.argsort(sort_keys, axis=-1).astype(jnp.int32)
    tail_picks = ordering[:, :, :NA - NJ]
    tail_positions = jnp.arange(NA - NJ, dtype=jnp.int32)
    tail_part = jnp.where(tail_positions[None, None, :] < counts[:, :, None], tail_picks, -1)
    return jnp.concatenate([head_part, tail_part], axis=-1).astype(jnp.int32)


def plant(array, rng, least, high):
    shape = array.shape
    spot = [jax.random.randint(jax.random.fold_in(rng, axis), (), 0, shape[axis]) for axis in range(len(shape))]
    array = array.at[tuple(spot)].set(least)
    longest = shape.index(max(shape))
    spot[longest] = (spot[longest] + 1) % shape[longest]
    return array.at[tuple(spot)].set(high)


def block_levels(stream_key, shape, shards, smallest, top_value):
    def one(position, parts):
        heights = jax.random.uniform(jax.random.fold_in(jax.random.fold_in(stream_key, 6), position), (parts,), jnp.float32, smallest / len(shards), top_value / len(shards))
        return jnp.repeat(jnp.exp(heights), shape[position] // parts).reshape((-1,) + (1,) * (len(shape) - position - 1))

    level = one(*shards[0])
    for cut in shards[1:]:
        level = level * one(*cut)
    return level


def centred(key, shape, spread, most, cuts=(), kind=jnp.bfloat16):
    values = jax.random.normal(key, shape, jnp.float32) * spread
    if len(cuts) > 0:
        values = block_levels(key, shape, cuts, -0.22, 0.18) * values
    return jnp.clip(values, min=-most, max=most).astype(kind)


def setup_inputs(seed: int = 0) -> dict:
    streams_of = jax.random.split(jax.random.key(seed), 6)
    return {
        "sigma_top": draw_sigma_top(jax.random.fold_in(streams_of[5], 71), 0),
        "panels": centred(streams_of[1], (SEC, NODES, NA * TILE, NJ * TILE), (NA * TILE) ** -0.5, 0.1875, ((0, 4), (2, 8), (3, 4)), jnp.float32),
        "inverse_diag": draw_inverse_diag(jax.random.fold_in(streams_of[5], 71), 0),
        "slot_lists": draw_slot_lists(jax.random.fold_in(streams_of[5], 71), 0),
        "parent_links": plant(jax.random.randint(streams_of[4], (SEC, NODES - 3), 1, 3), jax.random.fold_in(streams_of[4], 1), 1, 2).astype(jnp.int32),
    }


HIGHEST = lax.Precision.HIGHEST


def select_block(extended, picks):
    count_tiles = extended.shape[0] // TILE
    blocks = extended.reshape(count_tiles, TILE, count_tiles, TILE)
    living = picks >= 0
    indices = jnp.maximum(picks, 0).astype(jnp.int32)
    chosen = jnp.take(blocks, indices, axis=0)
    chosen = jnp.take(chosen, indices, axis=2)
    weights = (living[:, None] & living[None, :]).astype(jnp.float32)
    chosen = chosen * weights[:, None, :, None]
    return chosen.reshape(picks.shape[0] * TILE, picks.shape[0] * TILE)


def extend_block(ancestor, product, diagonal):
    upper = jnp.concatenate([ancestor, -product], axis=1)
    lower = jnp.concatenate([-product.T, diagonal], axis=1)
    return jnp.concatenate([upper, lower], axis=0)


def node_step(ancestor, factor_u, gram):
    product = jnp.dot(ancestor, factor_u, precision=HIGHEST, preferred_element_type=jnp.float32)
    diagonal = gram + jnp.dot(factor_u.T, product, precision=HIGHEST, preferred_element_type=jnp.float32)
    return product, diagonal


def reference(sigma_top, panels, inverse_diag, slot_lists, parent_links):
    ancestor_out = []
    diagonal_out = []
    for section in range(SEC):
        picks_all = slot_lists[section]
        living = jnp.concatenate([jnp.ones((1, NA), jnp.bool_), picks_all >= 0], axis=0)
        row_weight = jnp.repeat(living.astype(jnp.float32), TILE, axis=1)
        factors = jnp.einsum("vak,vkj->vaj", panels[section], inverse_diag[section], precision=HIGHEST)
        factors = factors * row_weight[:, :, None]
        grams = jnp.einsum("vki,vkj->vij", inverse_diag[section], inverse_diag[section], precision=HIGHEST)
        extended_list = []
        products = []
        diagonals = []
        for node in range(NODES):
            if node == 0:
                ancestor = sigma_top
            elif node < 3:
                ancestor = select_block(extended_list[0], picks_all[node - 1])
            else:
                parent = parent_links[section, node - 3]
                source = jnp.where(parent == 1, extended_list[1], extended_list[2])
                ancestor = select_block(source, picks_all[node - 1])
            product, diagonal = node_step(ancestor, factors[node], grams[node])
            products.append(-product)
            diagonals.append(diagonal)
            if node < 3:
                extended_list.append(extend_block(ancestor, product, diagonal))
        ancestor_out.append(jnp.stack(products))
        diagonal_out.append(jnp.stack(diagonals))
    return jnp.stack(ancestor_out), jnp.stack(diagonal_out)
```

```python
import jax
import jax.numpy as jnp
from jax import lax
from jax.sharding import PartitionSpec as P

TILE = 128
HIGHEST = lax.Precision.HIGHEST


def mm(a, b):
    return jnp.matmul(a, b, precision=HIGHEST, preferred_element_type=jnp.float32)


def tile_rows(matrix, index, tile):
    return lax.dynamic_slice_in_dim(matrix, index * tile, tile, 0)


def tile_cols(matrix, index, tile):
    return lax.dynamic_slice_in_dim(matrix, index * tile, tile, 1)


def scatter_factor(factor_col, slots, positions, tile):
    tiles = factor_col.reshape(slots.shape[0], tile, factor_col.shape[1])
    hits = slots[:, None] == jnp.arange(positions, dtype=slots.dtype)[None, :]
    present = jnp.any(hits, axis=0)
    source = jnp.argmax(hits, axis=0)
    moved = jnp.take(tiles, source, axis=0)
    moved = jnp.where(present[:, None, None], moved, 0.0)
    return moved.reshape(positions * tile, factor_col.shape[1])


def pick_transposed(column_block, picks, tile):
    tiles = column_block.reshape(-1, tile, tile)
    chosen = jnp.take(tiles, jnp.maximum(picks, 0), axis=0)
    chosen = jnp.where((picks >= 0)[:, None, None], chosen, 0.0)
    return jnp.transpose(chosen, (2, 0, 1)).reshape(tile, picks.shape[0] * tile)


def body(sigma_top, panels, inverse_diag, slot_lists, parent_links):
    tile = TILE
    row_count = lax.axis_size("row")
    col_count = lax.axis_size("col")
    leaf_count = lax.axis_size("leaf")
    r = lax.axis_index("row")
    c = lax.axis_index("col")
    panel = panels[0]
    inverse = inverse_diag[0]
    picks_all = slot_lists[0]
    parents = parent_links[0]
    nodes = panel.shape[0]
    width = inverse.shape[2]
    own_tiles = width // tile
    slot_count = picks_all.shape[1]
    positions = slot_count + own_tiles
    band = width // row_count

    partial_factor = mm(panel, inverse)
    factor_rows = lax.psum(partial_factor, "col")
    living = jnp.concatenate([jnp.ones((1, slot_count), jnp.bool_), picks_all >= 0], axis=0)
    live_here = jnp.take(living, r, axis=1).astype(jnp.float32)
    factor_rows = factor_rows * live_here[:, None, None]
    factor_tile = lax.dynamic_slice_in_dim(factor_rows, c * tile, tile, 2)
    factor_cols = lax.all_gather(factor_tile, "row", axis=1, tiled=True)

    inverse_band = lax.dynamic_slice_in_dim(inverse, r * band, band, 2)
    partial_gram = mm(jnp.transpose(inverse_band, (0, 2, 1)), inverse)
    gram_piece = lax.psum_scatter(partial_gram, "col", scatter_dimension=2, tiled=True)

    local_rows, local_cols = sigma_top.shape
    gathered = lax.all_gather(sigma_top, ("leaf", "row", "col"), axis=0)
    sigma = gathered.reshape(leaf_count * row_count, col_count, local_rows, local_cols)
    sigma = jnp.transpose(sigma, (0, 2, 1, 3)).reshape(
        leaf_count * row_count * local_rows, col_count * local_cols
    )

    def diag_partial(first, products):
        rows = factor_rows[first:first + products.shape[0]]
        return mm(jnp.transpose(rows, (0, 2, 1)), products)

    def reduce_and_gather(first, products):
        count = products.shape[0]
        piece = lax.psum_scatter(diag_partial(first, products), "row", scatter_dimension=1, tiled=True)
        piece = piece + gram_piece[first:first + count]
        both = jnp.concatenate([products, piece], axis=1)
        everything = lax.all_gather(both, ("row", "col"), axis=0)
        everything = everything.reshape(row_count, col_count, count, tile + band, tile)
        product_full = jnp.transpose(everything[:, :, :, :tile], (2, 0, 3, 1, 4)).reshape(
            count, row_count * tile, col_count * tile
        )
        diag_full = jnp.transpose(everything[:, :, :, tile:], (2, 0, 3, 1, 4)).reshape(
            count, row_count * band, col_count * tile
        )
        return product_full, diag_full

    own_row = jnp.minimum(r, own_tiles - 1)
    upper = r < own_tiles

    product_0 = mm(tile_rows(sigma, r, tile), factor_cols[0])
    product_full_0, diag_full_0 = reduce_and_gather(0, product_0[None])
    product_full_0 = product_full_0[0]
    diag_full_0 = diag_full_0[0]

    level_1 = []
    for node in (1, 2):
        slots = picks_all[node - 1]
        spread = scatter_factor(factor_cols[node], slots, positions, tile)
        top_row = jnp.concatenate(
            [-jnp.transpose(tile_cols(product_full_0, own_row, tile)), tile_rows(diag_full_0, own_row, tile)],
            axis=1,
        )
        source = slots[jnp.maximum(r, own_tiles)]
        source_row = jnp.maximum(source, 0)
        low_row = jnp.concatenate(
            [tile_rows(sigma, source_row, tile), -tile_rows(product_full_0, source_row, tile)], axis=1
        )
        low_row = jnp.where(source >= 0, low_row, 0.0)
        row = jnp.where(upper, top_row, low_row)
        level_1.append(mm(row, spread))
    product_1 = jnp.stack(level_1)
    product_full_1, diag_full_1 = reduce_and_gather(1, product_1)

    level_2 = []
    for node in range(3, nodes):
        slots = picks_all[node - 1]
        parent = parents[node - 3] - 1
        parent_slots = jnp.take(picks_all, parent, axis=0)
        product_p = jnp.take(product_full_1, parent, axis=0)
        diag_p = jnp.take(diag_full_1, parent, axis=0)
        spread = scatter_factor(factor_cols[node], slots, positions, tile)
        top_row = jnp.concatenate(
            [-jnp.transpose(tile_cols(product_p, own_row, tile)), tile_rows(diag_p, own_row, tile)], axis=1
        )
        source = slots[jnp.maximum(r, own_tiles)]
        source_row = jnp.clip(source, 0, own_tiles - 1)
        corner = pick_transposed(
            -tile_cols(product_full_0, source_row, tile), parent_slots[own_tiles:], tile
        )
        low_row = jnp.concatenate(
            [
                tile_rows(diag_full_0, source_row, tile),
                corner,
                -tile_rows(product_p, source_row, tile),
            ],
            axis=1,
        )
        low_row = jnp.where(source >= 0, low_row, 0.0)
        row = jnp.where(upper, top_row, low_row)
        level_2.append(mm(row, spread))
    product_2 = jnp.stack(level_2)
    first_2 = 3
    count_2 = product_2.shape[0]
    gram_rows = jnp.zeros((count_2, width, tile), jnp.float32)
    gram_rows = lax.dynamic_update_slice_in_dim(gram_rows, gram_piece[first_2:first_2 + count_2], r * band, 1)
    diag_2 = lax.psum(diag_partial(first_2, product_2) + gram_rows, "row")

    products = jnp.concatenate([product_0[None], product_1, product_2], axis=0)
    diag_cols = jnp.concatenate(
        [
            tile_cols(diag_full_0, c, tile)[None],
            lax.dynamic_slice_in_dim(diag_full_1, c * tile, tile, 2),
            diag_2,
        ],
        axis=0,
    )
    return (-products)[None], diag_cols[None]


def solution(mesh):
    return jax.shard_map(
        body,
        mesh=mesh,
        in_specs=(
            P(("leaf", "row"), "col"),
            P("leaf", None, "row", "col"),
            P("leaf", None, "col", None),
            P("leaf", None, None),
            P("leaf", None),
        ),
        out_specs=(P("leaf", None, "row", "col"), P("leaf", None, None, "col")),
        check_vma=False,
    )
```

```python
import jax
import jax.numpy as jnp
from jax import lax
from jax.sharding import PartitionSpec as P

TILE = 128
HIGHEST = lax.Precision.HIGHEST


def mm(a, b):
    return jnp.matmul(a, b, precision=HIGHEST, preferred_element_type=jnp.float32)


def tile_rows(matrix, index, tile):
    return lax.dynamic_slice_in_dim(matrix, index * tile, tile, 0)


def tile_cols(matrix, index, tile):
    return lax.dynamic_slice_in_dim(matrix, index * tile, tile, 1)


def scatter_factor(factor_col, slots, positions, tile):
    tiles = factor_col.reshape(slots.shape[0], tile, factor_col.shape[1])
    hits = slots[:, None] == jnp.arange(positions, dtype=slots.dtype)[None, :]
    present = jnp.any(hits, axis=0)
    source = jnp.argmax(hits, axis=0)
    moved = jnp.take(tiles, source, axis=0)
    moved = jnp.where(present[:, None, None], moved, 0.0)
    return moved.reshape(positions * tile, factor_col.shape[1])


def body(sigma_top, panels, inverse_diag, slot_lists, parent_links):
    tile = TILE
    row_count = lax.axis_size("row")
    col_count = lax.axis_size("col")
    leaf_count = lax.axis_size("leaf")
    r = lax.axis_index("row")
    c = lax.axis_index("col")
    panel = panels[0]
    inverse = inverse_diag[0]
    picks_all = slot_lists[0]
    parents = parent_links[0]
    nodes = panel.shape[0]
    width = inverse.shape[2]
    own_tiles = width // tile
    slot_count = picks_all.shape[1]
    positions = slot_count + own_tiles
    band = width // row_count

    partial_factor = mm(panel, inverse)
    factor_rows = lax.psum(partial_factor, "col")
    living = jnp.concatenate([jnp.ones((1, slot_count), jnp.bool_), picks_all >= 0], axis=0)
    live_here = jnp.take(living, r, axis=1).astype(jnp.float32)
    factor_rows = factor_rows * live_here[:, None, None]
    factor_tile = lax.dynamic_slice_in_dim(factor_rows, c * tile, tile, 2)
    factor_cols = lax.all_gather(factor_tile, "row", axis=1, tiled=True)

    inverse_band = lax.dynamic_slice_in_dim(inverse, r * band, band, 2)
    partial_gram = mm(jnp.transpose(inverse_band, (0, 2, 1)), inverse)
    gram_piece = lax.psum_scatter(partial_gram, "col", scatter_dimension=2, tiled=True)

    local_rows, local_cols = sigma_top.shape
    gathered = lax.all_gather(sigma_top, ("leaf", "row", "col"), axis=0)
    sigma = gathered.reshape(leaf_count * row_count, col_count, local_rows, local_cols)
    sigma = jnp.transpose(sigma, (0, 2, 1, 3)).reshape(
        leaf_count * row_count * local_rows, col_count * local_cols
    )

    def diag_partial(first, products):
        rows = factor_rows[first:first + products.shape[0]]
        return mm(jnp.transpose(rows, (0, 2, 1)), products)

    def reduce_and_gather(first, products):
        count = products.shape[0]
        piece = lax.psum_scatter(diag_partial(first, products), "row", scatter_dimension=1, tiled=True)
        piece = piece + gram_piece[first:first + count]
        both = jnp.concatenate([products, piece], axis=1)
        everything = lax.all_gather(both, ("row", "col"), axis=0)
        return everything.reshape(row_count, col_count, count, tile + band, tile)

    bands_per_tile = tile // band

    def product_col_t(gathered, node, m):
        tiles = lax.dynamic_index_in_dim(gathered[:, :, :, :tile], m, 1, keepdims=False)
        tiles = lax.dynamic_index_in_dim(tiles, node, 1, keepdims=False)
        return jnp.transpose(tiles, (2, 0, 1)).reshape(tile, -1)

    def product_row(gathered, node, q):
        tiles = lax.dynamic_index_in_dim(gathered[:, :, :, :tile], q, 0, keepdims=False)
        tiles = lax.dynamic_index_in_dim(tiles, node, 1, keepdims=False)
        return jnp.transpose(tiles, (1, 0, 2)).reshape(tile, -1)

    def diag_row(gathered, node, m):
        pieces = lax.dynamic_slice_in_dim(gathered[:, :, :, tile:], m * bands_per_tile, bands_per_tile, 0)
        pieces = lax.dynamic_index_in_dim(pieces, node, 2, keepdims=False)
        return jnp.transpose(pieces, (0, 2, 1, 3)).reshape(tile, -1)

    def diag_col(gathered, m):
        pieces = lax.dynamic_index_in_dim(gathered[:, :, :, tile:], m, 1, keepdims=False)
        return jnp.transpose(pieces, (1, 0, 2, 3)).reshape(pieces.shape[1], -1, tile)

    own_row = jnp.minimum(r, own_tiles - 1)
    upper = r < own_tiles

    product_0 = mm(tile_rows(sigma, r, tile), factor_cols[0])
    gathered_0 = reduce_and_gather(0, product_0[None])

    top_row_1 = jnp.concatenate(
        [-product_col_t(gathered_0, 0, own_row), diag_row(gathered_0, 0, own_row)], axis=1
    )
    level_1 = []
    for node in (1, 2):
        slots = picks_all[node - 1]
        spread = scatter_factor(factor_cols[node], slots, positions, tile)
        source = slots[jnp.maximum(r, own_tiles)]
        source_row = jnp.maximum(source, 0)
        low_row = jnp.concatenate(
            [tile_rows(sigma, source_row, tile), -product_row(gathered_0, 0, source_row)], axis=1
        )
        low_row = jnp.where(source >= 0, low_row, 0.0)
        row = jnp.where(upper, top_row_1, low_row)
        level_1.append(mm(row, spread))
    product_1 = jnp.stack(level_1)
    gathered_1 = reduce_and_gather(1, product_1)

    level_2 = []
    for node in range(3, nodes):
        slots = picks_all[node - 1]
        parent = parents[node - 3] - 1
        parent_slots = jnp.take(picks_all, parent, axis=0)
        spread = scatter_factor(factor_cols[node], slots, positions, tile)
        top_row = jnp.concatenate(
            [-product_col_t(gathered_1, parent, own_row), diag_row(gathered_1, parent, own_row)], axis=1
        )
        source = slots[jnp.maximum(r, own_tiles)]
        source_row = jnp.clip(source, 0, own_tiles - 1)
        corner_tiles = product_col_t(gathered_0, 0, source_row).reshape(tile, slot_count, tile)
        corner_picks = parent_slots[own_tiles:]
        corner = jnp.take(corner_tiles, jnp.maximum(corner_picks, 0), axis=1)
        corner = jnp.where((corner_picks >= 0)[None, :, None], -corner, 0.0).reshape(tile, -1)
        low_row = jnp.concatenate(
            [diag_row(gathered_0, 0, source_row), corner, -product_row(gathered_1, parent, source_row)],
            axis=1,
        )
        low_row = jnp.where(source >= 0, low_row, 0.0)
        row = jnp.where(upper, top_row, low_row)
        level_2.append(mm(row, spread))
    product_2 = jnp.stack(level_2)
    first_2 = 3
    count_2 = product_2.shape[0]
    gram_rows = jnp.zeros((count_2, width, tile), jnp.float32)
    gram_rows = lax.dynamic_update_slice_in_dim(gram_rows, gram_piece[first_2:first_2 + count_2], r * band, 1)
    diag_2 = lax.psum(diag_partial(first_2, product_2) + gram_rows, "row")

    products = jnp.concatenate([product_0[None], product_1, product_2], axis=0)
    diag_cols = jnp.concatenate([diag_col(gathered_0, c), diag_col(gathered_1, c), diag_2], axis=0)
    return (-products)[None], diag_cols[None]


def solution(mesh):
    return jax.shard_map(
        body,
        mesh=mesh,
        in_specs=(
            P(("leaf", "row"), "col"),
            P("leaf", None, "row", "col"),
            P("leaf", None, "col", None),
            P("leaf", None, None),
            P("leaf", None),
        ),
        out_specs=(P("leaf", None, "row", "col"), P("leaf", None, None, "col")),
        check_vma=False,
    )
```

```python
import functools

import jax
import jax.numpy as jnp
from jax import lax
from jax.experimental import pallas as pl
from jax.experimental.pallas import tpu as pltpu
from jax.sharding import PartitionSpec as P

TILE = 128
HIGHEST = lax.Precision.HIGHEST


def mm(a, b):
    return jnp.matmul(a, b, precision=HIGHEST, preferred_element_type=jnp.float32)


def tile_rows(matrix, index, tile):
    return lax.dynamic_slice_in_dim(matrix, index * tile, tile, 0)


def tile_cols(matrix, index, tile):
    return lax.dynamic_slice_in_dim(matrix, index * tile, tile, 1)


def scatter_factor(factor_col, slots, positions, tile):
    tiles = factor_col.reshape(slots.shape[0], tile, factor_col.shape[1])
    hits = slots[:, None] == jnp.arange(positions, dtype=slots.dtype)[None, :]
    present = jnp.any(hits, axis=0)
    source = jnp.argmax(hits, axis=0)
    moved = jnp.take(tiles, source, axis=0)
    moved = jnp.where(present[:, None, None], moved, 0.0)
    return moved.reshape(positions * tile, factor_col.shape[1])


def dot_hi(a, b):
    return jnp.dot(a, b, precision=HIGHEST, preferred_element_type=jnp.float32)


def dot_t_hi(a, b):
    return lax.dot_general(
        a, b, (((0,), (0,)), ((), ())), precision=HIGHEST, preferred_element_type=jnp.float32
    )


def level_kernel(info_ref, par_ref, low_ref, fac_ref, out_ref, *, level, tile, band, own_tiles, slot_count):
    count = out_ref.shape[0]
    split = tile // band
    r = info_ref[0]
    own = jnp.minimum(r, own_tiles - 1)

    def p_tile(ref, node, q, m):
        return ref[q, m, node, 0:tile, :]

    def d_tile(ref, node, a, m):
        return jnp.concatenate([ref[a * split + h, m, node, tile:tile + band, :] for h in range(split)], axis=0)

    for i in range(count):
        base = 1 + i * slot_count
        parent = info_ref[1 + count * slot_count + i]
        factor = [fac_ref[i, k * tile:(k + 1) * tile, :] for k in range(slot_count)]
        picks = [jnp.clip(info_ref[base + k], 0, slot_count - 1) for k in range(slot_count)]
        source = info_ref[base + jnp.maximum(r, own_tiles)]

        @pl.when(r < own_tiles)
        def _():
            acc = dot_hi(d_tile(par_ref, parent, own, 0), factor[0])
            for k in range(1, own_tiles):
                acc += dot_hi(d_tile(par_ref, parent, own, k), factor[k])
            for k in range(own_tiles, slot_count):
                acc -= dot_t_hi(p_tile(par_ref, parent, picks[k], own), factor[k])
            out_ref[i] = acc

        @pl.when(jnp.logical_and(r >= own_tiles, source >= 0))
        def _():
            if level == 1:
                s = jnp.clip(source, 0, slot_count - 1)
                start = pl.multiple_of(s * tile, tile)
                acc = -dot_hi(p_tile(par_ref, parent, s, 0), factor[0])
                for k in range(1, own_tiles):
                    acc -= dot_hi(p_tile(par_ref, parent, s, k), factor[k])
                for k in range(own_tiles, slot_count):
                    acc += dot_hi(low_ref[picks[k], pl.ds(start, tile), :], factor[k])
            else:
                s = jnp.clip(source, 0, own_tiles - 1)
                acc = -dot_hi(p_tile(par_ref, parent, s, 0), factor[0])
                for k in range(1, own_tiles):
                    acc -= dot_hi(p_tile(par_ref, parent, s, k), factor[k])
                for k in range(own_tiles, slot_count):
                    q = jnp.minimum(picks[k], own_tiles - 1)
                    acc += dot_hi(d_tile(low_ref, 0, s, q), factor[k])
            out_ref[i] = acc

        @pl.when(jnp.logical_and(r >= own_tiles, source < 0))
        def _():
            out_ref[i] = jnp.zeros((tile, tile), jnp.float32)


def level_products(info, parent_data, low_data, factors, level, tile, band, own_tiles, slot_count):
    kernel = functools.partial(
        level_kernel, level=level, tile=tile, band=band, own_tiles=own_tiles, slot_count=slot_count
    )
    vmem = pl.BlockSpec(memory_space=pltpu.VMEM)
    return pl.pallas_call(
        kernel,
        out_shape=jax.ShapeDtypeStruct((factors.shape[0], tile, tile), jnp.float32),
        in_specs=[pl.BlockSpec(memory_space=pltpu.SMEM), vmem, vmem, vmem],
        out_specs=vmem,
    )(info, parent_data, low_data, factors)


def body(sigma_top, panels, inverse_diag, slot_lists, parent_links):
    tile = TILE
    row_count = lax.axis_size("row")
    col_count = lax.axis_size("col")
    leaf_count = lax.axis_size("leaf")
    r = lax.axis_index("row")
    c = lax.axis_index("col")
    panel = panels[0]
    inverse = inverse_diag[0]
    picks_all = slot_lists[0]
    parents = parent_links[0]
    nodes = panel.shape[0]
    width = inverse.shape[2]
    own_tiles = width // tile
    slot_count = picks_all.shape[1]
    positions = slot_count + own_tiles
    band = width // row_count

    partial_factor = mm(panel, inverse)
    factor_rows = lax.psum(partial_factor, "col")
    living = jnp.concatenate([jnp.ones((1, slot_count), jnp.bool_), picks_all >= 0], axis=0)
    live_here = jnp.take(living, r, axis=1).astype(jnp.float32)
    factor_rows = factor_rows * live_here[:, None, None]
    factor_tile = lax.dynamic_slice_in_dim(factor_rows, c * tile, tile, 2)
    factor_cols = lax.all_gather(factor_tile, "row", axis=1, tiled=True)

    inverse_band = lax.dynamic_slice_in_dim(inverse, r * band, band, 2)
    partial_gram = mm(jnp.transpose(inverse_band, (0, 2, 1)), inverse)
    gram_piece = lax.psum_scatter(partial_gram, "col", scatter_dimension=2, tiled=True)

    local_rows, local_cols = sigma_top.shape
    gathered = lax.all_gather(sigma_top, ("leaf", "row", "col"), axis=0)
    sigma = gathered.reshape(leaf_count * row_count, col_count, local_rows, local_cols)
    sigma = jnp.transpose(sigma, (0, 2, 1, 3)).reshape(
        leaf_count * row_count * local_rows, col_count * local_cols
    )

    def diag_partial(first, products):
        rows = factor_rows[first:first + products.shape[0]]
        return mm(jnp.transpose(rows, (0, 2, 1)), products)

    def reduce_and_gather(first, products):
        count = products.shape[0]
        piece = lax.psum_scatter(diag_partial(first, products), "row", scatter_dimension=1, tiled=True)
        piece = piece + gram_piece[first:first + count]
        both = jnp.concatenate([products, piece], axis=1)
        everything = lax.all_gather(both, ("row", "col"), axis=0)
        return everything.reshape(row_count, col_count, count, tile + band, tile)

    bands_per_tile = tile // band

    def product_col_t(gathered, node, m):
        tiles = lax.dynamic_index_in_dim(gathered[:, :, :, :tile], m, 1, keepdims=False)
        tiles = lax.dynamic_index_in_dim(tiles, node, 1, keepdims=False)
        return jnp.transpose(tiles, (2, 0, 1)).reshape(tile, -1)

    def product_row(gathered, node, q):
        tiles = lax.dynamic_index_in_dim(gathered[:, :, :, :tile], q, 0, keepdims=False)
        tiles = lax.dynamic_index_in_dim(tiles, node, 1, keepdims=False)
        return jnp.transpose(tiles, (1, 0, 2)).reshape(tile, -1)

    def diag_row(gathered, node, m):
        pieces = lax.dynamic_slice_in_dim(gathered[:, :, :, tile:], m * bands_per_tile, bands_per_tile, 0)
        pieces = lax.dynamic_index_in_dim(pieces, node, 2, keepdims=False)
        return jnp.transpose(pieces, (0, 2, 1, 3)).reshape(tile, -1)

    def diag_col(gathered, m):
        pieces = lax.dynamic_index_in_dim(gathered[:, :, :, tile:], m, 1, keepdims=False)
        return jnp.transpose(pieces, (1, 0, 2, 3)).reshape(pieces.shape[1], -1, tile)

    own_row = jnp.minimum(r, own_tiles - 1)
    upper = r < own_tiles

    product_0 = mm(tile_rows(sigma, r, tile), factor_cols[0])
    gathered_0 = reduce_and_gather(0, product_0[None])

    sigma_tiles = jnp.transpose(sigma.reshape(sigma.shape[0], slot_count, tile), (1, 0, 2))
    info_1 = jnp.concatenate([r.astype(jnp.int32)[None], picks_all[0:2].reshape(-1), jnp.zeros((2,), jnp.int32)])
    product_1 = level_products(
        info_1, gathered_0, sigma_tiles, factor_cols[1:3], 1, tile, band, own_tiles, slot_count
    )
    gathered_1 = reduce_and_gather(1, product_1)

    info_2 = jnp.concatenate(
        [r.astype(jnp.int32)[None], picks_all[2:nodes - 1].reshape(-1), (parents - 1).astype(jnp.int32)]
    )
    product_2 = level_products(
        info_2, gathered_1, gathered_0, factor_cols[3:nodes], 2, tile, band, own_tiles, slot_count
    )
    first_2 = 3
    count_2 = product_2.shape[0]
    gram_rows = jnp.zeros((count_2, width, tile), jnp.float32)
    gram_rows = lax.dynamic_update_slice_in_dim(gram_rows, gram_piece[first_2:first_2 + count_2], r * band, 1)
    diag_2 = lax.psum(diag_partial(first_2, product_2) + gram_rows, "row")

    products = jnp.concatenate([product_0[None], product_1, product_2], axis=0)
    diag_cols = jnp.concatenate([diag_col(gathered_0, c), diag_col(gathered_1, c), diag_2], axis=0)
    return (-products)[None], diag_cols[None]


def solution(mesh):
    return jax.shard_map(
        body,
        mesh=mesh,
        in_specs=(
            P(("leaf", "row"), "col"),
            P("leaf", None, "row", "col"),
            P("leaf", None, "col", None),
            P("leaf", None, None),
            P("leaf", None),
        ),
        out_specs=(P("leaf", None, "row", "col"), P("leaf", None, None, "col")),
        check_vma=False,
    )
```

```python
import functools

import jax
import jax.numpy as jnp
from jax import lax
from jax.experimental import pallas as pl
from jax.experimental.pallas import tpu as pltpu
from jax.sharding import PartitionSpec as P

TILE = 128
HIGHEST = lax.Precision.HIGHEST


def mm(a, b):
    return jnp.matmul(a, b, precision=HIGHEST, preferred_element_type=jnp.float32)


def tile_rows(matrix, index, tile):
    return lax.dynamic_slice_in_dim(matrix, index * tile, tile, 0)


def tile_cols(matrix, index, tile):
    return lax.dynamic_slice_in_dim(matrix, index * tile, tile, 1)


def scatter_factor(factor_col, slots, positions, tile):
    tiles = factor_col.reshape(slots.shape[0], tile, factor_col.shape[1])
    hits = slots[:, None] == jnp.arange(positions, dtype=slots.dtype)[None, :]
    present = jnp.any(hits, axis=0)
    source = jnp.argmax(hits, axis=0)
    moved = jnp.take(tiles, source, axis=0)
    moved = jnp.where(present[:, None, None], moved, 0.0)
    return moved.reshape(positions * tile, factor_col.shape[1])


def dot_hi(a, b):
    return jnp.dot(a, b, precision=HIGHEST, preferred_element_type=jnp.float32)


def dot_t_hi(a, b):
    return lax.dot_general(
        a, b, (((0,), (0,)), ((), ())), precision=HIGHEST, preferred_element_type=jnp.float32
    )


def level_kernel(info_ref, par_ref, low_ref, fac_ref, out_ref, *, level, tile, band, own_tiles, slot_count):
    count = out_ref.shape[0]
    split = tile // band
    r = info_ref[0]
    own = jnp.minimum(r, own_tiles - 1)

    def p_tile(ref, node, q, m):
        return ref[q, m, node, 0:tile, :]

    def d_tile(ref, node, a, m):
        return jnp.concatenate([ref[a * split + h, m, node, tile:tile + band, :] for h in range(split)], axis=0)

    for i in range(count):
        base = 1 + i * slot_count
        parent = info_ref[1 + count * slot_count + i]
        factor = [fac_ref[i, k * tile:(k + 1) * tile, :] for k in range(slot_count)]
        picks = [jnp.clip(info_ref[base + k], 0, slot_count - 1) for k in range(slot_count)]
        source = info_ref[base + jnp.maximum(r, own_tiles)]

        @pl.when(r < own_tiles)
        def _():
            acc = dot_hi(d_tile(par_ref, parent, own, 0), factor[0])
            for k in range(1, own_tiles):
                acc += dot_hi(d_tile(par_ref, parent, own, k), factor[k])
            for k in range(own_tiles, slot_count):
                acc -= dot_t_hi(p_tile(par_ref, parent, picks[k], own), factor[k])
            out_ref[i] = acc

        @pl.when(jnp.logical_and(r >= own_tiles, source >= 0))
        def _():
            if level == 1:
                s = jnp.clip(source, 0, slot_count - 1)
                start = pl.multiple_of(s * tile, tile)
                acc = -dot_hi(p_tile(par_ref, parent, s, 0), factor[0])
                for k in range(1, own_tiles):
                    acc -= dot_hi(p_tile(par_ref, parent, s, k), factor[k])
                for k in range(own_tiles, slot_count):
                    acc += dot_hi(low_ref[picks[k], pl.ds(start, tile), :], factor[k])
            else:
                s = jnp.clip(source, 0, own_tiles - 1)
                acc = -dot_hi(p_tile(par_ref, parent, s, 0), factor[0])
                for k in range(1, own_tiles):
                    acc -= dot_hi(p_tile(par_ref, parent, s, k), factor[k])
                for k in range(own_tiles, slot_count):
                    q = jnp.minimum(picks[k], own_tiles - 1)
                    acc += dot_hi(d_tile(low_ref, 0, s, q), factor[k])
            out_ref[i] = acc

        @pl.when(jnp.logical_and(r >= own_tiles, source < 0))
        def _():
            out_ref[i] = jnp.zeros((tile, tile), jnp.float32)


def level_products(info, parent_data, low_data, factors, level, tile, band, own_tiles, slot_count):
    kernel = functools.partial(
        level_kernel, level=level, tile=tile, band=band, own_tiles=own_tiles, slot_count=slot_count
    )
    vmem = pl.BlockSpec(memory_space=pltpu.VMEM)
    return pl.pallas_call(
        kernel,
        out_shape=jax.ShapeDtypeStruct((factors.shape[0], tile, tile), jnp.float32),
        in_specs=[pl.BlockSpec(memory_space=pltpu.SMEM), vmem, vmem, vmem],
        out_specs=vmem,
    )(info, parent_data, low_data, factors)


def reduce_kernel(x_ref, out_ref, recv_ref, send_sem, recv_sem, back_send, back_recv, *, axis, count, band, gather):
    me = lax.axis_index(axis)
    ids = {name: lax.axis_index(name) for name in ("leaf", "row", "col")}

    def device(peer):
        where = dict(ids)
        where[axis] = peer
        return (where["leaf"], where["row"], where["col"])

    mesh_ids = pl.DeviceIdType.MESH
    barrier = pltpu.get_barrier_semaphore()
    for d in range(1, count):
        pl.semaphore_signal(barrier, inc=1, device_id=device(lax.rem(me + d, count)), device_id_type=mesh_ids)
    pl.semaphore_wait(barrier, count - 1)

    sends = []
    for d in range(1, count):
        peer = lax.rem(me + d, count)
        copy = pltpu.make_async_remote_copy(
            src_ref=x_ref.at[:, pl.ds(pl.multiple_of(peer * band, band), band), :],
            dst_ref=recv_ref.at[d - 1],
            send_sem=send_sem.at[d - 1],
            recv_sem=recv_sem.at[d - 1],
            device_id=device(peer),
            device_id_type=mesh_ids,
        )
        copy.start()
        sends.append(copy)
    for copy in sends:
        copy.wait_recv()
    for copy in sends:
        copy.wait_send()
    own = pl.ds(pl.multiple_of(me * band, band), band)
    total = x_ref[:, own, :]
    for d in range(1, count):
        total = total + recv_ref[d - 1]
    if not gather:
        out_ref[...] = total
        return
    out_ref[:, own, :] = total
    backs = []
    for d in range(1, count):
        peer = lax.rem(me + d, count)
        copy = pltpu.make_async_remote_copy(
            src_ref=out_ref.at[:, own, :],
            dst_ref=out_ref.at[:, own, :],
            send_sem=back_send.at[d - 1],
            recv_sem=back_recv.at[d - 1],
            device_id=device(peer),
            device_id_type=mesh_ids,
        )
        copy.start()
        backs.append(copy)
    for d in range(1, count):
        source = lax.rem(me + count - d, count)
        part = pl.ds(pl.multiple_of(source * band, band), band)
        pltpu.make_async_remote_copy(
            src_ref=out_ref.at[:, part, :],
            dst_ref=out_ref.at[:, part, :],
            send_sem=back_send.at[d - 1],
            recv_sem=back_recv.at[d - 1],
            device_id=device(source),
            device_id_type=mesh_ids,
        ).wait_recv()
    for copy in backs:
        copy.wait_send()


def axis_reduce(x, axis, count, gather, collective_id):
    lead, rows, last = x.shape
    band = rows // count
    kernel = functools.partial(reduce_kernel, axis=axis, count=count, band=band, gather=gather)
    out_rows = rows if gather else band
    vmem = pl.BlockSpec(memory_space=pltpu.VMEM)
    return pl.pallas_call(
        kernel,
        out_shape=jax.ShapeDtypeStruct((lead, out_rows, last), x.dtype),
        in_specs=[vmem],
        out_specs=vmem,
        scratch_shapes=[
            pltpu.VMEM((count - 1, lead, band, last), x.dtype),
            pltpu.SemaphoreType.DMA((count - 1,)),
            pltpu.SemaphoreType.DMA((count - 1,)),
            pltpu.SemaphoreType.DMA((count - 1,)),
            pltpu.SemaphoreType.DMA((count - 1,)),
        ],
        compiler_params=pltpu.CompilerParams(collective_id=collective_id, has_side_effects=True),
    )(x)


def body(sigma_top, panels, inverse_diag, slot_lists, parent_links):
    tile = TILE
    row_count = lax.axis_size("row")
    col_count = lax.axis_size("col")
    leaf_count = lax.axis_size("leaf")
    r = lax.axis_index("row")
    c = lax.axis_index("col")
    panel = panels[0]
    inverse = inverse_diag[0]
    picks_all = slot_lists[0]
    parents = parent_links[0]
    nodes = panel.shape[0]
    width = inverse.shape[2]
    own_tiles = width // tile
    slot_count = picks_all.shape[1]
    positions = slot_count + own_tiles
    band = width // row_count

    partial_factor = mm(panel, inverse)
    factor_rows = lax.psum(partial_factor, "col")
    living = jnp.concatenate([jnp.ones((1, slot_count), jnp.bool_), picks_all >= 0], axis=0)
    live_here = jnp.take(living, r, axis=1).astype(jnp.float32)
    factor_rows = factor_rows * live_here[:, None, None]
    factor_tile = lax.dynamic_slice_in_dim(factor_rows, c * tile, tile, 2)
    factor_cols = lax.all_gather(factor_tile, "row", axis=1, tiled=True)

    inverse_band = lax.dynamic_slice_in_dim(inverse, r * band, band, 2)
    partial_gram = mm(jnp.transpose(inverse_band, (0, 2, 1)), inverse)
    gram_piece = lax.psum_scatter(partial_gram, "col", scatter_dimension=2, tiled=True)

    local_rows, local_cols = sigma_top.shape
    gathered = lax.all_gather(sigma_top, ("leaf", "row", "col"), axis=0)
    sigma = gathered.reshape(leaf_count * row_count, col_count, local_rows, local_cols)
    sigma = jnp.transpose(sigma, (0, 2, 1, 3)).reshape(
        leaf_count * row_count * local_rows, col_count * local_cols
    )

    def diag_partial(first, products):
        rows = factor_rows[first:first + products.shape[0]]
        return mm(jnp.transpose(rows, (0, 2, 1)), products)

    def reduce_and_gather(first, products):
        count = products.shape[0]
        piece = axis_reduce(diag_partial(first, products), "row", row_count, False, first)
        piece = piece + gram_piece[first:first + count]
        both = jnp.concatenate([products, piece], axis=1)
        everything = lax.all_gather(both, ("row", "col"), axis=0)
        return everything.reshape(row_count, col_count, count, tile + band, tile)

    bands_per_tile = tile // band

    def product_col_t(gathered, node, m):
        tiles = lax.dynamic_index_in_dim(gathered[:, :, :, :tile], m, 1, keepdims=False)
        tiles = lax.dynamic_index_in_dim(tiles, node, 1, keepdims=False)
        return jnp.transpose(tiles, (2, 0, 1)).reshape(tile, -1)

    def product_row(gathered, node, q):
        tiles = lax.dynamic_index_in_dim(gathered[:, :, :, :tile], q, 0, keepdims=False)
        tiles = lax.dynamic_index_in_dim(tiles, node, 1, keepdims=False)
        return jnp.transpose(tiles, (1, 0, 2)).reshape(tile, -1)

    def diag_row(gathered, node, m):
        pieces = lax.dynamic_slice_in_dim(gathered[:, :, :, tile:], m * bands_per_tile, bands_per_tile, 0)
        pieces = lax.dynamic_index_in_dim(pieces, node, 2, keepdims=False)
        return jnp.transpose(pieces, (0, 2, 1, 3)).reshape(tile, -1)

    def diag_col(gathered, m):
        pieces = lax.dynamic_index_in_dim(gathered[:, :, :, tile:], m, 1, keepdims=False)
        return jnp.transpose(pieces, (1, 0, 2, 3)).reshape(pieces.shape[1], -1, tile)

    own_row = jnp.minimum(r, own_tiles - 1)
    upper = r < own_tiles

    product_0 = mm(tile_rows(sigma, r, tile), factor_cols[0])
    gathered_0 = reduce_and_gather(0, product_0[None])

    sigma_tiles = jnp.transpose(sigma.reshape(sigma.shape[0], slot_count, tile), (1, 0, 2))
    info_1 = jnp.concatenate([r.astype(jnp.int32)[None], picks_all[0:2].reshape(-1), jnp.zeros((2,), jnp.int32)])
    product_1 = level_products(
        info_1, gathered_0, sigma_tiles, factor_cols[1:3], 1, tile, band, own_tiles, slot_count
    )
    gathered_1 = reduce_and_gather(1, product_1)

    info_2 = jnp.concatenate(
        [r.astype(jnp.int32)[None], picks_all[2:nodes - 1].reshape(-1), (parents - 1).astype(jnp.int32)]
    )
    product_2 = level_products(
        info_2, gathered_1, gathered_0, factor_cols[3:nodes], 2, tile, band, own_tiles, slot_count
    )
    first_2 = 3
    count_2 = product_2.shape[0]
    gram_rows = jnp.zeros((count_2, width, tile), jnp.float32)
    gram_rows = lax.dynamic_update_slice_in_dim(gram_rows, gram_piece[first_2:first_2 + count_2], r * band, 1)
    diag_2 = axis_reduce(diag_partial(first_2, product_2) + gram_rows, "row", row_count, True, 2)

    products = jnp.concatenate([product_0[None], product_1, product_2], axis=0)
    diag_cols = jnp.concatenate([diag_col(gathered_0, c), diag_col(gathered_1, c), diag_2], axis=0)
    return (-products)[None], diag_cols[None]


def solution(mesh):
    return jax.shard_map(
        body,
        mesh=mesh,
        in_specs=(
            P(("leaf", "row"), "col"),
            P("leaf", None, "row", "col"),
            P("leaf", None, "col", None),
            P("leaf", None, None),
            P("leaf", None),
        ),
        out_specs=(P("leaf", None, "row", "col"), P("leaf", None, None, "col")),
        check_vma=False,
    )
```

```python
import functools

import jax
import jax.numpy as jnp
from jax import lax
from jax.experimental import pallas as pl
from jax.experimental.pallas import tpu as pltpu
from jax.sharding import PartitionSpec as P

TILE = 128
HIGHEST = lax.Precision.HIGHEST


def mm(a, b):
    return jnp.matmul(a, b, precision=HIGHEST, preferred_element_type=jnp.float32)


def tile_rows(matrix, index, tile):
    return lax.dynamic_slice_in_dim(matrix, index * tile, tile, 0)


def tile_cols(matrix, index, tile):
    return lax.dynamic_slice_in_dim(matrix, index * tile, tile, 1)


def scatter_factor(factor_col, slots, positions, tile):
    tiles = factor_col.reshape(slots.shape[0], tile, factor_col.shape[1])
    hits = slots[:, None] == jnp.arange(positions, dtype=slots.dtype)[None, :]
    present = jnp.any(hits, axis=0)
    source = jnp.argmax(hits, axis=0)
    moved = jnp.take(tiles, source, axis=0)
    moved = jnp.where(present[:, None, None], moved, 0.0)
    return moved.reshape(positions * tile, factor_col.shape[1])


def dot_hi(a, b):
    return jnp.dot(a, b, precision=HIGHEST, preferred_element_type=jnp.float32)


def dot_t_hi(a, b):
    return lax.dot_general(
        a, b, (((0,), (0,)), ((), ())), precision=HIGHEST, preferred_element_type=jnp.float32
    )


def level_kernel(info_ref, par_ref, low_ref, fac_ref, out_ref, *, level, tile, band, own_tiles, slot_count):
    count = out_ref.shape[0]
    split = tile // band
    r = info_ref[0]
    own = jnp.minimum(r, own_tiles - 1)

    def p_tile(ref, node, q, m):
        return ref[q, m, node, 0:tile, :]

    def d_tile(ref, node, a, m):
        return jnp.concatenate([ref[a * split + h, m, node, tile:tile + band, :] for h in range(split)], axis=0)

    for i in range(count):
        base = 1 + i * slot_count
        parent = info_ref[1 + count * slot_count + i]
        factor = [fac_ref[i, k * tile:(k + 1) * tile, :] for k in range(slot_count)]
        picks = [jnp.clip(info_ref[base + k], 0, slot_count - 1) for k in range(slot_count)]
        source = info_ref[base + jnp.maximum(r, own_tiles)]

        @pl.when(r < own_tiles)
        def _():
            acc = dot_hi(d_tile(par_ref, parent, own, 0), factor[0])
            for k in range(1, own_tiles):
                acc += dot_hi(d_tile(par_ref, parent, own, k), factor[k])
            for k in range(own_tiles, slot_count):
                acc -= dot_t_hi(p_tile(par_ref, parent, picks[k], own), factor[k])
            out_ref[i] = acc

        @pl.when(jnp.logical_and(r >= own_tiles, source >= 0))
        def _():
            if level == 1:
                s = jnp.clip(source, 0, slot_count - 1)
                start = pl.multiple_of(s * tile, tile)
                acc = -dot_hi(p_tile(par_ref, parent, s, 0), factor[0])
                for k in range(1, own_tiles):
                    acc -= dot_hi(p_tile(par_ref, parent, s, k), factor[k])
                for k in range(own_tiles, slot_count):
                    acc += dot_hi(low_ref[picks[k], pl.ds(start, tile), :], factor[k])
            else:
                s = jnp.clip(source, 0, own_tiles - 1)
                acc = -dot_hi(p_tile(par_ref, parent, s, 0), factor[0])
                for k in range(1, own_tiles):
                    acc -= dot_hi(p_tile(par_ref, parent, s, k), factor[k])
                for k in range(own_tiles, slot_count):
                    q = jnp.minimum(picks[k], own_tiles - 1)
                    acc += dot_hi(d_tile(low_ref, 0, s, q), factor[k])
            out_ref[i] = acc

        @pl.when(jnp.logical_and(r >= own_tiles, source < 0))
        def _():
            out_ref[i] = jnp.zeros((tile, tile), jnp.float32)


def level_products(info, parent_data, low_data, factors, level, tile, band, own_tiles, slot_count):
    kernel = functools.partial(
        level_kernel, level=level, tile=tile, band=band, own_tiles=own_tiles, slot_count=slot_count
    )
    vmem = pl.BlockSpec(memory_space=pltpu.VMEM)
    return pl.pallas_call(
        kernel,
        out_shape=jax.ShapeDtypeStruct((factors.shape[0], tile, tile), jnp.float32),
        in_specs=[pl.BlockSpec(memory_space=pltpu.SMEM), vmem, vmem, vmem],
        out_specs=vmem,
    )(info, parent_data, low_data, factors)


def reduce_kernel(x_ref, out_ref, recv_ref, send_sem, recv_sem, back_send, back_recv, *, axis, count, band, gather):
    me = lax.axis_index(axis)
    ids = {name: lax.axis_index(name) for name in ("leaf", "row", "col")}

    def device(peer):
        where = dict(ids)
        where[axis] = peer
        return (where["leaf"], where["row"], where["col"])

    mesh_ids = pl.DeviceIdType.MESH
    barrier = pltpu.get_barrier_semaphore()
    for d in range(1, count):
        pl.semaphore_signal(barrier, inc=1, device_id=device(lax.rem(me + d, count)), device_id_type=mesh_ids)
    pl.semaphore_wait(barrier, count - 1)

    sends = []
    for d in range(1, count):
        peer = lax.rem(me + d, count)
        copy = pltpu.make_async_remote_copy(
            src_ref=x_ref.at[:, pl.ds(pl.multiple_of(peer * band, band), band), :],
            dst_ref=recv_ref.at[d - 1],
            send_sem=send_sem.at[d - 1],
            recv_sem=recv_sem.at[d - 1],
            device_id=device(peer),
            device_id_type=mesh_ids,
        )
        copy.start()
        sends.append(copy)
    for copy in sends:
        copy.wait_recv()
    for copy in sends:
        copy.wait_send()
    own = pl.ds(pl.multiple_of(me * band, band), band)
    total = x_ref[:, own, :]
    for d in range(1, count):
        total = total + recv_ref[d - 1]
    if not gather:
        out_ref[...] = total
        return
    out_ref[:, own, :] = total
    backs = []
    for d in range(1, count):
        peer = lax.rem(me + d, count)
        copy = pltpu.make_async_remote_copy(
            src_ref=out_ref.at[:, own, :],
            dst_ref=out_ref.at[:, own, :],
            send_sem=back_send.at[d - 1],
            recv_sem=back_recv.at[d - 1],
            device_id=device(peer),
            device_id_type=mesh_ids,
        )
        copy.start()
        backs.append(copy)
    for d in range(1, count):
        source = lax.rem(me + count - d, count)
        part = pl.ds(pl.multiple_of(source * band, band), band)
        pltpu.make_async_remote_copy(
            src_ref=out_ref.at[:, part, :],
            dst_ref=out_ref.at[:, part, :],
            send_sem=back_send.at[d - 1],
            recv_sem=back_recv.at[d - 1],
            device_id=device(source),
            device_id_type=mesh_ids,
        ).wait_recv()
    for copy in backs:
        copy.wait_send()


def axis_reduce(x, axis, count, gather, collective_id):
    lead, rows, last = x.shape
    band = rows // count
    kernel = functools.partial(reduce_kernel, axis=axis, count=count, band=band, gather=gather)
    out_rows = rows if gather else band
    vmem = pl.BlockSpec(memory_space=pltpu.VMEM)
    return pl.pallas_call(
        kernel,
        out_shape=jax.ShapeDtypeStruct((lead, out_rows, last), x.dtype),
        in_specs=[vmem],
        out_specs=vmem,
        scratch_shapes=[
            pltpu.VMEM((count - 1, lead, band, last), x.dtype),
            pltpu.SemaphoreType.DMA((count - 1,)),
            pltpu.SemaphoreType.DMA((count - 1,)),
            pltpu.SemaphoreType.DMA((count - 1,)),
            pltpu.SemaphoreType.DMA((count - 1,)),
        ],
        compiler_params=pltpu.CompilerParams(collective_id=collective_id, has_side_effects=True),
    )(x)


def body(sigma_top, panels, inverse_diag, slot_lists, parent_links):
    tile = TILE
    row_count = lax.axis_size("row")
    col_count = lax.axis_size("col")
    leaf_count = lax.axis_size("leaf")
    r = lax.axis_index("row")
    c = lax.axis_index("col")
    panel = panels[0]
    inverse = inverse_diag[0]
    picks_all = slot_lists[0]
    parents = parent_links[0]
    nodes = panel.shape[0]
    width = inverse.shape[2]
    own_tiles = width // tile
    slot_count = picks_all.shape[1]
    positions = slot_count + own_tiles
    band = width // row_count

    partial_factor = mm(panel, inverse)
    factor_rows = axis_reduce(partial_factor, "col", col_count, True, 3)
    living = jnp.concatenate([jnp.ones((1, slot_count), jnp.bool_), picks_all >= 0], axis=0)
    live_here = jnp.take(living, r, axis=1).astype(jnp.float32)
    factor_rows = factor_rows * live_here[:, None, None]
    factor_tile = lax.dynamic_slice_in_dim(factor_rows, c * tile, tile, 2)
    factor_cols = lax.all_gather(factor_tile, "row", axis=1, tiled=True)

    inverse_band = lax.dynamic_slice_in_dim(inverse, r * band, band, 2)
    partial_gram = mm(jnp.transpose(inverse_band, (0, 2, 1)), inverse)
    gram_piece = lax.psum_scatter(partial_gram, "col", scatter_dimension=2, tiled=True)

    local_rows, local_cols = sigma_top.shape
    gathered = lax.all_gather(sigma_top, ("leaf", "row", "col"), axis=0)
    sigma = gathered.reshape(leaf_count * row_count, col_count, local_rows, local_cols)
    sigma = jnp.transpose(sigma, (0, 2, 1, 3)).reshape(
        leaf_count * row_count * local_rows, col_count * local_cols
    )

    def diag_partial(first, products):
        rows = factor_rows[first:first + products.shape[0]]
        return mm(jnp.transpose(rows, (0, 2, 1)), products)

    def reduce_and_gather(first, products):
        count = products.shape[0]
        piece = axis_reduce(diag_partial(first, products), "row", row_count, False, first)
        piece = piece + gram_piece[first:first + count]
        both = jnp.concatenate([products, piece], axis=1)
        everything = lax.all_gather(both, ("row", "col"), axis=0)
        return everything.reshape(row_count, col_count, count, tile + band, tile)

    bands_per_tile = tile // band

    def product_col_t(gathered, node, m):
        tiles = lax.dynamic_index_in_dim(gathered[:, :, :, :tile], m, 1, keepdims=False)
        tiles = lax.dynamic_index_in_dim(tiles, node, 1, keepdims=False)
        return jnp.transpose(tiles, (2, 0, 1)).reshape(tile, -1)

    def product_row(gathered, node, q):
        tiles = lax.dynamic_index_in_dim(gathered[:, :, :, :tile], q, 0, keepdims=False)
        tiles = lax.dynamic_index_in_dim(tiles, node, 1, keepdims=False)
        return jnp.transpose(tiles, (1, 0, 2)).reshape(tile, -1)

    def diag_row(gathered, node, m):
        pieces = lax.dynamic_slice_in_dim(gathered[:, :, :, tile:], m * bands_per_tile, bands_per_tile, 0)
        pieces = lax.dynamic_index_in_dim(pieces, node, 2, keepdims=False)
        return jnp.transpose(pieces, (0, 2, 1, 3)).reshape(tile, -1)

    def diag_col(gathered, m):
        pieces = lax.dynamic_index_in_dim(gathered[:, :, :, tile:], m, 1, keepdims=False)
        return jnp.transpose(pieces, (1, 0, 2, 3)).reshape(pieces.shape[1], -1, tile)

    own_row = jnp.minimum(r, own_tiles - 1)
    upper = r < own_tiles

    product_0 = mm(tile_rows(sigma, r, tile), factor_cols[0])
    gathered_0 = reduce_and_gather(0, product_0[None])

    sigma_tiles = jnp.transpose(sigma.reshape(sigma.shape[0], slot_count, tile), (1, 0, 2))
    info_1 = jnp.concatenate([r.astype(jnp.int32)[None], picks_all[0:2].reshape(-1), jnp.zeros((2,), jnp.int32)])
    product_1 = level_products(
        info_1, gathered_0, sigma_tiles, factor_cols[1:3], 1, tile, band, own_tiles, slot_count
    )
    gathered_1 = reduce_and_gather(1, product_1)

    info_2 = jnp.concatenate(
        [r.astype(jnp.int32)[None], picks_all[2:nodes - 1].reshape(-1), (parents - 1).astype(jnp.int32)]
    )
    product_2 = level_products(
        info_2, gathered_1, gathered_0, factor_cols[3:nodes], 2, tile, band, own_tiles, slot_count
    )
    first_2 = 3
    count_2 = product_2.shape[0]
    gram_rows = jnp.zeros((count_2, width, tile), jnp.float32)
    gram_rows = lax.dynamic_update_slice_in_dim(gram_rows, gram_piece[first_2:first_2 + count_2], r * band, 1)
    diag_2 = axis_reduce(diag_partial(first_2, product_2) + gram_rows, "row", row_count, True, 2)

    products = jnp.concatenate([product_0[None], product_1, product_2], axis=0)
    diag_cols = jnp.concatenate([diag_col(gathered_0, c), diag_col(gathered_1, c), diag_2], axis=0)
    return (-products)[None], diag_cols[None]


def solution(mesh):
    return jax.shard_map(
        body,
        mesh=mesh,
        in_specs=(
            P(("leaf", "row"), "col"),
            P("leaf", None, "row", "col"),
            P("leaf", None, "col", None),
            P("leaf", None, None),
            P("leaf", None),
        ),
        out_specs=(P("leaf", None, "row", "col"), P("leaf", None, None, "col")),
        check_vma=False,
    )
```

```python
import functools

import jax
import jax.numpy as jnp
from jax import lax
from jax.experimental import pallas as pl
from jax.experimental.pallas import tpu as pltpu
from jax.sharding import PartitionSpec as P

TILE = 128
HIGHEST = lax.Precision.HIGHEST


def mm(a, b):
    return jnp.matmul(a, b, precision=HIGHEST, preferred_element_type=jnp.float32)


def tile_rows(matrix, index, tile):
    return lax.dynamic_slice_in_dim(matrix, index * tile, tile, 0)


def tile_cols(matrix, index, tile):
    return lax.dynamic_slice_in_dim(matrix, index * tile, tile, 1)


def scatter_factor(factor_col, slots, positions, tile):
    tiles = factor_col.reshape(slots.shape[0], tile, factor_col.shape[1])
    hits = slots[:, None] == jnp.arange(positions, dtype=slots.dtype)[None, :]
    present = jnp.any(hits, axis=0)
    source = jnp.argmax(hits, axis=0)
    moved = jnp.take(tiles, source, axis=0)
    moved = jnp.where(present[:, None, None], moved, 0.0)
    return moved.reshape(positions * tile, factor_col.shape[1])


def dot_hi(a, b):
    return jnp.dot(a, b, precision=HIGHEST, preferred_element_type=jnp.float32)


def dot_t_hi(a, b):
    return lax.dot_general(
        a, b, (((0,), (0,)), ((), ())), precision=HIGHEST, preferred_element_type=jnp.float32
    )


def level_kernel(info_ref, par_ref, low_ref, fac_ref, out_ref, *rest, level, tile, band, own_tiles, slot_count,
                 par_prow, low_prow, halves):
    count = out_ref.shape[0]
    split = tile // band
    r = info_ref[0]
    own = lax.rem(r, own_tiles)

    def p_tile(ref, prow, node, q, m):
        if prow == tile:
            return ref[q, m, node, 0:tile, :]
        parts = tile // prow
        return jnp.concatenate([ref[q + j * own_tiles, m, node, 0:prow, :] for j in range(parts)], axis=0)

    def d_tile(ref, prow, node, a, m):
        return jnp.concatenate([ref[a * split + h, m, node, prow:prow + band, :] for h in range(split)], axis=0)

    for i in range(count):
        base = 1 + i * slot_count
        parent = info_ref[1 + count * slot_count + i]
        factor = [fac_ref[i, k * tile:(k + 1) * tile, :] for k in range(slot_count)]
        picks = [jnp.clip(info_ref[base + k], 0, slot_count - 1) for k in range(slot_count)]
        source = info_ref[base + jnp.maximum(r, own_tiles)]

        upper = dot_hi(d_tile(par_ref, par_prow, parent, own, 0), factor[0])
        for k in range(1, own_tiles):
            upper += dot_hi(d_tile(par_ref, par_prow, parent, own, k), factor[k])
        for k in range(own_tiles, slot_count):
            pick = picks[k] if par_prow == tile else jnp.minimum(picks[k], own_tiles - 1)
            upper -= dot_t_hi(p_tile(par_ref, par_prow, parent, pick, own), factor[k])

        if halves:
            half_ref = rest[0]
            rows = tile // halves
            which = r // own_tiles
            half = upper[0:rows]
            for j in range(1, halves):
                half = jnp.where(which == j, upper[j * rows:(j + 1) * rows], half)
            half_ref[i] = half

        @pl.when(r < own_tiles)
        def _():
            out_ref[i] = upper

        @pl.when(jnp.logical_and(r >= own_tiles, source >= 0))
        def _():
            if level == 1:
                s = jnp.clip(source, 0, slot_count - 1)
                start = pl.multiple_of(s * tile, tile)
                acc = -dot_hi(p_tile(par_ref, par_prow, parent, s, 0), factor[0])
                for k in range(1, own_tiles):
                    acc -= dot_hi(p_tile(par_ref, par_prow, parent, s, k), factor[k])
                for k in range(own_tiles, slot_count):
                    acc += dot_hi(low_ref[picks[k], pl.ds(start, tile), :], factor[k])
            else:
                s = jnp.clip(source, 0, own_tiles - 1)
                acc = -dot_hi(p_tile(par_ref, par_prow, parent, s, 0), factor[0])
                for k in range(1, own_tiles):
                    acc -= dot_hi(p_tile(par_ref, par_prow, parent, s, k), factor[k])
                for k in range(own_tiles, slot_count):
                    q = jnp.minimum(picks[k], own_tiles - 1)
                    acc += dot_hi(d_tile(low_ref, low_prow, 0, s, q), factor[k])
            out_ref[i] = acc

        @pl.when(jnp.logical_and(r >= own_tiles, source < 0))
        def _():
            out_ref[i] = jnp.zeros((tile, tile), jnp.float32)


def level_products(info, parent_data, low_data, factors, level, tile, band, own_tiles, slot_count,
                   par_prow, low_prow, halves):
    kernel = functools.partial(
        level_kernel, level=level, tile=tile, band=band, own_tiles=own_tiles, slot_count=slot_count,
        par_prow=par_prow, low_prow=low_prow, halves=halves,
    )
    vmem = pl.BlockSpec(memory_space=pltpu.VMEM)
    count = factors.shape[0]
    shapes = [jax.ShapeDtypeStruct((count, tile, tile), jnp.float32)]
    if halves:
        shapes.append(jax.ShapeDtypeStruct((count, tile // halves, tile), jnp.float32))
    return pl.pallas_call(
        kernel,
        out_shape=tuple(shapes),
        in_specs=[pl.BlockSpec(memory_space=pltpu.SMEM), vmem, vmem, vmem],
        out_specs=tuple([vmem] * len(shapes)),
    )(info, parent_data, low_data, factors)


def reduce_kernel(x_ref, out_ref, recv_ref, send_sem, recv_sem, back_send, back_recv, *, axis, count, band, gather):
    me = lax.axis_index(axis)
    ids = {name: lax.axis_index(name) for name in ("leaf", "row", "col")}

    def device(peer):
        where = dict(ids)
        where[axis] = peer
        return (where["leaf"], where["row"], where["col"])

    mesh_ids = pl.DeviceIdType.MESH
    barrier = pltpu.get_barrier_semaphore()
    for d in range(1, count):
        pl.semaphore_signal(barrier, inc=1, device_id=device(lax.rem(me + d, count)), device_id_type=mesh_ids)
    pl.semaphore_wait(barrier, count - 1)

    sends = []
    for d in range(1, count):
        peer = lax.rem(me + d, count)
        copy = pltpu.make_async_remote_copy(
            src_ref=x_ref.at[:, pl.ds(pl.multiple_of(peer * band, band), band), :],
            dst_ref=recv_ref.at[d - 1],
            send_sem=send_sem.at[d - 1],
            recv_sem=recv_sem.at[d - 1],
            device_id=device(peer),
            device_id_type=mesh_ids,
        )
        copy.start()
        sends.append(copy)
    for copy in sends:
        copy.wait_recv()
    for copy in sends:
        copy.wait_send()
    own = pl.ds(pl.multiple_of(me * band, band), band)
    total = x_ref[:, own, :]
    for d in range(1, count):
        total = total + recv_ref[d - 1]
    if not gather:
        out_ref[...] = total
        return
    out_ref[:, own, :] = total
    backs = []
    for d in range(1, count):
        peer = lax.rem(me + d, count)
        copy = pltpu.make_async_remote_copy(
            src_ref=out_ref.at[:, own, :],
            dst_ref=out_ref.at[:, own, :],
            send_sem=back_send.at[d - 1],
            recv_sem=back_recv.at[d - 1],
            device_id=device(peer),
            device_id_type=mesh_ids,
        )
        copy.start()
        backs.append(copy)
    for d in range(1, count):
        source = lax.rem(me + count - d, count)
        part = pl.ds(pl.multiple_of(source * band, band), band)
        pltpu.make_async_remote_copy(
            src_ref=out_ref.at[:, part, :],
            dst_ref=out_ref.at[:, part, :],
            send_sem=back_send.at[d - 1],
            recv_sem=back_recv.at[d - 1],
            device_id=device(source),
            device_id_type=mesh_ids,
        ).wait_recv()
    for copy in backs:
        copy.wait_send()


def axis_reduce(x, axis, count, gather, collective_id):
    lead, rows, last = x.shape
    band = rows // count
    kernel = functools.partial(reduce_kernel, axis=axis, count=count, band=band, gather=gather)
    out_rows = rows if gather else band
    vmem = pl.BlockSpec(memory_space=pltpu.VMEM)
    return pl.pallas_call(
        kernel,
        out_shape=jax.ShapeDtypeStruct((lead, out_rows, last), x.dtype),
        in_specs=[vmem],
        out_specs=vmem,
        scratch_shapes=[
            pltpu.VMEM((count - 1, lead, band, last), x.dtype),
            pltpu.SemaphoreType.DMA((count - 1,)),
            pltpu.SemaphoreType.DMA((count - 1,)),
            pltpu.SemaphoreType.DMA((count - 1,)),
            pltpu.SemaphoreType.DMA((count - 1,)),
        ],
        compiler_params=pltpu.CompilerParams(collective_id=collective_id, has_side_effects=True),
    )(x)


def body(sigma_top, panels, inverse_diag, slot_lists, parent_links):
    tile = TILE
    row_count = lax.axis_size("row")
    col_count = lax.axis_size("col")
    leaf_count = lax.axis_size("leaf")
    r = lax.axis_index("row")
    c = lax.axis_index("col")
    panel = panels[0]
    inverse = inverse_diag[0]
    picks_all = slot_lists[0]
    parents = parent_links[0]
    nodes = panel.shape[0]
    width = inverse.shape[2]
    own_tiles = width // tile
    slot_count = picks_all.shape[1]
    positions = slot_count + own_tiles
    band = width // row_count

    partial_factor = mm(panel, inverse)
    factor_rows = axis_reduce(partial_factor, "col", col_count, True, 3)
    living = jnp.concatenate([jnp.ones((1, slot_count), jnp.bool_), picks_all >= 0], axis=0)
    live_here = jnp.take(living, r, axis=1).astype(jnp.float32)
    factor_rows = factor_rows * live_here[:, None, None]
    factor_tile = lax.dynamic_slice_in_dim(factor_rows, c * tile, tile, 2)
    factor_cols = lax.all_gather(factor_tile, "row", axis=1, tiled=True)

    inverse_band = lax.dynamic_slice_in_dim(inverse, r * band, band, 2)
    partial_gram = mm(jnp.transpose(inverse_band, (0, 2, 1)), inverse)
    gram_piece = lax.psum_scatter(partial_gram, "col", scatter_dimension=2, tiled=True)

    local_rows, local_cols = sigma_top.shape
    gathered = lax.all_gather(sigma_top, ("leaf", "row", "col"), axis=0)
    sigma = gathered.reshape(leaf_count * row_count, col_count, local_rows, local_cols)
    sigma = jnp.transpose(sigma, (0, 2, 1, 3)).reshape(
        leaf_count * row_count * local_rows, col_count * local_cols
    )

    def diag_partial(first, products):
        rows = factor_rows[first:first + products.shape[0]]
        return mm(jnp.transpose(rows, (0, 2, 1)), products)

    def reduce_and_gather(first, products, sent):
        count = products.shape[0]
        piece = axis_reduce(diag_partial(first, products), "row", row_count, False, first)
        piece = piece + gram_piece[first:first + count]
        both = jnp.concatenate([sent, piece], axis=1)
        everything = lax.all_gather(both, ("row", "col"), axis=0)
        return everything.reshape(row_count, col_count, count, sent.shape[1] + band, tile)

    bands_per_tile = tile // band

    def product_col_t(gathered, node, m):
        tiles = lax.dynamic_index_in_dim(gathered[:, :, :, :tile], m, 1, keepdims=False)
        tiles = lax.dynamic_index_in_dim(tiles, node, 1, keepdims=False)
        return jnp.transpose(tiles, (2, 0, 1)).reshape(tile, -1)

    def product_row(gathered, node, q):
        tiles = lax.dynamic_index_in_dim(gathered[:, :, :, :tile], q, 0, keepdims=False)
        tiles = lax.dynamic_index_in_dim(tiles, node, 1, keepdims=False)
        return jnp.transpose(tiles, (1, 0, 2)).reshape(tile, -1)

    def diag_row(gathered, node, m):
        pieces = lax.dynamic_slice_in_dim(gathered[:, :, :, tile:], m * bands_per_tile, bands_per_tile, 0)
        pieces = lax.dynamic_index_in_dim(pieces, node, 2, keepdims=False)
        return jnp.transpose(pieces, (0, 2, 1, 3)).reshape(tile, -1)

    def diag_col(gathered, m):
        pieces = lax.dynamic_index_in_dim(gathered[:, :, :, -band:], m, 1, keepdims=False)
        return jnp.transpose(pieces, (1, 0, 2, 3)).reshape(pieces.shape[1], -1, tile)

    own_row = jnp.minimum(r, own_tiles - 1)
    upper = r < own_tiles

    product_0 = mm(tile_rows(sigma, r, tile), factor_cols[0])
    gathered_0 = reduce_and_gather(0, product_0[None], product_0[None])

    sigma_tiles = jnp.transpose(sigma.reshape(sigma.shape[0], slot_count, tile), (1, 0, 2))
    info_1 = jnp.concatenate([r.astype(jnp.int32)[None], picks_all[0:2].reshape(-1), jnp.zeros((2,), jnp.int32)])
    halves = row_count // own_tiles
    product_1, upper_half = level_products(
        info_1, gathered_0, sigma_tiles, factor_cols[1:3], 1, tile, band, own_tiles, slot_count,
        tile, tile, halves,
    )
    gathered_1 = reduce_and_gather(1, product_1, upper_half)

    info_2 = jnp.concatenate(
        [r.astype(jnp.int32)[None], picks_all[2:nodes - 1].reshape(-1), (parents - 1).astype(jnp.int32)]
    )
    (product_2,) = level_products(
        info_2, gathered_1, gathered_0, factor_cols[3:nodes], 2, tile, band, own_tiles, slot_count,
        tile // halves, tile, 0,
    )
    first_2 = 3
    count_2 = product_2.shape[0]
    gram_rows = jnp.zeros((count_2, width, tile), jnp.float32)
    gram_rows = lax.dynamic_update_slice_in_dim(gram_rows, gram_piece[first_2:first_2 + count_2], r * band, 1)
    diag_2 = axis_reduce(diag_partial(first_2, product_2) + gram_rows, "row", row_count, True, 2)

    products = jnp.concatenate([product_0[None], product_1, product_2], axis=0)
    diag_cols = jnp.concatenate([diag_col(gathered_0, c), diag_col(gathered_1, c), diag_2], axis=0)
    return (-products)[None], diag_cols[None]


def solution(mesh):
    return jax.shard_map(
        body,
        mesh=mesh,
        in_specs=(
            P(("leaf", "row"), "col"),
            P("leaf", None, "row", "col"),
            P("leaf", None, "col", None),
            P("leaf", None, None),
            P("leaf", None),
        ),
        out_specs=(P("leaf", None, "row", "col"), P("leaf", None, None, "col")),
        check_vma=False,
    )
```

```python
import functools

import jax
import jax.numpy as jnp
from jax import lax
from jax.experimental import pallas as pl
from jax.experimental.pallas import tpu as pltpu
from jax.sharding import PartitionSpec as P

TILE = 128
HIGHEST = lax.Precision.HIGHEST


def mm(a, b):
    return jnp.matmul(a, b, precision=HIGHEST, preferred_element_type=jnp.float32)


def tile_rows(matrix, index, tile):
    return lax.dynamic_slice_in_dim(matrix, index * tile, tile, 0)


def tile_cols(matrix, index, tile):
    return lax.dynamic_slice_in_dim(matrix, index * tile, tile, 1)


def scatter_factor(factor_col, slots, positions, tile):
    tiles = factor_col.reshape(slots.shape[0], tile, factor_col.shape[1])
    hits = slots[:, None] == jnp.arange(positions, dtype=slots.dtype)[None, :]
    present = jnp.any(hits, axis=0)
    source = jnp.argmax(hits, axis=0)
    moved = jnp.take(tiles, source, axis=0)
    moved = jnp.where(present[:, None, None], moved, 0.0)
    return moved.reshape(positions * tile, factor_col.shape[1])


def dot_hi(a, b):
    return jnp.dot(a, b, precision=HIGHEST, preferred_element_type=jnp.float32)


def dot_t_hi(a, b):
    return lax.dot_general(
        a, b, (((0,), (0,)), ((), ())), precision=HIGHEST, preferred_element_type=jnp.float32
    )


def level_kernel(info_ref, par_ref, low_ref, fac_ref, out_ref, *rest, level, tile, band, own_tiles, slot_count,
                 par_prow, low_prow, halves):
    count = out_ref.shape[0]
    split = tile // band
    r = info_ref[0]
    own = lax.rem(r, own_tiles)

    def p_tile(ref, prow, node, q, m):
        if prow == tile:
            return ref[q, m, node, 0:tile, :]
        parts = tile // prow
        return jnp.concatenate([ref[q + j * own_tiles, m, node, 0:prow, :] for j in range(parts)], axis=0)

    def d_tile(ref, prow, node, a, m):
        return jnp.concatenate([ref[a * split + h, m, node, prow:prow + band, :] for h in range(split)], axis=0)

    for i in range(count):
        base = 1 + i * slot_count
        parent = info_ref[1 + count * slot_count + i]
        factor = [fac_ref[i, k * tile:(k + 1) * tile, :] for k in range(slot_count)]
        picks = [jnp.clip(info_ref[base + k], 0, slot_count - 1) for k in range(slot_count)]
        source = info_ref[base + jnp.maximum(r, own_tiles)]

        upper = dot_hi(d_tile(par_ref, par_prow, parent, own, 0), factor[0])
        for k in range(1, own_tiles):
            upper += dot_hi(d_tile(par_ref, par_prow, parent, own, k), factor[k])
        for k in range(own_tiles, slot_count):
            pick = picks[k] if par_prow == tile else jnp.minimum(picks[k], own_tiles - 1)
            upper -= dot_t_hi(p_tile(par_ref, par_prow, parent, pick, own), factor[k])

        if halves:
            half_ref = rest[0]
            rows = tile // halves
            which = r // own_tiles
            half = upper[0:rows]
            for j in range(1, halves):
                half = jnp.where(which == j, upper[j * rows:(j + 1) * rows], half)
            half_ref[i] = half

        @pl.when(r < own_tiles)
        def _():
            out_ref[i] = upper

        @pl.when(jnp.logical_and(r >= own_tiles, source >= 0))
        def _():
            if level == 1:
                s = jnp.clip(source, 0, slot_count - 1)
                start = pl.multiple_of(s * tile, tile)
                acc = -dot_hi(p_tile(par_ref, par_prow, parent, s, 0), factor[0])
                for k in range(1, own_tiles):
                    acc -= dot_hi(p_tile(par_ref, par_prow, parent, s, k), factor[k])
                for k in range(own_tiles, slot_count):
                    acc += dot_hi(low_ref[picks[k], pl.ds(start, tile), :], factor[k])
            else:
                s = jnp.clip(source, 0, own_tiles - 1)
                acc = -dot_hi(p_tile(par_ref, par_prow, parent, s, 0), factor[0])
                for k in range(1, own_tiles):
                    acc -= dot_hi(p_tile(par_ref, par_prow, parent, s, k), factor[k])
                for k in range(own_tiles, slot_count):
                    q = jnp.minimum(picks[k], own_tiles - 1)
                    acc += dot_hi(d_tile(low_ref, low_prow, 0, s, q), factor[k])
            out_ref[i] = acc

        @pl.when(jnp.logical_and(r >= own_tiles, source < 0))
        def _():
            out_ref[i] = jnp.zeros((tile, tile), jnp.float32)


def level_products(info, parent_data, low_data, factors, level, tile, band, own_tiles, slot_count,
                   par_prow, low_prow, halves):
    kernel = functools.partial(
        level_kernel, level=level, tile=tile, band=band, own_tiles=own_tiles, slot_count=slot_count,
        par_prow=par_prow, low_prow=low_prow, halves=halves,
    )
    vmem = pl.BlockSpec(memory_space=pltpu.VMEM)
    count = factors.shape[0]
    shapes = [jax.ShapeDtypeStruct((count, tile, tile), jnp.float32)]
    if halves:
        shapes.append(jax.ShapeDtypeStruct((count, tile // halves, tile), jnp.float32))
    return pl.pallas_call(
        kernel,
        out_shape=tuple(shapes),
        in_specs=[pl.BlockSpec(memory_space=pltpu.SMEM), vmem, vmem, vmem],
        out_specs=tuple([vmem] * len(shapes)),
    )(info, parent_data, low_data, factors)


def reduce_kernel(x_ref, out_ref, recv_ref, send_sem, recv_sem, back_send, back_recv, *, axis, count, band, gather):
    me = lax.axis_index(axis)
    ids = {name: lax.axis_index(name) for name in ("leaf", "row", "col")}

    def device(peer):
        where = dict(ids)
        where[axis] = peer
        return (where["leaf"], where["row"], where["col"])

    mesh_ids = pl.DeviceIdType.MESH
    barrier = pltpu.get_barrier_semaphore()
    for d in range(1, count):
        pl.semaphore_signal(barrier, inc=1, device_id=device(lax.rem(me + d, count)), device_id_type=mesh_ids)
    pl.semaphore_wait(barrier, count - 1)

    sends = []
    for d in range(1, count):
        peer = lax.rem(me + d, count)
        copy = pltpu.make_async_remote_copy(
            src_ref=x_ref.at[:, pl.ds(pl.multiple_of(peer * band, band), band), :],
            dst_ref=recv_ref.at[d - 1],
            send_sem=send_sem.at[d - 1],
            recv_sem=recv_sem.at[d - 1],
            device_id=device(peer),
            device_id_type=mesh_ids,
        )
        copy.start()
        sends.append(copy)
    for copy in sends:
        copy.wait_recv()
    for copy in sends:
        copy.wait_send()
    own = pl.ds(pl.multiple_of(me * band, band), band)
    total = x_ref[:, own, :]
    for d in range(1, count):
        total = total + recv_ref[d - 1]
    if not gather:
        out_ref[...] = total
        return
    out_ref[:, own, :] = total
    backs = []
    for d in range(1, count):
        peer = lax.rem(me + d, count)
        copy = pltpu.make_async_remote_copy(
            src_ref=out_ref.at[:, own, :],
            dst_ref=out_ref.at[:, own, :],
            send_sem=back_send.at[d - 1],
            recv_sem=back_recv.at[d - 1],
            device_id=device(peer),
            device_id_type=mesh_ids,
        )
        copy.start()
        backs.append(copy)
    for d in range(1, count):
        source = lax.rem(me + count - d, count)
        part = pl.ds(pl.multiple_of(source * band, band), band)
        pltpu.make_async_remote_copy(
            src_ref=out_ref.at[:, part, :],
            dst_ref=out_ref.at[:, part, :],
            send_sem=back_send.at[d - 1],
            recv_sem=back_recv.at[d - 1],
            device_id=device(source),
            device_id_type=mesh_ids,
        ).wait_recv()
    for copy in backs:
        copy.wait_send()


def axis_reduce(x, axis, count, gather, collective_id):
    lead, rows, last = x.shape
    band = rows // count
    kernel = functools.partial(reduce_kernel, axis=axis, count=count, band=band, gather=gather)
    out_rows = rows if gather else band
    vmem = pl.BlockSpec(memory_space=pltpu.VMEM)
    return pl.pallas_call(
        kernel,
        out_shape=jax.ShapeDtypeStruct((lead, out_rows, last), x.dtype),
        in_specs=[vmem],
        out_specs=vmem,
        scratch_shapes=[
            pltpu.VMEM((count - 1, lead, band, last), x.dtype),
            pltpu.SemaphoreType.DMA((count - 1,)),
            pltpu.SemaphoreType.DMA((count - 1,)),
            pltpu.SemaphoreType.DMA((count - 1,)),
            pltpu.SemaphoreType.DMA((count - 1,)),
        ],
        compiler_params=pltpu.CompilerParams(collective_id=collective_id, has_side_effects=True),
    )(x)


def factor_kernel(x_ref, rows_ref, cols_ref, recv_ref, sems, *, tile):
    r = lax.axis_index("row")
    c = lax.axis_index("col")
    leaf = lax.axis_index("leaf")
    row_count = lax.axis_size("row")
    col_count = lax.axis_size("col")
    mesh_ids = pl.DeviceIdType.MESH
    col_peers = [lax.rem(c + d, col_count) for d in range(1, col_count)]
    row_peers = [lax.rem(r + d, row_count) for d in range(1, row_count)]

    barrier = pltpu.get_barrier_semaphore()
    for peer in col_peers:
        pl.semaphore_signal(barrier, inc=1, device_id=(leaf, r, peer), device_id_type=mesh_ids)
    for peer in row_peers:
        pl.semaphore_signal(barrier, inc=1, device_id=(leaf, peer, c), device_id_type=mesh_ids)
    pl.semaphore_wait(barrier, len(col_peers) + len(row_peers))

    def col_slice(index):
        return pl.ds(pl.multiple_of(index * tile, tile), tile)

    sends = []
    for d, peer in enumerate(col_peers):
        copy = pltpu.make_async_remote_copy(
            src_ref=x_ref.at[:, :, col_slice(peer)],
            dst_ref=recv_ref.at[d],
            send_sem=sems.at[0, d],
            recv_sem=sems.at[1, d],
            device_id=(leaf, r, peer),
            device_id_type=mesh_ids,
        )
        copy.start()
        sends.append(copy)
    for copy in sends:
        copy.wait_recv()
    for copy in sends:
        copy.wait_send()
    total = x_ref[:, :, col_slice(c)]
    for d in range(len(col_peers)):
        total = total + recv_ref[d]
    rows_ref[:, :, col_slice(c)] = total
    cols_ref[:, col_slice(r), :] = total

    sends = []
    for d, peer in enumerate(row_peers):
        copy = pltpu.make_async_remote_copy(
            src_ref=cols_ref.at[:, col_slice(r), :],
            dst_ref=cols_ref.at[:, col_slice(r), :],
            send_sem=sems.at[2, d],
            recv_sem=sems.at[3, d],
            device_id=(leaf, peer, c),
            device_id_type=mesh_ids,
        )
        copy.start()
        sends.append(copy)
    for d, peer in enumerate(col_peers):
        copy = pltpu.make_async_remote_copy(
            src_ref=rows_ref.at[:, :, col_slice(c)],
            dst_ref=rows_ref.at[:, :, col_slice(c)],
            send_sem=sems.at[4, d],
            recv_sem=sems.at[5, d],
            device_id=(leaf, r, peer),
            device_id_type=mesh_ids,
        )
        copy.start()
        sends.append(copy)
    for d in range(1, row_count):
        source = lax.rem(r + row_count - d, row_count)
        pltpu.make_async_remote_copy(
            src_ref=cols_ref.at[:, col_slice(source), :],
            dst_ref=cols_ref.at[:, col_slice(source), :],
            send_sem=sems.at[2, d - 1],
            recv_sem=sems.at[3, d - 1],
            device_id=(leaf, source, c),
            device_id_type=mesh_ids,
        ).wait_recv()
    for d in range(1, col_count):
        source = lax.rem(c + col_count - d, col_count)
        pltpu.make_async_remote_copy(
            src_ref=rows_ref.at[:, :, col_slice(source)],
            dst_ref=rows_ref.at[:, :, col_slice(source)],
            send_sem=sems.at[4, d - 1],
            recv_sem=sems.at[5, d - 1],
            device_id=(leaf, r, source),
            device_id_type=mesh_ids,
        ).wait_recv()
    for copy in sends:
        copy.wait_send()


def factor_exchange(partial, row_count, col_count, tile, collective_id):
    nodes, rows, width = partial.shape
    vmem = pl.BlockSpec(memory_space=pltpu.VMEM)
    peers = max(row_count, col_count) - 1
    return pl.pallas_call(
        functools.partial(factor_kernel, tile=tile),
        out_shape=(
            jax.ShapeDtypeStruct((nodes, rows, width), partial.dtype),
            jax.ShapeDtypeStruct((nodes, row_count * tile, tile), partial.dtype),
        ),
        in_specs=[vmem],
        out_specs=(vmem, vmem),
        scratch_shapes=[
            pltpu.VMEM((col_count - 1, nodes, rows, tile), partial.dtype),
            pltpu.SemaphoreType.DMA((6, peers)),
        ],
        compiler_params=pltpu.CompilerParams(collective_id=collective_id, has_side_effects=True),
    )(partial)


def body(sigma_top, panels, inverse_diag, slot_lists, parent_links):
    tile = TILE
    row_count = lax.axis_size("row")
    col_count = lax.axis_size("col")
    leaf_count = lax.axis_size("leaf")
    r = lax.axis_index("row")
    c = lax.axis_index("col")
    panel = panels[0]
    inverse = inverse_diag[0]
    picks_all = slot_lists[0]
    parents = parent_links[0]
    nodes = panel.shape[0]
    width = inverse.shape[2]
    own_tiles = width // tile
    slot_count = picks_all.shape[1]
    positions = slot_count + own_tiles
    band = width // row_count

    partial_factor = mm(panel, inverse)
    factor_rows, factor_cols = factor_exchange(partial_factor, row_count, col_count, tile, 3)
    living = jnp.concatenate([jnp.ones((1, slot_count), jnp.bool_), picks_all >= 0], axis=0)
    live_weight = living.astype(jnp.float32)
    factor_rows = factor_rows * jnp.take(live_weight, r, axis=1)[:, None, None]
    factor_cols = factor_cols * jnp.repeat(live_weight, tile, axis=1)[:, :, None]

    inverse_band = lax.dynamic_slice_in_dim(inverse, r * band, band, 2)
    partial_gram = mm(jnp.transpose(inverse_band, (0, 2, 1)), inverse)
    gram_piece = lax.psum_scatter(partial_gram, "col", scatter_dimension=2, tiled=True)

    local_rows, local_cols = sigma_top.shape
    gathered = lax.all_gather(sigma_top, ("leaf", "row", "col"), axis=0)
    sigma = gathered.reshape(leaf_count * row_count, col_count, local_rows, local_cols)
    sigma = jnp.transpose(sigma, (0, 2, 1, 3)).reshape(
        leaf_count * row_count * local_rows, col_count * local_cols
    )

    def diag_partial(first, products):
        rows = factor_rows[first:first + products.shape[0]]
        return mm(jnp.transpose(rows, (0, 2, 1)), products)

    def reduce_and_gather(first, products, sent):
        count = products.shape[0]
        piece = axis_reduce(diag_partial(first, products), "row", row_count, False, first)
        piece = piece + gram_piece[first:first + count]
        both = jnp.concatenate([sent, piece], axis=1)
        everything = lax.all_gather(both, ("row", "col"), axis=0)
        return everything.reshape(row_count, col_count, count, sent.shape[1] + band, tile)

    bands_per_tile = tile // band

    def product_col_t(gathered, node, m):
        tiles = lax.dynamic_index_in_dim(gathered[:, :, :, :tile], m, 1, keepdims=False)
        tiles = lax.dynamic_index_in_dim(tiles, node, 1, keepdims=False)
        return jnp.transpose(tiles, (2, 0, 1)).reshape(tile, -1)

    def product_row(gathered, node, q):
        tiles = lax.dynamic_index_in_dim(gathered[:, :, :, :tile], q, 0, keepdims=False)
        tiles = lax.dynamic_index_in_dim(tiles, node, 1, keepdims=False)
        return jnp.transpose(tiles, (1, 0, 2)).reshape(tile, -1)

    def diag_row(gathered, node, m):
        pieces = lax.dynamic_slice_in_dim(gathered[:, :, :, tile:], m * bands_per_tile, bands_per_tile, 0)
        pieces = lax.dynamic_index_in_dim(pieces, node, 2, keepdims=False)
        return jnp.transpose(pieces, (0, 2, 1, 3)).reshape(tile, -1)

    def diag_col(gathered, m):
        pieces = lax.dynamic_index_in_dim(gathered[:, :, :, -band:], m, 1, keepdims=False)
        return jnp.transpose(pieces, (1, 0, 2, 3)).reshape(pieces.shape[1], -1, tile)

    own_row = jnp.minimum(r, own_tiles - 1)
    upper = r < own_tiles

    product_0 = mm(tile_rows(sigma, r, tile), factor_cols[0])
    gathered_0 = reduce_and_gather(0, product_0[None], product_0[None])

    sigma_tiles = jnp.transpose(sigma.reshape(sigma.shape[0], slot_count, tile), (1, 0, 2))
    info_1 = jnp.concatenate([r.astype(jnp.int32)[None], picks_all[0:2].reshape(-1), jnp.zeros((2,), jnp.int32)])
    halves = row_count // own_tiles
    product_1, upper_half = level_products(
        info_1, gathered_0, sigma_tiles, factor_cols[1:3], 1, tile, band, own_tiles, slot_count,
        tile, tile, halves,
    )
    gathered_1 = reduce_and_gather(1, product_1, upper_half)

    info_2 = jnp.concatenate(
        [r.astype(jnp.int32)[None], picks_all[2:nodes - 1].reshape(-1), (parents - 1).astype(jnp.int32)]
    )
    (product_2,) = level_products(
        info_2, gathered_1, gathered_0, factor_cols[3:nodes], 2, tile, band, own_tiles, slot_count,
        tile // halves, tile, 0,
    )
    first_2 = 3
    count_2 = product_2.shape[0]
    gram_rows = jnp.zeros((count_2, width, tile), jnp.float32)
    gram_rows = lax.dynamic_update_slice_in_dim(gram_rows, gram_piece[first_2:first_2 + count_2], r * band, 1)
    diag_2 = axis_reduce(diag_partial(first_2, product_2) + gram_rows, "row", row_count, True, 2)

    products = jnp.concatenate([product_0[None], product_1, product_2], axis=0)
    diag_cols = jnp.concatenate([diag_col(gathered_0, c), diag_col(gathered_1, c), diag_2], axis=0)
    return (-products)[None], diag_cols[None]


def solution(mesh):
    return jax.shard_map(
        body,
        mesh=mesh,
        in_specs=(
            P(("leaf", "row"), "col"),
            P("leaf", None, "row", "col"),
            P("leaf", None, "col", None),
            P("leaf", None, None),
            P("leaf", None),
        ),
        out_specs=(P("leaf", None, "row", "col"), P("leaf", None, None, "col")),
        check_vma=False,
    )
```

```python
import functools

import jax
import jax.numpy as jnp
from jax import lax
from jax.experimental import pallas as pl
from jax.experimental.pallas import tpu as pltpu
from jax.sharding import PartitionSpec as P

TILE = 128
HIGHEST = lax.Precision.HIGHEST


def mm(a, b):
    return jnp.matmul(a, b, precision=HIGHEST, preferred_element_type=jnp.float32)


def tile_rows(matrix, index, tile):
    return lax.dynamic_slice_in_dim(matrix, index * tile, tile, 0)


def tile_cols(matrix, index, tile):
    return lax.dynamic_slice_in_dim(matrix, index * tile, tile, 1)


def scatter_factor(factor_col, slots, positions, tile):
    tiles = factor_col.reshape(slots.shape[0], tile, factor_col.shape[1])
    hits = slots[:, None] == jnp.arange(positions, dtype=slots.dtype)[None, :]
    present = jnp.any(hits, axis=0)
    source = jnp.argmax(hits, axis=0)
    moved = jnp.take(tiles, source, axis=0)
    moved = jnp.where(present[:, None, None], moved, 0.0)
    return moved.reshape(positions * tile, factor_col.shape[1])


def dot_hi(a, b):
    return jnp.dot(a, b, precision=HIGHEST, preferred_element_type=jnp.float32)


def dot_t_hi(a, b):
    return lax.dot_general(
        a, b, (((0,), (0,)), ((), ())), precision=HIGHEST, preferred_element_type=jnp.float32
    )


def level_kernel(info_ref, par_ref, low_ref, fac_ref, out_ref, *rest, level, tile, band, own_tiles, slot_count,
                 par_prow, low_prow, halves):
    count = out_ref.shape[0]
    split = tile // band
    r = info_ref[0]
    col = info_ref[1 + count * slot_count + count]
    own = lax.rem(r, own_tiles)

    def p_tile(ref, prow, node, q, m):
        if prow == tile:
            return ref[q, m, node, 0:tile, :]
        parts = tile // prow
        return jnp.concatenate([ref[q + j * own_tiles, m, node, 0:prow, :] for j in range(parts)], axis=0)

    def d_tile(ref, prow, node, a, m):
        return jnp.concatenate([ref[a * split + h, m, node, prow:prow + band, :] for h in range(split)], axis=0)

    for i in range(count):
        base = 1 + i * slot_count
        parent = info_ref[1 + count * slot_count + i]
        factor = [fac_ref[i, k * tile:(k + 1) * tile, :] for k in range(slot_count)]
        picks = [jnp.clip(info_ref[base + k], 0, slot_count - 1) for k in range(slot_count)]
        source = info_ref[base + jnp.maximum(r, own_tiles)]

        upper = dot_hi(d_tile(par_ref, par_prow, parent, own, 0), factor[0])
        for k in range(1, own_tiles):
            upper += dot_hi(d_tile(par_ref, par_prow, parent, own, k), factor[k])
        for k in range(own_tiles, slot_count):
            pick = picks[k] if par_prow == tile else jnp.minimum(picks[k], own_tiles - 1)
            upper -= dot_t_hi(p_tile(par_ref, par_prow, parent, pick, own), factor[k])

        if halves:
            half_ref = rest[0]
            rows = tile // halves
            which = r // own_tiles
            half = upper[0:rows]
            for j in range(1, halves):
                half = jnp.where(which == j, upper[j * rows:(j + 1) * rows], half)
            half_ref[i] = half

        @pl.when(r < own_tiles)
        def _():
            out_ref[i] = upper

        @pl.when(jnp.logical_and(r >= own_tiles, source >= 0))
        def _():
            if level == 1:
                s = jnp.clip(source, 0, slot_count - 1)
                lifted = tile + band + i * tile
                acc = par_ref[s, col, parent, lifted:lifted + tile, :]
                for k in range(own_tiles):
                    acc -= dot_hi(p_tile(par_ref, par_prow, parent, s, k), factor[k])
            else:
                s = jnp.clip(source, 0, own_tiles - 1)
                acc = -dot_hi(p_tile(par_ref, par_prow, parent, s, 0), factor[0])
                for k in range(1, own_tiles):
                    acc -= dot_hi(p_tile(par_ref, par_prow, parent, s, k), factor[k])
                for k in range(own_tiles, slot_count):
                    q = jnp.minimum(picks[k], own_tiles - 1)
                    acc += dot_hi(d_tile(low_ref, low_prow, 0, s, q), factor[k])
            out_ref[i] = acc

        @pl.when(jnp.logical_and(r >= own_tiles, source < 0))
        def _():
            out_ref[i] = jnp.zeros((tile, tile), jnp.float32)


def level_products(info, parent_data, low_data, factors, level, tile, band, own_tiles, slot_count,
                   par_prow, low_prow, halves):
    kernel = functools.partial(
        level_kernel, level=level, tile=tile, band=band, own_tiles=own_tiles, slot_count=slot_count,
        par_prow=par_prow, low_prow=low_prow, halves=halves,
    )
    vmem = pl.BlockSpec(memory_space=pltpu.VMEM)
    count = factors.shape[0]
    shapes = [jax.ShapeDtypeStruct((count, tile, tile), jnp.float32)]
    if halves:
        shapes.append(jax.ShapeDtypeStruct((count, tile // halves, tile), jnp.float32))
    return pl.pallas_call(
        kernel,
        out_shape=tuple(shapes),
        in_specs=[pl.BlockSpec(memory_space=pltpu.SMEM), vmem, vmem, vmem],
        out_specs=tuple([vmem] * len(shapes)),
    )(info, parent_data, low_data, factors)


def reduce_kernel(x_ref, out_ref, recv_ref, send_sem, recv_sem, back_send, back_recv, *, axis, count, band, gather):
    me = lax.axis_index(axis)
    ids = {name: lax.axis_index(name) for name in ("leaf", "row", "col")}

    def device(peer):
        where = dict(ids)
        where[axis] = peer
        return (where["leaf"], where["row"], where["col"])

    mesh_ids = pl.DeviceIdType.MESH
    barrier = pltpu.get_barrier_semaphore()
    for d in range(1, count):
        pl.semaphore_signal(barrier, inc=1, device_id=device(lax.rem(me + d, count)), device_id_type=mesh_ids)
    pl.semaphore_wait(barrier, count - 1)

    sends = []
    for d in range(1, count):
        peer = lax.rem(me + d, count)
        copy = pltpu.make_async_remote_copy(
            src_ref=x_ref.at[:, pl.ds(pl.multiple_of(peer * band, band), band), :],
            dst_ref=recv_ref.at[d - 1],
            send_sem=send_sem.at[d - 1],
            recv_sem=recv_sem.at[d - 1],
            device_id=device(peer),
            device_id_type=mesh_ids,
        )
        copy.start()
        sends.append(copy)
    for copy in sends:
        copy.wait_recv()
    for copy in sends:
        copy.wait_send()
    own = pl.ds(pl.multiple_of(me * band, band), band)
    total = x_ref[:, own, :]
    for d in range(1, count):
        total = total + recv_ref[d - 1]
    if not gather:
        out_ref[...] = total
        return
    out_ref[:, own, :] = total
    backs = []
    for d in range(1, count):
        peer = lax.rem(me + d, count)
        copy = pltpu.make_async_remote_copy(
            src_ref=out_ref.at[:, own, :],
            dst_ref=out_ref.at[:, own, :],
            send_sem=back_send.at[d - 1],
            recv_sem=back_recv.at[d - 1],
            device_id=device(peer),
            device_id_type=mesh_ids,
        )
        copy.start()
        backs.append(copy)
    for d in range(1, count):
        source = lax.rem(me + count - d, count)
        part = pl.ds(pl.multiple_of(source * band, band), band)
        pltpu.make_async_remote_copy(
            src_ref=out_ref.at[:, part, :],
            dst_ref=out_ref.at[:, part, :],
            send_sem=back_send.at[d - 1],
            recv_sem=back_recv.at[d - 1],
            device_id=device(source),
            device_id_type=mesh_ids,
        ).wait_recv()
    for copy in backs:
        copy.wait_send()


def axis_reduce(x, axis, count, gather, collective_id):
    lead, rows, last = x.shape
    band = rows // count
    kernel = functools.partial(reduce_kernel, axis=axis, count=count, band=band, gather=gather)
    out_rows = rows if gather else band
    vmem = pl.BlockSpec(memory_space=pltpu.VMEM)
    return pl.pallas_call(
        kernel,
        out_shape=jax.ShapeDtypeStruct((lead, out_rows, last), x.dtype),
        in_specs=[vmem],
        out_specs=vmem,
        scratch_shapes=[
            pltpu.VMEM((count - 1, lead, band, last), x.dtype),
            pltpu.SemaphoreType.DMA((count - 1,)),
            pltpu.SemaphoreType.DMA((count - 1,)),
            pltpu.SemaphoreType.DMA((count - 1,)),
            pltpu.SemaphoreType.DMA((count - 1,)),
        ],
        compiler_params=pltpu.CompilerParams(collective_id=collective_id, has_side_effects=True),
    )(x)


def factor_kernel(x_ref, rows_ref, cols_ref, recv_ref, sems, *, tile):
    r = lax.axis_index("row")
    c = lax.axis_index("col")
    leaf = lax.axis_index("leaf")
    row_count = lax.axis_size("row")
    col_count = lax.axis_size("col")
    mesh_ids = pl.DeviceIdType.MESH
    col_peers = [lax.rem(c + d, col_count) for d in range(1, col_count)]
    row_peers = [lax.rem(r + d, row_count) for d in range(1, row_count)]

    barrier = pltpu.get_barrier_semaphore()
    for peer in col_peers:
        pl.semaphore_signal(barrier, inc=1, device_id=(leaf, r, peer), device_id_type=mesh_ids)
    for peer in row_peers:
        pl.semaphore_signal(barrier, inc=1, device_id=(leaf, peer, c), device_id_type=mesh_ids)
    pl.semaphore_wait(barrier, len(col_peers) + len(row_peers))

    def col_slice(index):
        return pl.ds(pl.multiple_of(index * tile, tile), tile)

    sends = []
    for d, peer in enumerate(col_peers):
        copy = pltpu.make_async_remote_copy(
            src_ref=x_ref.at[:, :, col_slice(peer)],
            dst_ref=recv_ref.at[d],
            send_sem=sems.at[0, d],
            recv_sem=sems.at[1, d],
            device_id=(leaf, r, peer),
            device_id_type=mesh_ids,
        )
        copy.start()
        sends.append(copy)
    for copy in sends:
        copy.wait_recv()
    for copy in sends:
        copy.wait_send()
    total = x_ref[:, :, col_slice(c)]
    for d in range(len(col_peers)):
        total = total + recv_ref[d]
    rows_ref[:, :, col_slice(c)] = total
    cols_ref[:, col_slice(r), :] = total

    sends = []
    for d, peer in enumerate(row_peers):
        copy = pltpu.make_async_remote_copy(
            src_ref=cols_ref.at[:, col_slice(r), :],
            dst_ref=cols_ref.at[:, col_slice(r), :],
            send_sem=sems.at[2, d],
            recv_sem=sems.at[3, d],
            device_id=(leaf, peer, c),
            device_id_type=mesh_ids,
        )
        copy.start()
        sends.append(copy)
    for d, peer in enumerate(col_peers):
        copy = pltpu.make_async_remote_copy(
            src_ref=rows_ref.at[:, :, col_slice(c)],
            dst_ref=rows_ref.at[:, :, col_slice(c)],
            send_sem=sems.at[4, d],
            recv_sem=sems.at[5, d],
            device_id=(leaf, r, peer),
            device_id_type=mesh_ids,
        )
        copy.start()
        sends.append(copy)
    for d in range(1, row_count):
        source = lax.rem(r + row_count - d, row_count)
        pltpu.make_async_remote_copy(
            src_ref=cols_ref.at[:, col_slice(source), :],
            dst_ref=cols_ref.at[:, col_slice(source), :],
            send_sem=sems.at[2, d - 1],
            recv_sem=sems.at[3, d - 1],
            device_id=(leaf, source, c),
            device_id_type=mesh_ids,
        ).wait_recv()
    for d in range(1, col_count):
        source = lax.rem(c + col_count - d, col_count)
        pltpu.make_async_remote_copy(
            src_ref=rows_ref.at[:, :, col_slice(source)],
            dst_ref=rows_ref.at[:, :, col_slice(source)],
            send_sem=sems.at[4, d - 1],
            recv_sem=sems.at[5, d - 1],
            device_id=(leaf, r, source),
            device_id_type=mesh_ids,
        ).wait_recv()
    for copy in sends:
        copy.wait_send()


def factor_exchange(partial, row_count, col_count, tile, collective_id):
    nodes, rows, width = partial.shape
    vmem = pl.BlockSpec(memory_space=pltpu.VMEM)
    peers = max(row_count, col_count) - 1
    return pl.pallas_call(
        functools.partial(factor_kernel, tile=tile),
        out_shape=(
            jax.ShapeDtypeStruct((nodes, rows, width), partial.dtype),
            jax.ShapeDtypeStruct((nodes, row_count * tile, tile), partial.dtype),
        ),
        in_specs=[vmem],
        out_specs=(vmem, vmem),
        scratch_shapes=[
            pltpu.VMEM((col_count - 1, nodes, rows, tile), partial.dtype),
            pltpu.SemaphoreType.DMA((6, peers)),
        ],
        compiler_params=pltpu.CompilerParams(collective_id=collective_id, has_side_effects=True),
    )(partial)


def body(sigma_top, panels, inverse_diag, slot_lists, parent_links):
    tile = TILE
    row_count = lax.axis_size("row")
    col_count = lax.axis_size("col")
    leaf_count = lax.axis_size("leaf")
    r = lax.axis_index("row")
    c = lax.axis_index("col")
    panel = panels[0]
    inverse = inverse_diag[0]
    picks_all = slot_lists[0]
    parents = parent_links[0]
    nodes = panel.shape[0]
    width = inverse.shape[2]
    own_tiles = width // tile
    slot_count = picks_all.shape[1]
    positions = slot_count + own_tiles
    band = width // row_count

    partial_factor = mm(panel, inverse)
    factor_rows, factor_cols = factor_exchange(partial_factor, row_count, col_count, tile, 3)
    living = jnp.concatenate([jnp.ones((1, slot_count), jnp.bool_), picks_all >= 0], axis=0)
    live_weight = living.astype(jnp.float32)
    factor_rows = factor_rows * jnp.take(live_weight, r, axis=1)[:, None, None]
    factor_cols = factor_cols * jnp.repeat(live_weight, tile, axis=1)[:, :, None]

    inverse_band = lax.dynamic_slice_in_dim(inverse, r * band, band, 2)
    partial_gram = mm(jnp.transpose(inverse_band, (0, 2, 1)), inverse)
    gram_piece = lax.psum_scatter(partial_gram, "col", scatter_dimension=2, tiled=True)

    leaf = lax.axis_index("leaf")
    local_rows = sigma_top.shape[0]
    chunk_rows = lax.all_gather(sigma_top, "col", axis=1, tiled=True)
    chunks_per_tile = tile // local_rows
    rounds = []
    for t in range(chunks_per_tile):
        pairs = []
        for src_leaf in range(leaf_count):
            for src_row in range(row_count):
                q = src_leaf * row_count + src_row
                dst_leaf = (q % chunks_per_tile + t) % leaf_count
                dst_row = q // chunks_per_tile
                for col in range(col_count):
                    pairs.append(
                        ((src_leaf * row_count + src_row) * col_count + col,
                         (dst_leaf * row_count + dst_row) * col_count + col)
                    )
        rounds.append(lax.ppermute(chunk_rows, ("leaf", "row", "col"), pairs))
    order = lax.rem(leaf - jnp.arange(chunks_per_tile, dtype=jnp.int32) + 4 * leaf_count, leaf_count)
    sigma_rows = jnp.take(jnp.stack(rounds), order, axis=0).reshape(tile, -1)

    def diag_partial(first, products):
        rows = factor_rows[first:first + products.shape[0]]
        return mm(jnp.transpose(rows, (0, 2, 1)), products)

    def reduce_and_gather(first, products, sent, extra):
        count = products.shape[0]
        piece = axis_reduce(diag_partial(first, products), "row", row_count, False, first)
        piece = piece + gram_piece[first:first + count]
        both = jnp.concatenate([sent, piece] + extra, axis=1)
        everything = lax.all_gather(both, ("row", "col"), axis=0)
        return everything.reshape(row_count, col_count, count, both.shape[1], tile)

    bands_per_tile = tile // band

    def product_col_t(gathered, node, m):
        tiles = lax.dynamic_index_in_dim(gathered[:, :, :, :tile], m, 1, keepdims=False)
        tiles = lax.dynamic_index_in_dim(tiles, node, 1, keepdims=False)
        return jnp.transpose(tiles, (2, 0, 1)).reshape(tile, -1)

    def product_row(gathered, node, q):
        tiles = lax.dynamic_index_in_dim(gathered[:, :, :, :tile], q, 0, keepdims=False)
        tiles = lax.dynamic_index_in_dim(tiles, node, 1, keepdims=False)
        return jnp.transpose(tiles, (1, 0, 2)).reshape(tile, -1)

    def diag_row(gathered, node, m):
        pieces = lax.dynamic_slice_in_dim(gathered[:, :, :, tile:], m * bands_per_tile, bands_per_tile, 0)
        pieces = lax.dynamic_index_in_dim(pieces, node, 2, keepdims=False)
        return jnp.transpose(pieces, (0, 2, 1, 3)).reshape(tile, -1)

    def diag_col(gathered, m, offset):
        pieces = lax.dynamic_index_in_dim(gathered[:, :, :, offset:offset + band], m, 1, keepdims=False)
        return jnp.transpose(pieces, (1, 0, 2, 3)).reshape(pieces.shape[1], -1, tile)

    own_row = jnp.minimum(r, own_tiles - 1)
    upper = r < own_tiles

    product_0 = mm(sigma_rows, factor_cols[0])
    lifted = [
        mm(sigma_rows, scatter_factor(factor_cols[node], picks_all[node - 1], slot_count, tile))[None]
        for node in (1, 2)
    ]
    gathered_0 = reduce_and_gather(0, product_0[None], product_0[None], lifted)

    info_1 = jnp.concatenate(
        [r.astype(jnp.int32)[None], picks_all[0:2].reshape(-1), jnp.zeros((2,), jnp.int32), c.astype(jnp.int32)[None]]
    )
    halves = row_count // own_tiles
    product_1, upper_half = level_products(
        info_1, gathered_0, gathered_0, factor_cols[1:3], 1, tile, band, own_tiles, slot_count,
        tile, tile, halves,
    )
    gathered_1 = reduce_and_gather(1, product_1, upper_half, [])

    info_2 = jnp.concatenate(
        [r.astype(jnp.int32)[None], picks_all[2:nodes - 1].reshape(-1), (parents - 1).astype(jnp.int32),
         c.astype(jnp.int32)[None]]
    )
    (product_2,) = level_products(
        info_2, gathered_1, gathered_0, factor_cols[3:nodes], 2, tile, band, own_tiles, slot_count,
        tile // halves, tile, 0,
    )
    first_2 = 3
    count_2 = product_2.shape[0]
    gram_rows = jnp.zeros((count_2, width, tile), jnp.float32)
    gram_rows = lax.dynamic_update_slice_in_dim(gram_rows, gram_piece[first_2:first_2 + count_2], r * band, 1)
    diag_2 = axis_reduce(diag_partial(first_2, product_2) + gram_rows, "row", row_count, True, 2)

    products = jnp.concatenate([product_0[None], product_1, product_2], axis=0)
    diag_cols = jnp.concatenate(
        [diag_col(gathered_0, c, tile), diag_col(gathered_1, c, tile // halves), diag_2], axis=0
    )
    return (-products)[None], diag_cols[None]


def solution(mesh):
    return jax.shard_map(
        body,
        mesh=mesh,
        in_specs=(
            P(("leaf", "row"), "col"),
            P("leaf", None, "row", "col"),
            P("leaf", None, "col", None),
            P("leaf", None, None),
            P("leaf", None),
        ),
        out_specs=(P("leaf", None, "row", "col"), P("leaf", None, None, "col")),
        check_vma=False,
    )
```

```python
import functools

import jax
import jax.numpy as jnp
from jax import lax
from jax.experimental import pallas as pl
from jax.experimental.pallas import tpu as pltpu
from jax.sharding import PartitionSpec as P

TILE = 128
HIGHEST = lax.Precision.HIGHEST


def mm(a, b):
    return jnp.matmul(a, b, precision=HIGHEST, preferred_element_type=jnp.float32)


def tile_rows(matrix, index, tile):
    return lax.dynamic_slice_in_dim(matrix, index * tile, tile, 0)


def tile_cols(matrix, index, tile):
    return lax.dynamic_slice_in_dim(matrix, index * tile, tile, 1)


def scatter_factor(factor_col, slots, positions, tile):
    tiles = factor_col.reshape(slots.shape[0], tile, factor_col.shape[1])
    hits = slots[:, None] == jnp.arange(positions, dtype=slots.dtype)[None, :]
    present = jnp.any(hits, axis=0)
    source = jnp.argmax(hits, axis=0)
    moved = jnp.take(tiles, source, axis=0)
    moved = jnp.where(present[:, None, None], moved, 0.0)
    return moved.reshape(positions * tile, factor_col.shape[1])


def dot_hi(a, b):
    return jnp.dot(a, b, precision=HIGHEST, preferred_element_type=jnp.float32)


def dot_t_hi(a, b):
    return lax.dot_general(
        a, b, (((0,), (0,)), ((), ())), precision=HIGHEST, preferred_element_type=jnp.float32
    )


def level_kernel(info_ref, par_ref, low_ref, fac_ref, out_ref, *rest, level, tile, band, own_tiles, slot_count,
                 par_prow, low_prow, halves):
    count = out_ref.shape[0]
    split = tile // band
    r = info_ref[0]
    col = info_ref[1 + count * slot_count + count]
    own = lax.rem(r, own_tiles)

    def p_tile(ref, prow, node, q, m):
        if prow == tile:
            return ref[q, m, node, 0:tile, :]
        parts = tile // prow
        return jnp.concatenate([ref[q + j * own_tiles, m, node, 0:prow, :] for j in range(parts)], axis=0)

    def d_tile(ref, prow, node, a, m):
        return jnp.concatenate([ref[a * split + h, m, node, prow:prow + band, :] for h in range(split)], axis=0)

    for i in range(count):
        base = 1 + i * slot_count
        parent = info_ref[1 + count * slot_count + i]
        factor = [fac_ref[i, k * tile:(k + 1) * tile, :] for k in range(slot_count)]
        picks = [jnp.clip(info_ref[base + k], 0, slot_count - 1) for k in range(slot_count)]
        source = info_ref[base + jnp.maximum(r, own_tiles)]

        upper = dot_hi(d_tile(par_ref, par_prow, parent, own, 0), factor[0])
        for k in range(1, own_tiles):
            upper += dot_hi(d_tile(par_ref, par_prow, parent, own, k), factor[k])
        for k in range(own_tiles, slot_count):
            pick = picks[k] if par_prow == tile else jnp.minimum(picks[k], own_tiles - 1)
            upper -= dot_t_hi(p_tile(par_ref, par_prow, parent, pick, own), factor[k])

        if halves:
            half_ref = rest[0]
            rows = tile // halves
            which = r // own_tiles
            half = upper[0:rows]
            for j in range(1, halves):
                half = jnp.where(which == j, upper[j * rows:(j + 1) * rows], half)
            half_ref[i] = half

        @pl.when(r < own_tiles)
        def _():
            out_ref[i] = upper

        @pl.when(jnp.logical_and(r >= own_tiles, source >= 0))
        def _():
            if level == 1:
                s = jnp.clip(source, 0, slot_count - 1)
                lifted = tile + band + i * tile
                acc = par_ref[s, col, parent, lifted:lifted + tile, :]
                for k in range(own_tiles):
                    acc -= dot_hi(p_tile(par_ref, par_prow, parent, s, k), factor[k])
            else:
                s = jnp.clip(source, 0, own_tiles - 1)
                acc = -dot_hi(p_tile(par_ref, par_prow, parent, s, 0), factor[0])
                for k in range(1, own_tiles):
                    acc -= dot_hi(p_tile(par_ref, par_prow, parent, s, k), factor[k])
                for k in range(own_tiles, slot_count):
                    q = jnp.minimum(picks[k], own_tiles - 1)
                    acc += dot_hi(d_tile(low_ref, low_prow, 0, s, q), factor[k])
            out_ref[i] = acc

        @pl.when(jnp.logical_and(r >= own_tiles, source < 0))
        def _():
            out_ref[i] = jnp.zeros((tile, tile), jnp.float32)


def level_products(info, parent_data, low_data, factors, level, tile, band, own_tiles, slot_count,
                   par_prow, low_prow, halves):
    kernel = functools.partial(
        level_kernel, level=level, tile=tile, band=band, own_tiles=own_tiles, slot_count=slot_count,
        par_prow=par_prow, low_prow=low_prow, halves=halves,
    )
    vmem = pl.BlockSpec(memory_space=pltpu.VMEM)
    count = factors.shape[0]
    shapes = [jax.ShapeDtypeStruct((count, tile, tile), jnp.float32)]
    if halves:
        shapes.append(jax.ShapeDtypeStruct((count, tile // halves, tile), jnp.float32))
    return pl.pallas_call(
        kernel,
        out_shape=tuple(shapes),
        in_specs=[pl.BlockSpec(memory_space=pltpu.SMEM), vmem, vmem, vmem],
        out_specs=tuple([vmem] * len(shapes)),
    )(info, parent_data, low_data, factors)


def reduce_kernel(x_ref, out_ref, recv_ref, send_sem, recv_sem, back_send, back_recv, *, axis, count, band, gather):
    me = lax.axis_index(axis)
    ids = {name: lax.axis_index(name) for name in ("leaf", "row", "col")}

    def device(peer):
        where = dict(ids)
        where[axis] = peer
        return (where["leaf"], where["row"], where["col"])

    mesh_ids = pl.DeviceIdType.MESH
    barrier = pltpu.get_barrier_semaphore()
    for d in range(1, count):
        pl.semaphore_signal(barrier, inc=1, device_id=device(lax.rem(me + d, count)), device_id_type=mesh_ids)
    pl.semaphore_wait(barrier, count - 1)

    sends = []
    for d in range(1, count):
        peer = lax.rem(me + d, count)
        copy = pltpu.make_async_remote_copy(
            src_ref=x_ref.at[:, pl.ds(pl.multiple_of(peer * band, band), band), :],
            dst_ref=recv_ref.at[d - 1],
            send_sem=send_sem.at[d - 1],
            recv_sem=recv_sem.at[d - 1],
            device_id=device(peer),
            device_id_type=mesh_ids,
        )
        copy.start()
        sends.append(copy)
    for copy in sends:
        copy.wait_recv()
    for copy in sends:
        copy.wait_send()
    own = pl.ds(pl.multiple_of(me * band, band), band)
    total = x_ref[:, own, :]
    for d in range(1, count):
        total = total + recv_ref[d - 1]
    if not gather:
        out_ref[...] = total
        return
    out_ref[:, own, :] = total
    backs = []
    for d in range(1, count):
        peer = lax.rem(me + d, count)
        copy = pltpu.make_async_remote_copy(
            src_ref=out_ref.at[:, own, :],
            dst_ref=out_ref.at[:, own, :],
            send_sem=back_send.at[d - 1],
            recv_sem=back_recv.at[d - 1],
            device_id=device(peer),
            device_id_type=mesh_ids,
        )
        copy.start()
        backs.append(copy)
    for d in range(1, count):
        source = lax.rem(me + count - d, count)
        part = pl.ds(pl.multiple_of(source * band, band), band)
        pltpu.make_async_remote_copy(
            src_ref=out_ref.at[:, part, :],
            dst_ref=out_ref.at[:, part, :],
            send_sem=back_send.at[d - 1],
            recv_sem=back_recv.at[d - 1],
            device_id=device(source),
            device_id_type=mesh_ids,
        ).wait_recv()
    for copy in backs:
        copy.wait_send()


def axis_reduce(x, axis, count, gather, collective_id):
    lead, rows, last = x.shape
    band = rows // count
    kernel = functools.partial(reduce_kernel, axis=axis, count=count, band=band, gather=gather)
    out_rows = rows if gather else band
    vmem = pl.BlockSpec(memory_space=pltpu.VMEM)
    return pl.pallas_call(
        kernel,
        out_shape=jax.ShapeDtypeStruct((lead, out_rows, last), x.dtype),
        in_specs=[vmem],
        out_specs=vmem,
        scratch_shapes=[
            pltpu.VMEM((count - 1, lead, band, last), x.dtype),
            pltpu.SemaphoreType.DMA((count - 1,)),
            pltpu.SemaphoreType.DMA((count - 1,)),
            pltpu.SemaphoreType.DMA((count - 1,)),
            pltpu.SemaphoreType.DMA((count - 1,)),
        ],
        compiler_params=pltpu.CompilerParams(collective_id=collective_id, has_side_effects=True),
    )(x)


def body(sigma_top, panels, inverse_diag, slot_lists, parent_links):
    tile = TILE
    row_count = lax.axis_size("row")
    col_count = lax.axis_size("col")
    leaf_count = lax.axis_size("leaf")
    r = lax.axis_index("row")
    c = lax.axis_index("col")
    panel = panels[0]
    inverse = inverse_diag[0]
    picks_all = slot_lists[0]
    parents = parent_links[0]
    nodes = panel.shape[0]
    width = inverse.shape[2]
    own_tiles = width // tile
    slot_count = picks_all.shape[1]
    positions = slot_count + own_tiles
    band = width // row_count

    partial_factor = mm(panel, inverse)
    factor_rows = axis_reduce(partial_factor, "col", col_count, True, 3)
    living = jnp.concatenate([jnp.ones((1, slot_count), jnp.bool_), picks_all >= 0], axis=0)
    live_here = jnp.take(living, r, axis=1).astype(jnp.float32)
    factor_rows = factor_rows * live_here[:, None, None]
    factor_tile = lax.dynamic_slice_in_dim(factor_rows, c * tile, tile, 2)
    factor_cols = lax.all_gather(factor_tile, "row", axis=1, tiled=True)

    inverse_band = lax.dynamic_slice_in_dim(inverse, r * band, band, 2)
    partial_gram = mm(jnp.transpose(inverse_band, (0, 2, 1)), inverse)
    gram_piece = lax.psum_scatter(partial_gram, "col", scatter_dimension=2, tiled=True)

    leaf = lax.axis_index("leaf")
    local_rows = sigma_top.shape[0]
    chunk_rows = lax.all_gather(sigma_top, "col", axis=1, tiled=True)
    chunks_per_tile = tile // local_rows
    rounds = []
    for t in range(chunks_per_tile):
        pairs = []
        for src_leaf in range(leaf_count):
            for src_row in range(row_count):
                q = src_leaf * row_count + src_row
                dst_leaf = (q % chunks_per_tile + t) % leaf_count
                dst_row = q // chunks_per_tile
                for col in range(col_count):
                    pairs.append(
                        ((src_leaf * row_count + src_row) * col_count + col,
                         (dst_leaf * row_count + dst_row) * col_count + col)
                    )
        rounds.append(lax.ppermute(chunk_rows, ("leaf", "row", "col"), pairs))
    order = lax.rem(leaf - jnp.arange(chunks_per_tile, dtype=jnp.int32) + 4 * leaf_count, leaf_count)
    sigma_rows = jnp.take(jnp.stack(rounds), order, axis=0).reshape(tile, -1)

    def diag_partial(first, products):
        rows = factor_rows[first:first + products.shape[0]]
        return mm(jnp.transpose(rows, (0, 2, 1)), products)

    def reduce_and_gather(first, products, sent, extra):
        count = products.shape[0]
        piece = axis_reduce(diag_partial(first, products), "row", row_count, False, first)
        piece = piece + gram_piece[first:first + count]
        both = jnp.concatenate([sent, piece] + extra, axis=1)
        everything = lax.all_gather(both, ("row", "col"), axis=0)
        return everything.reshape(row_count, col_count, count, both.shape[1], tile)

    bands_per_tile = tile // band

    def product_col_t(gathered, node, m):
        tiles = lax.dynamic_index_in_dim(gathered[:, :, :, :tile], m, 1, keepdims=False)
        tiles = lax.dynamic_index_in_dim(tiles, node, 1, keepdims=False)
        return jnp.transpose(tiles, (2, 0, 1)).reshape(tile, -1)

    def product_row(gathered, node, q):
        tiles = lax.dynamic_index_in_dim(gathered[:, :, :, :tile], q, 0, keepdims=False)
        tiles = lax.dynamic_index_in_dim(tiles, node, 1, keepdims=False)
        return jnp.transpose(tiles, (1, 0, 2)).reshape(tile, -1)

    def diag_row(gathered, node, m):
        pieces = lax.dynamic_slice_in_dim(gathered[:, :, :, tile:], m * bands_per_tile, bands_per_tile, 0)
        pieces = lax.dynamic_index_in_dim(pieces, node, 2, keepdims=False)
        return jnp.transpose(pieces, (0, 2, 1, 3)).reshape(tile, -1)

    def diag_col(gathered, m, offset):
        pieces = lax.dynamic_index_in_dim(gathered[:, :, :, offset:offset + band], m, 1, keepdims=False)
        return jnp.transpose(pieces, (1, 0, 2, 3)).reshape(pieces.shape[1], -1, tile)

    own_row = jnp.minimum(r, own_tiles - 1)
    upper = r < own_tiles

    product_0 = mm(sigma_rows, factor_cols[0])
    lifted = [
        mm(sigma_rows, scatter_factor(factor_cols[node], picks_all[node - 1], slot_count, tile))[None]
        for node in (1, 2)
    ]
    gathered_0 = reduce_and_gather(0, product_0[None], product_0[None], lifted)

    info_1 = jnp.concatenate(
        [r.astype(jnp.int32)[None], picks_all[0:2].reshape(-1), jnp.zeros((2,), jnp.int32), c.astype(jnp.int32)[None]]
    )
    halves = row_count // own_tiles
    product_1, upper_half = level_products(
        info_1, gathered_0, gathered_0, factor_cols[1:3], 1, tile, band, own_tiles, slot_count,
        tile, tile, halves,
    )
    gathered_1 = reduce_and_gather(1, product_1, upper_half, [])

    info_2 = jnp.concatenate(
        [r.astype(jnp.int32)[None], picks_all[2:nodes - 1].reshape(-1), (parents - 1).astype(jnp.int32),
         c.astype(jnp.int32)[None]]
    )
    (product_2,) = level_products(
        info_2, gathered_1, gathered_0, factor_cols[3:nodes], 2, tile, band, own_tiles, slot_count,
        tile // halves, tile, 0,
    )
    first_2 = 3
    count_2 = product_2.shape[0]
    gram_rows = jnp.zeros((count_2, width, tile), jnp.float32)
    gram_rows = lax.dynamic_update_slice_in_dim(gram_rows, gram_piece[first_2:first_2 + count_2], r * band, 1)
    diag_2 = axis_reduce(diag_partial(first_2, product_2) + gram_rows, "row", row_count, True, 2)

    products = jnp.concatenate([product_0[None], product_1, product_2], axis=0)
    diag_cols = jnp.concatenate(
        [diag_col(gathered_0, c, tile), diag_col(gathered_1, c, tile // halves), diag_2], axis=0
    )
    return (-products)[None], diag_cols[None]


def solution(mesh):
    return jax.shard_map(
        body,
        mesh=mesh,
        in_specs=(
            P(("leaf", "row"), "col"),
            P("leaf", None, "row", "col"),
            P("leaf", None, "col", None),
            P("leaf", None, None),
            P("leaf", None),
        ),
        out_specs=(P("leaf", None, "row", "col"), P("leaf", None, None, "col")),
        check_vma=False,
    )
```

```python
import functools

import jax
import jax.numpy as jnp
from jax import lax
from jax.experimental import pallas as pl
from jax.experimental.pallas import tpu as pltpu
from jax.sharding import PartitionSpec as P

TILE = 128
HIGHEST = lax.Precision.HIGHEST


def mm(a, b):
    return jnp.matmul(a, b, precision=HIGHEST, preferred_element_type=jnp.float32)


def tile_rows(matrix, index, tile):
    return lax.dynamic_slice_in_dim(matrix, index * tile, tile, 0)


def tile_cols(matrix, index, tile):
    return lax.dynamic_slice_in_dim(matrix, index * tile, tile, 1)


def scatter_factor(factor_col, slots, positions, tile):
    tiles = factor_col.reshape(slots.shape[0], tile, factor_col.shape[1])
    hits = slots[:, None] == jnp.arange(positions, dtype=slots.dtype)[None, :]
    present = jnp.any(hits, axis=0)
    source = jnp.argmax(hits, axis=0)
    moved = jnp.take(tiles, source, axis=0)
    moved = jnp.where(present[:, None, None], moved, 0.0)
    return moved.reshape(positions * tile, factor_col.shape[1])


def dot_hi(a, b):
    return jnp.dot(a, b, precision=HIGHEST, preferred_element_type=jnp.float32)


def dot_t_hi(a, b):
    return lax.dot_general(
        a, b, (((0,), (0,)), ((), ())), precision=HIGHEST, preferred_element_type=jnp.float32
    )


def level_kernel(info_ref, par_ref, low_ref, fac_ref, out_ref, *rest, level, tile, band, own_tiles, slot_count,
                 par_prow, low_prow, halves):
    count = out_ref.shape[0]
    split = tile // band
    r = info_ref[0]
    col = info_ref[1 + count * slot_count + count]
    own = lax.rem(r, own_tiles)

    def p_tile(ref, prow, node, q, m):
        if prow == tile:
            return ref[q, m, node, 0:tile, :]
        parts = tile // prow
        return jnp.concatenate([ref[q + j * own_tiles, m, node, 0:prow, :] for j in range(parts)], axis=0)

    def d_tile(ref, prow, node, a, m):
        return jnp.concatenate([ref[a * split + h, m, node, prow:prow + band, :] for h in range(split)], axis=0)

    for i in range(count):
        base = 1 + i * slot_count
        parent = info_ref[1 + count * slot_count + i]
        factor = [fac_ref[i, k * tile:(k + 1) * tile, :] for k in range(slot_count)]
        picks = [jnp.clip(info_ref[base + k], 0, slot_count - 1) for k in range(slot_count)]
        source = info_ref[base + jnp.maximum(r, own_tiles)]

        upper = dot_hi(d_tile(par_ref, par_prow, parent, own, 0), factor[0])
        for k in range(1, own_tiles):
            upper += dot_hi(d_tile(par_ref, par_prow, parent, own, k), factor[k])
        for k in range(own_tiles, slot_count):
            pick = picks[k] if par_prow == tile else jnp.minimum(picks[k], own_tiles - 1)
            upper -= dot_t_hi(p_tile(par_ref, par_prow, parent, pick, own), factor[k])

        if halves:
            half_ref = rest[0]
            rows = tile // halves
            which = r // own_tiles
            half = upper[0:rows]
            for j in range(1, halves):
                half = jnp.where(which == j, upper[j * rows:(j + 1) * rows], half)
            half_ref[i] = half

        @pl.when(r < own_tiles)
        def _():
            out_ref[i] = upper

        @pl.when(jnp.logical_and(r >= own_tiles, source >= 0))
        def _():
            if level == 1:
                s = jnp.clip(source, 0, slot_count - 1)
                lifted = tile + band + i * tile
                acc = par_ref[s, col, parent, lifted:lifted + tile, :]
                for k in range(own_tiles):
                    acc -= dot_hi(p_tile(par_ref, par_prow, parent, s, k), factor[k])
            else:
                s = jnp.clip(source, 0, own_tiles - 1)
                acc = -dot_hi(p_tile(par_ref, par_prow, parent, s, 0), factor[0])
                for k in range(1, own_tiles):
                    acc -= dot_hi(p_tile(par_ref, par_prow, parent, s, k), factor[k])
                for k in range(own_tiles, slot_count):
                    q = jnp.minimum(picks[k], own_tiles - 1)
                    acc += dot_hi(d_tile(low_ref, low_prow, 0, s, q), factor[k])
            out_ref[i] = acc

        @pl.when(jnp.logical_and(r >= own_tiles, source < 0))
        def _():
            out_ref[i] = jnp.zeros((tile, tile), jnp.float32)


def level_products(info, parent_data, low_data, factors, level, tile, band, own_tiles, slot_count,
                   par_prow, low_prow, halves):
    kernel = functools.partial(
        level_kernel, level=level, tile=tile, band=band, own_tiles=own_tiles, slot_count=slot_count,
        par_prow=par_prow, low_prow=low_prow, halves=halves,
    )
    vmem = pl.BlockSpec(memory_space=pltpu.VMEM)
    count = factors.shape[0]
    shapes = [jax.ShapeDtypeStruct((count, tile, tile), jnp.float32)]
    if halves:
        shapes.append(jax.ShapeDtypeStruct((count, tile // halves, tile), jnp.float32))
    return pl.pallas_call(
        kernel,
        out_shape=tuple(shapes),
        in_specs=[pl.BlockSpec(memory_space=pltpu.SMEM), vmem, vmem, vmem],
        out_specs=tuple([vmem] * len(shapes)),
    )(info, parent_data, low_data, factors)


def reduce_kernel(x_ref, out_ref, recv_ref, send_sem, recv_sem, back_send, back_recv, *, axis, count, band, gather):
    me = lax.axis_index(axis)
    ids = {name: lax.axis_index(name) for name in ("leaf", "row", "col")}

    def device(peer):
        where = dict(ids)
        where[axis] = peer
        return (where["leaf"], where["row"], where["col"])

    mesh_ids = pl.DeviceIdType.MESH
    barrier = pltpu.get_barrier_semaphore()
    for d in range(1, count):
        pl.semaphore_signal(barrier, inc=1, device_id=device(lax.rem(me + d, count)), device_id_type=mesh_ids)
    pl.semaphore_wait(barrier, count - 1)

    sends = []
    for d in range(1, count):
        peer = lax.rem(me + d, count)
        copy = pltpu.make_async_remote_copy(
            src_ref=x_ref.at[:, pl.ds(pl.multiple_of(peer * band, band), band), :],
            dst_ref=recv_ref.at[d - 1],
            send_sem=send_sem.at[d - 1],
            recv_sem=recv_sem.at[d - 1],
            device_id=device(peer),
            device_id_type=mesh_ids,
        )
        copy.start()
        sends.append(copy)
    for copy in sends:
        copy.wait_recv()
    for copy in sends:
        copy.wait_send()
    own = pl.ds(pl.multiple_of(me * band, band), band)
    total = x_ref[:, own, :]
    for d in range(1, count):
        total = total + recv_ref[d - 1]
    if not gather:
        out_ref[...] = total
        return
    out_ref[:, own, :] = total
    backs = []
    for d in range(1, count):
        peer = lax.rem(me + d, count)
        copy = pltpu.make_async_remote_copy(
            src_ref=out_ref.at[:, own, :],
            dst_ref=out_ref.at[:, own, :],
            send_sem=back_send.at[d - 1],
            recv_sem=back_recv.at[d - 1],
            device_id=device(peer),
            device_id_type=mesh_ids,
        )
        copy.start()
        backs.append(copy)
    for d in range(1, count):
        source = lax.rem(me + count - d, count)
        part = pl.ds(pl.multiple_of(source * band, band), band)
        pltpu.make_async_remote_copy(
            src_ref=out_ref.at[:, part, :],
            dst_ref=out_ref.at[:, part, :],
            send_sem=back_send.at[d - 1],
            recv_sem=back_recv.at[d - 1],
            device_id=device(source),
            device_id_type=mesh_ids,
        ).wait_recv()
    for copy in backs:
        copy.wait_send()


def axis_reduce(x, axis, count, gather, collective_id):
    lead, rows, last = x.shape
    band = rows // count
    kernel = functools.partial(reduce_kernel, axis=axis, count=count, band=band, gather=gather)
    out_rows = rows if gather else band
    vmem = pl.BlockSpec(memory_space=pltpu.VMEM)
    return pl.pallas_call(
        kernel,
        out_shape=jax.ShapeDtypeStruct((lead, out_rows, last), x.dtype),
        in_specs=[vmem],
        out_specs=vmem,
        scratch_shapes=[
            pltpu.VMEM((count - 1, lead, band, last), x.dtype),
            pltpu.SemaphoreType.DMA((count - 1,)),
            pltpu.SemaphoreType.DMA((count - 1,)),
            pltpu.SemaphoreType.DMA((count - 1,)),
            pltpu.SemaphoreType.DMA((count - 1,)),
        ],
        compiler_params=pltpu.CompilerParams(collective_id=collective_id, has_side_effects=True),
    )(x)


def body(sigma_top, panels, inverse_diag, slot_lists, parent_links):
    tile = TILE
    row_count = lax.axis_size("row")
    col_count = lax.axis_size("col")
    leaf_count = lax.axis_size("leaf")
    r = lax.axis_index("row")
    c = lax.axis_index("col")
    panel = panels[0]
    inverse = inverse_diag[0]
    picks_all = slot_lists[0]
    parents = parent_links[0]
    nodes = panel.shape[0]
    width = inverse.shape[2]
    own_tiles = width // tile
    slot_count = picks_all.shape[1]
    positions = slot_count + own_tiles
    band = width // row_count

    partial_t = jnp.einsum("vkj,vrk->vjr", inverse, panel, precision=HIGHEST, preferred_element_type=jnp.float32)
    factor_t = axis_reduce(partial_t, "col", col_count, False, 3)
    living = jnp.concatenate([jnp.ones((1, slot_count), jnp.bool_), picks_all >= 0], axis=0)
    live_here = jnp.take(living, r, axis=1).astype(jnp.float32)
    factor_tile = jnp.transpose(factor_t, (0, 2, 1)) * live_here[:, None, None]
    factor_cols = lax.all_gather(factor_tile, "row", axis=1, tiled=True)
    factor_rows = lax.all_gather(factor_tile, "col", axis=2, tiled=True)

    inverse_band = lax.dynamic_slice_in_dim(inverse, r * band, band, 2)
    partial_gram = mm(jnp.transpose(inverse_band, (0, 2, 1)), inverse)
    gram_piece = lax.psum_scatter(partial_gram, "col", scatter_dimension=2, tiled=True)

    leaf = lax.axis_index("leaf")
    local_rows = sigma_top.shape[0]
    chunk_rows = lax.all_gather(sigma_top, "col", axis=1, tiled=True)
    chunks_per_tile = tile // local_rows
    rounds = []
    for t in range(chunks_per_tile):
        pairs = []
        for src_leaf in range(leaf_count):
            for src_row in range(row_count):
                q = src_leaf * row_count + src_row
                dst_leaf = (q % chunks_per_tile + t) % leaf_count
                dst_row = q // chunks_per_tile
                for col in range(col_count):
                    pairs.append(
                        ((src_leaf * row_count + src_row) * col_count + col,
                         (dst_leaf * row_count + dst_row) * col_count + col)
                    )
        rounds.append(lax.ppermute(chunk_rows, ("leaf", "row", "col"), pairs))
    order = lax.rem(leaf - jnp.arange(chunks_per_tile, dtype=jnp.int32) + 4 * leaf_count, leaf_count)
    sigma_rows = jnp.take(jnp.stack(rounds), order, axis=0).reshape(tile, -1)

    def diag_partial(first, products):
        rows = factor_rows[first:first + products.shape[0]]
        return mm(jnp.transpose(rows, (0, 2, 1)), products)

    def reduce_and_gather(first, products, sent, extra):
        count = products.shape[0]
        piece = axis_reduce(diag_partial(first, products), "row", row_count, False, first)
        piece = piece + gram_piece[first:first + count]
        both = jnp.concatenate([sent, piece] + extra, axis=1)
        everything = lax.all_gather(both, ("row", "col"), axis=0)
        return everything.reshape(row_count, col_count, count, both.shape[1], tile)

    bands_per_tile = tile // band

    def product_col_t(gathered, node, m):
        tiles = lax.dynamic_index_in_dim(gathered[:, :, :, :tile], m, 1, keepdims=False)
        tiles = lax.dynamic_index_in_dim(tiles, node, 1, keepdims=False)
        return jnp.transpose(tiles, (2, 0, 1)).reshape(tile, -1)

    def product_row(gathered, node, q):
        tiles = lax.dynamic_index_in_dim(gathered[:, :, :, :tile], q, 0, keepdims=False)
        tiles = lax.dynamic_index_in_dim(tiles, node, 1, keepdims=False)
        return jnp.transpose(tiles, (1, 0, 2)).reshape(tile, -1)

    def diag_row(gathered, node, m):
        pieces = lax.dynamic_slice_in_dim(gathered[:, :, :, tile:], m * bands_per_tile, bands_per_tile, 0)
        pieces = lax.dynamic_index_in_dim(pieces, node, 2, keepdims=False)
        return jnp.transpose(pieces, (0, 2, 1, 3)).reshape(tile, -1)

    def diag_col(gathered, m, offset):
        pieces = lax.dynamic_index_in_dim(gathered[:, :, :, offset:offset + band], m, 1, keepdims=False)
        return jnp.transpose(pieces, (1, 0, 2, 3)).reshape(pieces.shape[1], -1, tile)

    own_row = jnp.minimum(r, own_tiles - 1)
    upper = r < own_tiles

    product_0 = mm(sigma_rows, factor_cols[0])
    lifted = [
        mm(sigma_rows, scatter_factor(factor_cols[node], picks_all[node - 1], slot_count, tile))[None]
        for node in (1, 2)
    ]
    gathered_0 = reduce_and_gather(0, product_0[None], product_0[None], lifted)

    info_1 = jnp.concatenate(
        [r.astype(jnp.int32)[None], picks_all[0:2].reshape(-1), jnp.zeros((2,), jnp.int32), c.astype(jnp.int32)[None]]
    )
    halves = row_count // own_tiles
    product_1, upper_half = level_products(
        info_1, gathered_0, gathered_0, factor_cols[1:3], 1, tile, band, own_tiles, slot_count,
        tile, tile, halves,
    )
    gathered_1 = reduce_and_gather(1, product_1, upper_half, [])

    info_2 = jnp.concatenate(
        [r.astype(jnp.int32)[None], picks_all[2:nodes - 1].reshape(-1), (parents - 1).astype(jnp.int32),
         c.astype(jnp.int32)[None]]
    )
    (product_2,) = level_products(
        info_2, gathered_1, gathered_0, factor_cols[3:nodes], 2, tile, band, own_tiles, slot_count,
        tile // halves, tile, 0,
    )
    first_2 = 3
    count_2 = product_2.shape[0]
    gram_rows = jnp.zeros((count_2, width, tile), jnp.float32)
    gram_rows = lax.dynamic_update_slice_in_dim(gram_rows, gram_piece[first_2:first_2 + count_2], r * band, 1)
    diag_2 = axis_reduce(diag_partial(first_2, product_2) + gram_rows, "row", row_count, True, 2)

    products = jnp.concatenate([product_0[None], product_1, product_2], axis=0)
    diag_cols = jnp.concatenate(
        [diag_col(gathered_0, c, tile), diag_col(gathered_1, c, tile // halves), diag_2], axis=0
    )
    return (-products)[None], diag_cols[None]


def solution(mesh):
    return jax.shard_map(
        body,
        mesh=mesh,
        in_specs=(
            P(("leaf", "row"), "col"),
            P("leaf", None, "row", "col"),
            P("leaf", None, "col", None),
            P("leaf", None, None),
            P("leaf", None),
        ),
        out_specs=(P("leaf", None, "row", "col"), P("leaf", None, None, "col")),
        check_vma=False,
    )
```

```python
import functools

import jax
import jax.numpy as jnp
from jax import lax
from jax.experimental import pallas as pl
from jax.experimental.pallas import tpu as pltpu
from jax.sharding import PartitionSpec as P

TILE = 128
HIGHEST = lax.Precision.HIGHEST


def mm(a, b):
    return jnp.matmul(a, b, precision=HIGHEST, preferred_element_type=jnp.float32)


def tile_rows(matrix, index, tile):
    return lax.dynamic_slice_in_dim(matrix, index * tile, tile, 0)


def tile_cols(matrix, index, tile):
    return lax.dynamic_slice_in_dim(matrix, index * tile, tile, 1)


def scatter_factor(factor_col, slots, positions, tile):
    tiles = factor_col.reshape(slots.shape[0], tile, factor_col.shape[1])
    hits = slots[:, None] == jnp.arange(positions, dtype=slots.dtype)[None, :]
    present = jnp.any(hits, axis=0)
    source = jnp.argmax(hits, axis=0)
    moved = jnp.take(tiles, source, axis=0)
    moved = jnp.where(present[:, None, None], moved, 0.0)
    return moved.reshape(positions * tile, factor_col.shape[1])


def dot_hi(a, b):
    return jnp.dot(a, b, precision=HIGHEST, preferred_element_type=jnp.float32)


def dot_t_hi(a, b):
    return lax.dot_general(
        a, b, (((0,), (0,)), ((), ())), precision=HIGHEST, preferred_element_type=jnp.float32
    )


def level_kernel(info_ref, par_ref, low_ref, fac_ref, out_ref, *rest, level, tile, band, own_tiles, slot_count,
                 par_prow, low_prow, halves):
    count = out_ref.shape[0]
    split = tile // band
    r = info_ref[0]
    col = info_ref[1 + count * slot_count + count]
    own = lax.rem(r, own_tiles)

    def p_tile(ref, prow, node, q, m):
        if prow == tile:
            return ref[q, m, node, 0:tile, :]
        parts = tile // prow
        return jnp.concatenate([ref[q + j * own_tiles, m, node, 0:prow, :] for j in range(parts)], axis=0)

    def d_tile(ref, prow, node, a, m):
        return jnp.concatenate([ref[a * split + h, m, node, prow:prow + band, :] for h in range(split)], axis=0)

    for i in range(count):
        base = 1 + i * slot_count
        parent = info_ref[1 + count * slot_count + i]
        factor = [fac_ref[i, k * tile:(k + 1) * tile, :] for k in range(slot_count)]
        picks = [jnp.clip(info_ref[base + k], 0, slot_count - 1) for k in range(slot_count)]
        source = info_ref[base + jnp.maximum(r, own_tiles)]

        upper = dot_hi(d_tile(par_ref, par_prow, parent, own, 0), factor[0])
        for k in range(1, own_tiles):
            upper += dot_hi(d_tile(par_ref, par_prow, parent, own, k), factor[k])
        for k in range(own_tiles, slot_count):
            pick = picks[k] if par_prow == tile else jnp.minimum(picks[k], own_tiles - 1)
            upper -= dot_t_hi(p_tile(par_ref, par_prow, parent, pick, own), factor[k])

        if halves:
            half_ref = rest[0]
            rows = tile // halves
            which = r // own_tiles
            half = upper[0:rows]
            for j in range(1, halves):
                half = jnp.where(which == j, upper[j * rows:(j + 1) * rows], half)
            half_ref[i] = half

        @pl.when(r < own_tiles)
        def _():
            out_ref[i] = upper

        @pl.when(jnp.logical_and(r >= own_tiles, source >= 0))
        def _():
            if level == 1:
                s = jnp.clip(source, 0, slot_count - 1)
                lifted = tile + band + i * tile
                acc = par_ref[s, col, parent, lifted:lifted + tile, :]
                for k in range(own_tiles):
                    acc -= dot_hi(p_tile(par_ref, par_prow, parent, s, k), factor[k])
            else:
                s = jnp.clip(source, 0, own_tiles - 1)
                acc = -dot_hi(p_tile(par_ref, par_prow, parent, s, 0), factor[0])
                for k in range(1, own_tiles):
                    acc -= dot_hi(p_tile(par_ref, par_prow, parent, s, k), factor[k])
                for k in range(own_tiles, slot_count):
                    q = jnp.minimum(picks[k], own_tiles - 1)
                    acc += dot_hi(d_tile(low_ref, low_prow, 0, s, q), factor[k])
            out_ref[i] = acc

        @pl.when(jnp.logical_and(r >= own_tiles, source < 0))
        def _():
            out_ref[i] = jnp.zeros((tile, tile), jnp.float32)


def level_products(info, parent_data, low_data, factors, level, tile, band, own_tiles, slot_count,
                   par_prow, low_prow, halves):
    kernel = functools.partial(
        level_kernel, level=level, tile=tile, band=band, own_tiles=own_tiles, slot_count=slot_count,
        par_prow=par_prow, low_prow=low_prow, halves=halves,
    )
    vmem = pl.BlockSpec(memory_space=pltpu.VMEM)
    count = factors.shape[0]
    shapes = [jax.ShapeDtypeStruct((count, tile, tile), jnp.float32)]
    if halves:
        shapes.append(jax.ShapeDtypeStruct((count, tile // halves, tile), jnp.float32))
    return pl.pallas_call(
        kernel,
        out_shape=tuple(shapes),
        in_specs=[pl.BlockSpec(memory_space=pltpu.SMEM), vmem, vmem, vmem],
        out_specs=tuple([vmem] * len(shapes)),
    )(info, parent_data, low_data, factors)


def reduce_kernel(x_ref, out_ref, recv_ref, send_sem, recv_sem, back_send, back_recv, *, axis, count, band, gather):
    me = lax.axis_index(axis)
    ids = {name: lax.axis_index(name) for name in ("leaf", "row", "col")}

    def device(peer):
        where = dict(ids)
        where[axis] = peer
        return (where["leaf"], where["row"], where["col"])

    mesh_ids = pl.DeviceIdType.MESH
    barrier = pltpu.get_barrier_semaphore()
    for d in range(1, count):
        pl.semaphore_signal(barrier, inc=1, device_id=device(lax.rem(me + d, count)), device_id_type=mesh_ids)
    pl.semaphore_wait(barrier, count - 1)

    sends = []
    for d in range(1, count):
        peer = lax.rem(me + d, count)
        copy = pltpu.make_async_remote_copy(
            src_ref=x_ref.at[:, pl.ds(pl.multiple_of(peer * band, band), band), :],
            dst_ref=recv_ref.at[d - 1],
            send_sem=send_sem.at[d - 1],
            recv_sem=recv_sem.at[d - 1],
            device_id=device(peer),
            device_id_type=mesh_ids,
        )
        copy.start()
        sends.append(copy)
    for copy in sends:
        copy.wait_recv()
    for copy in sends:
        copy.wait_send()
    own = pl.ds(pl.multiple_of(me * band, band), band)
    total = x_ref[:, own, :]
    for d in range(1, count):
        total = total + recv_ref[d - 1]
    if not gather:
        out_ref[...] = total
        return
    out_ref[:, own, :] = total
    backs = []
    for d in range(1, count):
        peer = lax.rem(me + d, count)
        copy = pltpu.make_async_remote_copy(
            src_ref=out_ref.at[:, own, :],
            dst_ref=out_ref.at[:, own, :],
            send_sem=back_send.at[d - 1],
            recv_sem=back_recv.at[d - 1],
            device_id=device(peer),
            device_id_type=mesh_ids,
        )
        copy.start()
        backs.append(copy)
    for d in range(1, count):
        source = lax.rem(me + count - d, count)
        part = pl.ds(pl.multiple_of(source * band, band), band)
        pltpu.make_async_remote_copy(
            src_ref=out_ref.at[:, part, :],
            dst_ref=out_ref.at[:, part, :],
            send_sem=back_send.at[d - 1],
            recv_sem=back_recv.at[d - 1],
            device_id=device(source),
            device_id_type=mesh_ids,
        ).wait_recv()
    for copy in backs:
        copy.wait_send()


def axis_reduce(x, axis, count, gather, collective_id):
    lead, rows, last = x.shape
    band = rows // count
    kernel = functools.partial(reduce_kernel, axis=axis, count=count, band=band, gather=gather)
    out_rows = rows if gather else band
    vmem = pl.BlockSpec(memory_space=pltpu.VMEM)
    return pl.pallas_call(
        kernel,
        out_shape=jax.ShapeDtypeStruct((lead, out_rows, last), x.dtype),
        in_specs=[vmem],
        out_specs=vmem,
        scratch_shapes=[
            pltpu.VMEM((count - 1, lead, band, last), x.dtype),
            pltpu.SemaphoreType.DMA((count - 1,)),
            pltpu.SemaphoreType.DMA((count - 1,)),
            pltpu.SemaphoreType.DMA((count - 1,)),
            pltpu.SemaphoreType.DMA((count - 1,)),
        ],
        compiler_params=pltpu.CompilerParams(collective_id=collective_id, has_side_effects=True),
    )(x)


def gather_kernel(x_ref, out_ref, send_sem, recv_sem, *, axis, count, band):
    me = lax.axis_index(axis)
    ids = {name: lax.axis_index(name) for name in ("leaf", "row", "col")}

    def device(peer):
        where = dict(ids)
        where[axis] = peer
        return (where["leaf"], where["row"], where["col"])

    mesh_ids = pl.DeviceIdType.MESH
    barrier = pltpu.get_barrier_semaphore()
    for d in range(1, count):
        pl.semaphore_signal(barrier, inc=1, device_id=device(lax.rem(me + d, count)), device_id_type=mesh_ids)
    pl.semaphore_wait(barrier, count - 1)
    own = pl.ds(pl.multiple_of(me * band, band), band)
    sends = []
    for d in range(1, count):
        peer = lax.rem(me + d, count)
        copy = pltpu.make_async_remote_copy(
            src_ref=x_ref,
            dst_ref=out_ref.at[:, own, :],
            send_sem=send_sem.at[d - 1],
            recv_sem=recv_sem.at[d - 1],
            device_id=device(peer),
            device_id_type=mesh_ids,
        )
        copy.start()
        sends.append(copy)
    out_ref[:, own, :] = x_ref[...]
    for d in range(1, count):
        source = lax.rem(me + count - d, count)
        part = pl.ds(pl.multiple_of(source * band, band), band)
        pltpu.make_async_remote_copy(
            src_ref=x_ref,
            dst_ref=out_ref.at[:, part, :],
            send_sem=send_sem.at[d - 1],
            recv_sem=recv_sem.at[d - 1],
            device_id=device(source),
            device_id_type=mesh_ids,
        ).wait_recv()
    for copy in sends:
        copy.wait_send()


def axis_gather(x, axis, count, collective_id):
    lead, band, last = x.shape
    vmem = pl.BlockSpec(memory_space=pltpu.VMEM)
    return pl.pallas_call(
        functools.partial(gather_kernel, axis=axis, count=count, band=band),
        out_shape=jax.ShapeDtypeStruct((lead, band * count, last), x.dtype),
        in_specs=[vmem],
        out_specs=vmem,
        scratch_shapes=[pltpu.SemaphoreType.DMA((count - 1,)), pltpu.SemaphoreType.DMA((count - 1,))],
        compiler_params=pltpu.CompilerParams(collective_id=collective_id, has_side_effects=True),
    )(x)


def body(sigma_top, panels, inverse_diag, slot_lists, parent_links):
    tile = TILE
    row_count = lax.axis_size("row")
    col_count = lax.axis_size("col")
    leaf_count = lax.axis_size("leaf")
    r = lax.axis_index("row")
    c = lax.axis_index("col")
    panel = panels[0]
    inverse = inverse_diag[0]
    picks_all = slot_lists[0]
    parents = parent_links[0]
    nodes = panel.shape[0]
    width = inverse.shape[2]
    own_tiles = width // tile
    slot_count = picks_all.shape[1]
    positions = slot_count + own_tiles
    band = width // row_count

    partial_t = jnp.einsum("vkj,vrk->vjr", inverse, panel, precision=HIGHEST, preferred_element_type=jnp.float32)
    factor_t = axis_reduce(partial_t, "col", col_count, False, 3)
    living = jnp.concatenate([jnp.ones((1, slot_count), jnp.bool_), picks_all >= 0], axis=0)
    live_here = jnp.take(living, r, axis=1).astype(jnp.float32)
    factor_tile = jnp.transpose(factor_t, (0, 2, 1)) * live_here[:, None, None]
    factor_cols = lax.all_gather(factor_tile, "row", axis=1, tiled=True)
    factor_rows = jnp.transpose(axis_gather(factor_t, "col", col_count, 4), (0, 2, 1)) * live_here[:, None, None]

    inverse_band = lax.dynamic_slice_in_dim(inverse, r * band, band, 2)
    partial_gram = mm(jnp.transpose(inverse_band, (0, 2, 1)), inverse)
    gram_piece = lax.psum_scatter(partial_gram, "col", scatter_dimension=2, tiled=True)

    leaf = lax.axis_index("leaf")
    local_rows = sigma_top.shape[0]
    chunk_rows = lax.all_gather(sigma_top, "col", axis=1, tiled=True)
    chunks_per_tile = tile // local_rows
    rounds = []
    for t in range(chunks_per_tile):
        pairs = []
        for src_leaf in range(leaf_count):
            for src_row in range(row_count):
                q = src_leaf * row_count + src_row
                dst_leaf = (q % chunks_per_tile + t) % leaf_count
                dst_row = q // chunks_per_tile
                for col in range(col_count):
                    pairs.append(
                        ((src_leaf * row_count + src_row) * col_count + col,
                         (dst_leaf * row_count + dst_row) * col_count + col)
                    )
        rounds.append(lax.ppermute(chunk_rows, ("leaf", "row", "col"), pairs))
    order = lax.rem(leaf - jnp.arange(chunks_per_tile, dtype=jnp.int32) + 4 * leaf_count, leaf_count)
    sigma_rows = jnp.take(jnp.stack(rounds), order, axis=0).reshape(tile, -1)

    def diag_partial(first, products):
        rows = factor_rows[first:first + products.shape[0]]
        return mm(jnp.transpose(rows, (0, 2, 1)), products)

    def reduce_and_gather(first, products, sent, extra):
        count = products.shape[0]
        piece = axis_reduce(diag_partial(first, products), "row", row_count, False, first)
        piece = piece + gram_piece[first:first + count]
        both = jnp.concatenate([sent, piece] + extra, axis=1)
        everything = lax.all_gather(both, ("row", "col"), axis=0)
        return everything.reshape(row_count, col_count, count, both.shape[1], tile)

    bands_per_tile = tile // band

    def product_col_t(gathered, node, m):
        tiles = lax.dynamic_index_in_dim(gathered[:, :, :, :tile], m, 1, keepdims=False)
        tiles = lax.dynamic_index_in_dim(tiles, node, 1, keepdims=False)
        return jnp.transpose(tiles, (2, 0, 1)).reshape(tile, -1)

    def product_row(gathered, node, q):
        tiles = lax.dynamic_index_in_dim(gathered[:, :, :, :tile], q, 0, keepdims=False)
        tiles = lax.dynamic_index_in_dim(tiles, node, 1, keepdims=False)
        return jnp.transpose(tiles, (1, 0, 2)).reshape(tile, -1)

    def diag_row(gathered, node, m):
        pieces = lax.dynamic_slice_in_dim(gathered[:, :, :, tile:], m * bands_per_tile, bands_per_tile, 0)
        pieces = lax.dynamic_index_in_dim(pieces, node, 2, keepdims=False)
        return jnp.transpose(pieces, (0, 2, 1, 3)).reshape(tile, -1)

    def diag_col(gathered, m, offset):
        pieces = lax.dynamic_index_in_dim(gathered[:, :, :, offset:offset + band], m, 1, keepdims=False)
        return jnp.transpose(pieces, (1, 0, 2, 3)).reshape(pieces.shape[1], -1, tile)

    own_row = jnp.minimum(r, own_tiles - 1)
    upper = r < own_tiles

    product_0 = mm(sigma_rows, factor_cols[0])
    lifted = [
        mm(sigma_rows, scatter_factor(factor_cols[node], picks_all[node - 1], slot_count, tile))[None]
        for node in (1, 2)
    ]
    gathered_0 = reduce_and_gather(0, product_0[None], product_0[None], lifted)

    info_1 = jnp.concatenate(
        [r.astype(jnp.int32)[None], picks_all[0:2].reshape(-1), jnp.zeros((2,), jnp.int32), c.astype(jnp.int32)[None]]
    )
    halves = row_count // own_tiles
    product_1, upper_half = level_products(
        info_1, gathered_0, gathered_0, factor_cols[1:3], 1, tile, band, own_tiles, slot_count,
        tile, tile, halves,
    )
    gathered_1 = reduce_and_gather(1, product_1, upper_half, [])

    info_2 = jnp.concatenate(
        [r.astype(jnp.int32)[None], picks_all[2:nodes - 1].reshape(-1), (parents - 1).astype(jnp.int32),
         c.astype(jnp.int32)[None]]
    )
    (product_2,) = level_products(
        info_2, gathered_1, gathered_0, factor_cols[3:nodes], 2, tile, band, own_tiles, slot_count,
        tile // halves, tile, 0,
    )
    first_2 = 3
    count_2 = product_2.shape[0]
    gram_rows = jnp.zeros((count_2, width, tile), jnp.float32)
    gram_rows = lax.dynamic_update_slice_in_dim(gram_rows, gram_piece[first_2:first_2 + count_2], r * band, 1)
    diag_2 = axis_reduce(diag_partial(first_2, product_2) + gram_rows, "row", row_count, True, 2)

    products = jnp.concatenate([product_0[None], product_1, product_2], axis=0)
    diag_cols = jnp.concatenate(
        [diag_col(gathered_0, c, tile), diag_col(gathered_1, c, tile // halves), diag_2], axis=0
    )
    return (-products)[None], diag_cols[None]


def solution(mesh):
    return jax.shard_map(
        body,
        mesh=mesh,
        in_specs=(
            P(("leaf", "row"), "col"),
            P("leaf", None, "row", "col"),
            P("leaf", None, "col", None),
            P("leaf", None, None),
            P("leaf", None),
        ),
        out_specs=(P("leaf", None, "row", "col"), P("leaf", None, None, "col")),
        check_vma=False,
    )
```

```python
import functools

import jax
import jax.numpy as jnp
from jax import lax
from jax.experimental import pallas as pl
from jax.experimental.pallas import tpu as pltpu
from jax.sharding import PartitionSpec as P

TILE = 128
HIGHEST = lax.Precision.HIGHEST


def mm(a, b):
    return jnp.matmul(a, b, precision=HIGHEST, preferred_element_type=jnp.float32)


def tile_rows(matrix, index, tile):
    return lax.dynamic_slice_in_dim(matrix, index * tile, tile, 0)


def tile_cols(matrix, index, tile):
    return lax.dynamic_slice_in_dim(matrix, index * tile, tile, 1)


def scatter_factor(factor_col, slots, positions, tile):
    tiles = factor_col.reshape(slots.shape[0], tile, factor_col.shape[1])
    hits = slots[:, None] == jnp.arange(positions, dtype=slots.dtype)[None, :]
    present = jnp.any(hits, axis=0)
    source = jnp.argmax(hits, axis=0)
    moved = jnp.take(tiles, source, axis=0)
    moved = jnp.where(present[:, None, None], moved, 0.0)
    return moved.reshape(positions * tile, factor_col.shape[1])


def dot_hi(a, b):
    return jnp.dot(a, b, precision=HIGHEST, preferred_element_type=jnp.float32)


def dot_t_hi(a, b):
    return lax.dot_general(
        a, b, (((0,), (0,)), ((), ())), precision=HIGHEST, preferred_element_type=jnp.float32
    )


def level_kernel(info_ref, par_ref, low_ref, fac_ref, out_ref, *rest, level, tile, band, own_tiles, slot_count,
                 par_prow, low_prow, halves):
    count = out_ref.shape[0]
    split = tile // band
    r = info_ref[0]
    col = info_ref[1 + count * slot_count + count]
    own = lax.rem(r, own_tiles)

    def p_tile(ref, prow, node, q, m):
        if prow == tile:
            return ref[q, m, node, 0:tile, :]
        parts = tile // prow
        return jnp.concatenate([ref[q + j * own_tiles, m, node, 0:prow, :] for j in range(parts)], axis=0)

    def d_tile(ref, prow, node, a, m):
        return jnp.concatenate([ref[a * split + h, m, node, prow:prow + band, :] for h in range(split)], axis=0)

    for i in range(count):
        base = 1 + i * slot_count
        parent = info_ref[1 + count * slot_count + i]
        factor = [fac_ref[i, k * tile:(k + 1) * tile, :] for k in range(slot_count)]
        picks = [jnp.clip(info_ref[base + k], 0, slot_count - 1) for k in range(slot_count)]
        source = info_ref[base + jnp.maximum(r, own_tiles)]

        upper = dot_hi(d_tile(par_ref, par_prow, parent, own, 0), factor[0])
        for k in range(1, own_tiles):
            upper += dot_hi(d_tile(par_ref, par_prow, parent, own, k), factor[k])
        for k in range(own_tiles, slot_count):
            pick = picks[k] if par_prow == tile else jnp.minimum(picks[k], own_tiles - 1)
            upper -= dot_t_hi(p_tile(par_ref, par_prow, parent, pick, own), factor[k])

        if halves:
            half_ref = rest[0]
            rows = tile // halves
            which = r // own_tiles
            half = upper[0:rows]
            for j in range(1, halves):
                half = jnp.where(which == j, upper[j * rows:(j + 1) * rows], half)
            half_ref[i] = half

        @pl.when(r < own_tiles)
        def _():
            out_ref[i] = upper

        @pl.when(jnp.logical_and(r >= own_tiles, source >= 0))
        def _():
            if level == 1:
                s = jnp.clip(source, 0, slot_count - 1)
                acc = low_ref[i, pl.ds(pl.multiple_of(s * tile, tile), tile), :]
                for k in range(own_tiles):
                    acc -= dot_hi(p_tile(par_ref, par_prow, parent, s, k), factor[k])
            else:
                s = jnp.clip(source, 0, own_tiles - 1)
                acc = -dot_hi(p_tile(par_ref, par_prow, parent, s, 0), factor[0])
                for k in range(1, own_tiles):
                    acc -= dot_hi(p_tile(par_ref, par_prow, parent, s, k), factor[k])
                for k in range(own_tiles, slot_count):
                    q = jnp.minimum(picks[k], own_tiles - 1)
                    acc += dot_hi(d_tile(low_ref, low_prow, 0, s, q), factor[k])
            out_ref[i] = acc

        @pl.when(jnp.logical_and(r >= own_tiles, source < 0))
        def _():
            out_ref[i] = jnp.zeros((tile, tile), jnp.float32)


def level_products(info, parent_data, low_data, factors, level, tile, band, own_tiles, slot_count,
                   par_prow, low_prow, halves):
    kernel = functools.partial(
        level_kernel, level=level, tile=tile, band=band, own_tiles=own_tiles, slot_count=slot_count,
        par_prow=par_prow, low_prow=low_prow, halves=halves,
    )
    vmem = pl.BlockSpec(memory_space=pltpu.VMEM)
    count = factors.shape[0]
    shapes = [jax.ShapeDtypeStruct((count, tile, tile), jnp.float32)]
    if halves:
        shapes.append(jax.ShapeDtypeStruct((count, tile // halves, tile), jnp.float32))
    return pl.pallas_call(
        kernel,
        out_shape=tuple(shapes),
        in_specs=[pl.BlockSpec(memory_space=pltpu.SMEM), vmem, vmem, vmem],
        out_specs=tuple([vmem] * len(shapes)),
    )(info, parent_data, low_data, factors)


def reduce_kernel(x_ref, out_ref, recv_ref, send_sem, recv_sem, back_send, back_recv, *, axis, count, band, gather):
    me = lax.axis_index(axis)
    ids = {name: lax.axis_index(name) for name in ("leaf", "row", "col")}

    def device(peer):
        where = dict(ids)
        where[axis] = peer
        return (where["leaf"], where["row"], where["col"])

    mesh_ids = pl.DeviceIdType.MESH
    barrier = pltpu.get_barrier_semaphore()
    for d in range(1, count):
        pl.semaphore_signal(barrier, inc=1, device_id=device(lax.rem(me + d, count)), device_id_type=mesh_ids)
    pl.semaphore_wait(barrier, count - 1)

    sends = []
    for d in range(1, count):
        peer = lax.rem(me + d, count)
        copy = pltpu.make_async_remote_copy(
            src_ref=x_ref.at[:, pl.ds(pl.multiple_of(peer * band, band), band), :],
            dst_ref=recv_ref.at[d - 1],
            send_sem=send_sem.at[d - 1],
            recv_sem=recv_sem.at[d - 1],
            device_id=device(peer),
            device_id_type=mesh_ids,
        )
        copy.start()
        sends.append(copy)
    for copy in sends:
        copy.wait_recv()
    for copy in sends:
        copy.wait_send()
    own = pl.ds(pl.multiple_of(me * band, band), band)
    total = x_ref[:, own, :]
    for d in range(1, count):
        total = total + recv_ref[d - 1]
    if not gather:
        out_ref[...] = total
        return
    out_ref[:, own, :] = total
    backs = []
    for d in range(1, count):
        peer = lax.rem(me + d, count)
        copy = pltpu.make_async_remote_copy(
            src_ref=out_ref.at[:, own, :],
            dst_ref=out_ref.at[:, own, :],
            send_sem=back_send.at[d - 1],
            recv_sem=back_recv.at[d - 1],
            device_id=device(peer),
            device_id_type=mesh_ids,
        )
        copy.start()
        backs.append(copy)
    for d in range(1, count):
        source = lax.rem(me + count - d, count)
        part = pl.ds(pl.multiple_of(source * band, band), band)
        pltpu.make_async_remote_copy(
            src_ref=out_ref.at[:, part, :],
            dst_ref=out_ref.at[:, part, :],
            send_sem=back_send.at[d - 1],
            recv_sem=back_recv.at[d - 1],
            device_id=device(source),
            device_id_type=mesh_ids,
        ).wait_recv()
    for copy in backs:
        copy.wait_send()


def axis_reduce(x, axis, count, gather, collective_id):
    lead, rows, last = x.shape
    band = rows // count
    kernel = functools.partial(reduce_kernel, axis=axis, count=count, band=band, gather=gather)
    out_rows = rows if gather else band
    vmem = pl.BlockSpec(memory_space=pltpu.VMEM)
    return pl.pallas_call(
        kernel,
        out_shape=jax.ShapeDtypeStruct((lead, out_rows, last), x.dtype),
        in_specs=[vmem],
        out_specs=vmem,
        scratch_shapes=[
            pltpu.VMEM((count - 1, lead, band, last), x.dtype),
            pltpu.SemaphoreType.DMA((count - 1,)),
            pltpu.SemaphoreType.DMA((count - 1,)),
            pltpu.SemaphoreType.DMA((count - 1,)),
            pltpu.SemaphoreType.DMA((count - 1,)),
        ],
        compiler_params=pltpu.CompilerParams(collective_id=collective_id, has_side_effects=True),
    )(x)


def gather_kernel(x_ref, out_ref, send_sem, recv_sem, *, axis, count, band):
    me = lax.axis_index(axis)
    ids = {name: lax.axis_index(name) for name in ("leaf", "row", "col")}

    def device(peer):
        where = dict(ids)
        where[axis] = peer
        return (where["leaf"], where["row"], where["col"])

    mesh_ids = pl.DeviceIdType.MESH
    barrier = pltpu.get_barrier_semaphore()
    for d in range(1, count):
        pl.semaphore_signal(barrier, inc=1, device_id=device(lax.rem(me + d, count)), device_id_type=mesh_ids)
    pl.semaphore_wait(barrier, count - 1)
    own = pl.ds(pl.multiple_of(me * band, band), band)
    sends = []
    for d in range(1, count):
        peer = lax.rem(me + d, count)
        copy = pltpu.make_async_remote_copy(
            src_ref=x_ref,
            dst_ref=out_ref.at[:, own, :],
            send_sem=send_sem.at[d - 1],
            recv_sem=recv_sem.at[d - 1],
            device_id=device(peer),
            device_id_type=mesh_ids,
        )
        copy.start()
        sends.append(copy)
    out_ref[:, own, :] = x_ref[...]
    for d in range(1, count):
        source = lax.rem(me + count - d, count)
        part = pl.ds(pl.multiple_of(source * band, band), band)
        pltpu.make_async_remote_copy(
            src_ref=x_ref,
            dst_ref=out_ref.at[:, part, :],
            send_sem=send_sem.at[d - 1],
            recv_sem=recv_sem.at[d - 1],
            device_id=device(source),
            device_id_type=mesh_ids,
        ).wait_recv()
    for copy in sends:
        copy.wait_send()


def axis_gather(x, axis, count, collective_id):
    lead, band, last = x.shape
    vmem = pl.BlockSpec(memory_space=pltpu.VMEM)
    return pl.pallas_call(
        functools.partial(gather_kernel, axis=axis, count=count, band=band),
        out_shape=jax.ShapeDtypeStruct((lead, band * count, last), x.dtype),
        in_specs=[vmem],
        out_specs=vmem,
        scratch_shapes=[pltpu.SemaphoreType.DMA((count - 1,)), pltpu.SemaphoreType.DMA((count - 1,))],
        compiler_params=pltpu.CompilerParams(collective_id=collective_id, has_side_effects=True),
    )(x)


def body(sigma_top, panels, inverse_diag, slot_lists, parent_links):
    tile = TILE
    row_count = lax.axis_size("row")
    col_count = lax.axis_size("col")
    leaf_count = lax.axis_size("leaf")
    r = lax.axis_index("row")
    c = lax.axis_index("col")
    panel = panels[0]
    inverse = inverse_diag[0]
    picks_all = slot_lists[0]
    parents = parent_links[0]
    nodes = panel.shape[0]
    width = inverse.shape[2]
    own_tiles = width // tile
    slot_count = picks_all.shape[1]
    positions = slot_count + own_tiles
    band = width // row_count

    partial_factor = mm(panel, inverse)
    factor_rows = axis_reduce(partial_factor, "col", col_count, True, 3)
    living = jnp.concatenate([jnp.ones((1, slot_count), jnp.bool_), picks_all >= 0], axis=0)
    live_here = jnp.take(living, r, axis=1).astype(jnp.float32)
    factor_rows = factor_rows * live_here[:, None, None]
    factor_tile = lax.dynamic_slice_in_dim(factor_rows, c * tile, tile, 2)
    factor_cols = lax.all_gather(factor_tile, "row", axis=1, tiled=True)

    inverse_band = lax.dynamic_slice_in_dim(inverse, r * band, band, 2)
    partial_gram = mm(jnp.transpose(inverse_band, (0, 2, 1)), inverse)
    gram_piece = lax.psum_scatter(partial_gram, "col", scatter_dimension=2, tiled=True)

    leaf = lax.axis_index("leaf")
    local_rows = sigma_top.shape[0]
    chunk_rows = lax.all_gather(sigma_top, "col", axis=1, tiled=True)
    chunks_per_tile = tile // local_rows
    rounds = []
    for t in range(chunks_per_tile):
        pairs = []
        for src_leaf in range(leaf_count):
            for src_row in range(row_count):
                q = src_leaf * row_count + src_row
                dst_leaf = (q % chunks_per_tile + t) % leaf_count
                dst_row = q // chunks_per_tile
                for col in range(col_count):
                    pairs.append(
                        ((src_leaf * row_count + src_row) * col_count + col,
                         (dst_leaf * row_count + dst_row) * col_count + col)
                    )
        rounds.append(lax.ppermute(chunk_rows, ("leaf", "row", "col"), pairs))
    order = lax.rem(leaf - jnp.arange(chunks_per_tile, dtype=jnp.int32) + 4 * leaf_count, leaf_count)
    sigma_rows = jnp.take(jnp.stack(rounds), order, axis=0).reshape(tile, -1)

    def diag_partial(first, products):
        rows = factor_rows[first:first + products.shape[0]]
        return mm(jnp.transpose(rows, (0, 2, 1)), products)

    def reduce_and_gather(first, products, sent, extra, tied=None):
        count = products.shape[0]
        piece = axis_reduce(diag_partial(first, products), "row", row_count, False, first)
        piece = piece + gram_piece[first:first + count]
        if tied is not None:
            piece, tied = lax.optimization_barrier((piece, tied))
            tied_out.append(tied)
        both = jnp.concatenate([sent, piece] + extra, axis=1)
        everything = lax.all_gather(both, ("row", "col"), axis=0)
        return everything.reshape(row_count, col_count, count, both.shape[1], tile)

    bands_per_tile = tile // band

    def product_col_t(gathered, node, m):
        tiles = lax.dynamic_index_in_dim(gathered[:, :, :, :tile], m, 1, keepdims=False)
        tiles = lax.dynamic_index_in_dim(tiles, node, 1, keepdims=False)
        return jnp.transpose(tiles, (2, 0, 1)).reshape(tile, -1)

    def product_row(gathered, node, q):
        tiles = lax.dynamic_index_in_dim(gathered[:, :, :, :tile], q, 0, keepdims=False)
        tiles = lax.dynamic_index_in_dim(tiles, node, 1, keepdims=False)
        return jnp.transpose(tiles, (1, 0, 2)).reshape(tile, -1)

    def diag_row(gathered, node, m):
        pieces = lax.dynamic_slice_in_dim(gathered[:, :, :, tile:], m * bands_per_tile, bands_per_tile, 0)
        pieces = lax.dynamic_index_in_dim(pieces, node, 2, keepdims=False)
        return jnp.transpose(pieces, (0, 2, 1, 3)).reshape(tile, -1)

    def diag_col(gathered, m, offset):
        pieces = lax.dynamic_index_in_dim(gathered[:, :, :, offset:offset + band], m, 1, keepdims=False)
        return jnp.transpose(pieces, (1, 0, 2, 3)).reshape(pieces.shape[1], -1, tile)

    own_row = jnp.minimum(r, own_tiles - 1)
    upper = r < own_tiles

    product_0 = mm(sigma_rows, factor_cols[0])
    lifted = [
        mm(sigma_rows, scatter_factor(factor_cols[node], picks_all[node - 1], slot_count, tile))[None]
        for node in (1, 2)
    ]
    tied_out = []
    gathered_0 = reduce_and_gather(0, product_0[None], product_0[None], [], jnp.concatenate(lifted, axis=0))
    lifted_cols = axis_gather(tied_out[0], "row", row_count, 4)

    info_1 = jnp.concatenate(
        [r.astype(jnp.int32)[None], picks_all[0:2].reshape(-1), jnp.zeros((2,), jnp.int32), c.astype(jnp.int32)[None]]
    )
    halves = row_count // own_tiles
    product_1, upper_half = level_products(
        info_1, gathered_0, lifted_cols, factor_cols[1:3], 1, tile, band, own_tiles, slot_count,
        tile, tile, halves,
    )
    gathered_1 = reduce_and_gather(1, product_1, upper_half, [])

    info_2 = jnp.concatenate(
        [r.astype(jnp.int32)[None], picks_all[2:nodes - 1].reshape(-1), (parents - 1).astype(jnp.int32),
         c.astype(jnp.int32)[None]]
    )
    (product_2,) = level_products(
        info_2, gathered_1, gathered_0, factor_cols[3:nodes], 2, tile, band, own_tiles, slot_count,
        tile // halves, tile, 0,
    )
    first_2 = 3
    count_2 = product_2.shape[0]
    gram_rows = jnp.zeros((count_2, width, tile), jnp.float32)
    gram_rows = lax.dynamic_update_slice_in_dim(gram_rows, gram_piece[first_2:first_2 + count_2], r * band, 1)
    diag_2 = axis_reduce(diag_partial(first_2, product_2) + gram_rows, "row", row_count, True, 2)

    products = jnp.concatenate([product_0[None], product_1, product_2], axis=0)
    diag_cols = jnp.concatenate(
        [diag_col(gathered_0, c, tile), diag_col(gathered_1, c, tile // halves), diag_2], axis=0
    )
    return (-products)[None], diag_cols[None]


def solution(mesh):
    return jax.shard_map(
        body,
        mesh=mesh,
        in_specs=(
            P(("leaf", "row"), "col"),
            P("leaf", None, "row", "col"),
            P("leaf", None, "col", None),
            P("leaf", None, None),
            P("leaf", None),
        ),
        out_specs=(P("leaf", None, "row", "col"), P("leaf", None, None, "col")),
        check_vma=False,
    )
```

```python
import functools

import jax
import jax.numpy as jnp
from jax import lax
from jax.experimental import pallas as pl
from jax.experimental.pallas import tpu as pltpu
from jax.sharding import PartitionSpec as P

TILE = 128
HIGHEST = lax.Precision.HIGHEST


def mm(a, b):
    return jnp.matmul(a, b, precision=HIGHEST, preferred_element_type=jnp.float32)


def tile_rows(matrix, index, tile):
    return lax.dynamic_slice_in_dim(matrix, index * tile, tile, 0)


def tile_cols(matrix, index, tile):
    return lax.dynamic_slice_in_dim(matrix, index * tile, tile, 1)


def scatter_factor(factor_col, slots, positions, tile):
    tiles = factor_col.reshape(slots.shape[0], tile, factor_col.shape[1])
    hits = slots[:, None] == jnp.arange(positions, dtype=slots.dtype)[None, :]
    present = jnp.any(hits, axis=0)
    source = jnp.argmax(hits, axis=0)
    moved = jnp.take(tiles, source, axis=0)
    moved = jnp.where(present[:, None, None], moved, 0.0)
    return moved.reshape(positions * tile, factor_col.shape[1])


def dot_hi(a, b):
    return jnp.dot(a, b, precision=HIGHEST, preferred_element_type=jnp.float32)


def dot_t_hi(a, b):
    return lax.dot_general(
        a, b, (((0,), (0,)), ((), ())), precision=HIGHEST, preferred_element_type=jnp.float32
    )


def level_kernel(info_ref, par_ref, low_ref, fac_ref, out_ref, *rest, level, tile, band, own_tiles, slot_count,
                 par_prow, low_prow, halves):
    count = out_ref.shape[0]
    split = tile // band
    r = info_ref[0]
    col = info_ref[1 + count * slot_count + count]
    own = lax.rem(r, own_tiles)

    def p_tile(ref, prow, node, q, m):
        if prow == tile:
            return ref[q, m, node, 0:tile, :]
        parts = tile // prow
        return jnp.concatenate([ref[q + j * own_tiles, m, node, 0:prow, :] for j in range(parts)], axis=0)

    def d_tile(ref, prow, node, a, m):
        return jnp.concatenate([ref[a * split + h, m, node, prow:prow + band, :] for h in range(split)], axis=0)

    for i in range(count):
        base = 1 + i * slot_count
        parent = info_ref[1 + count * slot_count + i]
        factor = [fac_ref[i, k * tile:(k + 1) * tile, :] for k in range(slot_count)]
        picks = [jnp.clip(info_ref[base + k], 0, slot_count - 1) for k in range(slot_count)]
        source = info_ref[base + jnp.maximum(r, own_tiles)]

        upper = dot_hi(d_tile(par_ref, par_prow, parent, own, 0), factor[0])
        for k in range(1, own_tiles):
            upper += dot_hi(d_tile(par_ref, par_prow, parent, own, k), factor[k])
        for k in range(own_tiles, slot_count):
            pick = picks[k] if par_prow == tile else jnp.minimum(picks[k], own_tiles - 1)
            upper -= dot_t_hi(p_tile(par_ref, par_prow, parent, pick, own), factor[k])

        if halves:
            half_ref = rest[0]
            rows = tile // halves
            which = r // own_tiles
            half = upper[0:rows]
            for j in range(1, halves):
                half = jnp.where(which == j, upper[j * rows:(j + 1) * rows], half)
            half_ref[i] = half

        @pl.when(r < own_tiles)
        def _():
            out_ref[i] = upper

        @pl.when(jnp.logical_and(r >= own_tiles, source >= 0))
        def _():
            if level == 1:
                s = jnp.clip(source, 0, slot_count - 1)
                acc = low_ref[i, pl.ds(pl.multiple_of(s * tile, tile), tile), :]
                for k in range(own_tiles):
                    acc -= dot_hi(p_tile(par_ref, par_prow, parent, s, k), factor[k])
            else:
                s = jnp.clip(source, 0, own_tiles - 1)
                acc = -dot_hi(p_tile(par_ref, par_prow, parent, s, 0), factor[0])
                for k in range(1, own_tiles):
                    acc -= dot_hi(p_tile(par_ref, par_prow, parent, s, k), factor[k])
                for k in range(own_tiles, slot_count):
                    q = jnp.minimum(picks[k], own_tiles - 1)
                    acc += dot_hi(d_tile(low_ref, low_prow, 0, s, q), factor[k])
            out_ref[i] = acc

        @pl.when(jnp.logical_and(r >= own_tiles, source < 0))
        def _():
            out_ref[i] = jnp.zeros((tile, tile), jnp.float32)


def level_products(info, parent_data, low_data, factors, level, tile, band, own_tiles, slot_count,
                   par_prow, low_prow, halves):
    kernel = functools.partial(
        level_kernel, level=level, tile=tile, band=band, own_tiles=own_tiles, slot_count=slot_count,
        par_prow=par_prow, low_prow=low_prow, halves=halves,
    )
    vmem = pl.BlockSpec(memory_space=pltpu.VMEM)
    count = factors.shape[0]
    shapes = [jax.ShapeDtypeStruct((count, tile, tile), jnp.float32)]
    if halves:
        shapes.append(jax.ShapeDtypeStruct((count, tile // halves, tile), jnp.float32))
    return pl.pallas_call(
        kernel,
        out_shape=tuple(shapes),
        in_specs=[pl.BlockSpec(memory_space=pltpu.SMEM), vmem, vmem, vmem],
        out_specs=tuple([vmem] * len(shapes)),
    )(info, parent_data, low_data, factors)


def reduce_kernel(x_ref, out_ref, recv_ref, send_sem, recv_sem, back_send, back_recv, *, axis, count, band, gather):
    me = lax.axis_index(axis)
    ids = {name: lax.axis_index(name) for name in ("leaf", "row", "col")}

    def device(peer):
        where = dict(ids)
        where[axis] = peer
        return (where["leaf"], where["row"], where["col"])

    mesh_ids = pl.DeviceIdType.MESH
    barrier = pltpu.get_barrier_semaphore()
    for d in range(1, count):
        pl.semaphore_signal(barrier, inc=1, device_id=device(lax.rem(me + d, count)), device_id_type=mesh_ids)
    pl.semaphore_wait(barrier, count - 1)

    sends = []
    for d in range(1, count):
        peer = lax.rem(me + d, count)
        copy = pltpu.make_async_remote_copy(
            src_ref=x_ref.at[:, pl.ds(pl.multiple_of(peer * band, band), band), :],
            dst_ref=recv_ref.at[d - 1],
            send_sem=send_sem.at[d - 1],
            recv_sem=recv_sem.at[d - 1],
            device_id=device(peer),
            device_id_type=mesh_ids,
        )
        copy.start()
        sends.append(copy)
    for copy in sends:
        copy.wait_recv()
    for copy in sends:
        copy.wait_send()
    own = pl.ds(pl.multiple_of(me * band, band), band)
    total = x_ref[:, own, :]
    for d in range(1, count):
        total = total + recv_ref[d - 1]
    if not gather:
        out_ref[...] = total
        return
    out_ref[:, own, :] = total
    backs = []
    for d in range(1, count):
        peer = lax.rem(me + d, count)
        copy = pltpu.make_async_remote_copy(
            src_ref=out_ref.at[:, own, :],
            dst_ref=out_ref.at[:, own, :],
            send_sem=back_send.at[d - 1],
            recv_sem=back_recv.at[d - 1],
            device_id=device(peer),
            device_id_type=mesh_ids,
        )
        copy.start()
        backs.append(copy)
    for d in range(1, count):
        source = lax.rem(me + count - d, count)
        part = pl.ds(pl.multiple_of(source * band, band), band)
        pltpu.make_async_remote_copy(
            src_ref=out_ref.at[:, part, :],
            dst_ref=out_ref.at[:, part, :],
            send_sem=back_send.at[d - 1],
            recv_sem=back_recv.at[d - 1],
            device_id=device(source),
            device_id_type=mesh_ids,
        ).wait_recv()
    for copy in backs:
        copy.wait_send()


def axis_reduce(x, axis, count, gather, collective_id):
    lead, rows, last = x.shape
    band = rows // count
    kernel = functools.partial(reduce_kernel, axis=axis, count=count, band=band, gather=gather)
    out_rows = rows if gather else band
    vmem = pl.BlockSpec(memory_space=pltpu.VMEM)
    return pl.pallas_call(
        kernel,
        out_shape=jax.ShapeDtypeStruct((lead, out_rows, last), x.dtype),
        in_specs=[vmem],
        out_specs=vmem,
        scratch_shapes=[
            pltpu.VMEM((count - 1, lead, band, last), x.dtype),
            pltpu.SemaphoreType.DMA((count - 1,)),
            pltpu.SemaphoreType.DMA((count - 1,)),
            pltpu.SemaphoreType.DMA((count - 1,)),
            pltpu.SemaphoreType.DMA((count - 1,)),
        ],
        compiler_params=pltpu.CompilerParams(collective_id=collective_id, has_side_effects=True),
    )(x)


def gather_kernel(x_ref, out_ref, send_sem, recv_sem, *, axis, count, band):
    me = lax.axis_index(axis)
    ids = {name: lax.axis_index(name) for name in ("leaf", "row", "col")}

    def device(peer):
        where = dict(ids)
        where[axis] = peer
        return (where["leaf"], where["row"], where["col"])

    mesh_ids = pl.DeviceIdType.MESH
    barrier = pltpu.get_barrier_semaphore()
    for d in range(1, count):
        pl.semaphore_signal(barrier, inc=1, device_id=device(lax.rem(me + d, count)), device_id_type=mesh_ids)
    pl.semaphore_wait(barrier, count - 1)
    own = pl.ds(pl.multiple_of(me * band, band), band)
    sends = []
    for d in range(1, count):
        peer = lax.rem(me + d, count)
        copy = pltpu.make_async_remote_copy(
            src_ref=x_ref,
            dst_ref=out_ref.at[:, own, :],
            send_sem=send_sem.at[d - 1],
            recv_sem=recv_sem.at[d - 1],
            device_id=device(peer),
            device_id_type=mesh_ids,
        )
        copy.start()
        sends.append(copy)
    out_ref[:, own, :] = x_ref[...]
    for d in range(1, count):
        source = lax.rem(me + count - d, count)
        part = pl.ds(pl.multiple_of(source * band, band), band)
        pltpu.make_async_remote_copy(
            src_ref=x_ref,
            dst_ref=out_ref.at[:, part, :],
            send_sem=send_sem.at[d - 1],
            recv_sem=recv_sem.at[d - 1],
            device_id=device(source),
            device_id_type=mesh_ids,
        ).wait_recv()
    for copy in sends:
        copy.wait_send()


def axis_gather(x, axis, count, collective_id):
    lead, band, last = x.shape
    vmem = pl.BlockSpec(memory_space=pltpu.VMEM)
    return pl.pallas_call(
        functools.partial(gather_kernel, axis=axis, count=count, band=band),
        out_shape=jax.ShapeDtypeStruct((lead, band * count, last), x.dtype),
        in_specs=[vmem],
        out_specs=vmem,
        scratch_shapes=[pltpu.SemaphoreType.DMA((count - 1,)), pltpu.SemaphoreType.DMA((count - 1,))],
        compiler_params=pltpu.CompilerParams(collective_id=collective_id, has_side_effects=True),
    )(x)


def body(sigma_top, panels, inverse_diag, slot_lists, parent_links):
    tile = TILE
    row_count = lax.axis_size("row")
    col_count = lax.axis_size("col")
    leaf_count = lax.axis_size("leaf")
    r = lax.axis_index("row")
    c = lax.axis_index("col")
    panel = panels[0]
    inverse = inverse_diag[0]
    picks_all = slot_lists[0]
    parents = parent_links[0]
    nodes = panel.shape[0]
    width = inverse.shape[2]
    own_tiles = width // tile
    slot_count = picks_all.shape[1]
    positions = slot_count + own_tiles
    band = width // row_count

    partial_factor = mm(panel, inverse)
    factor_rows = axis_reduce(partial_factor, "col", col_count, True, 3)
    inverse_band = lax.dynamic_slice_in_dim(inverse, r * band, band, 2)
    partial_gram = mm(jnp.transpose(inverse_band, (0, 2, 1)), inverse)
    partial_gram, factor_rows = lax.optimization_barrier((partial_gram, factor_rows))
    living = jnp.concatenate([jnp.ones((1, slot_count), jnp.bool_), picks_all >= 0], axis=0)
    live_here = jnp.take(living, r, axis=1).astype(jnp.float32)
    factor_rows = factor_rows * live_here[:, None, None]
    factor_tile = lax.dynamic_slice_in_dim(factor_rows, c * tile, tile, 2)
    factor_cols = lax.all_gather(factor_tile, "row", axis=1, tiled=True)

    gram_piece = lax.psum_scatter(partial_gram, "col", scatter_dimension=2, tiled=True)

    leaf = lax.axis_index("leaf")
    local_rows = sigma_top.shape[0]
    chunk_rows = lax.all_gather(sigma_top, "col", axis=1, tiled=True)
    chunks_per_tile = tile // local_rows
    rounds = []
    for t in range(chunks_per_tile):
        pairs = []
        for src_leaf in range(leaf_count):
            for src_row in range(row_count):
                q = src_leaf * row_count + src_row
                dst_leaf = (q % chunks_per_tile + t) % leaf_count
                dst_row = q // chunks_per_tile
                for col in range(col_count):
                    pairs.append(
                        ((src_leaf * row_count + src_row) * col_count + col,
                         (dst_leaf * row_count + dst_row) * col_count + col)
                    )
        rounds.append(lax.ppermute(chunk_rows, ("leaf", "row", "col"), pairs))
    order = lax.rem(leaf - jnp.arange(chunks_per_tile, dtype=jnp.int32) + 4 * leaf_count, leaf_count)
    sigma_rows = jnp.take(jnp.stack(rounds), order, axis=0).reshape(tile, -1)

    def diag_partial(first, products):
        rows = factor_rows[first:first + products.shape[0]]
        return mm(jnp.transpose(rows, (0, 2, 1)), products)

    def reduce_and_gather(first, products, sent, extra, tied=None):
        count = products.shape[0]
        piece = axis_reduce(diag_partial(first, products), "row", row_count, False, first)
        piece = piece + gram_piece[first:first + count]
        if tied is not None:
            piece, tied = lax.optimization_barrier((piece, tied))
            tied_out.append(tied)
        both = jnp.concatenate([sent, piece] + extra, axis=1)
        everything = lax.all_gather(both, ("row", "col"), axis=0)
        return everything.reshape(row_count, col_count, count, both.shape[1], tile)

    bands_per_tile = tile // band

    def product_col_t(gathered, node, m):
        tiles = lax.dynamic_index_in_dim(gathered[:, :, :, :tile], m, 1, keepdims=False)
        tiles = lax.dynamic_index_in_dim(tiles, node, 1, keepdims=False)
        return jnp.transpose(tiles, (2, 0, 1)).reshape(tile, -1)

    def product_row(gathered, node, q):
        tiles = lax.dynamic_index_in_dim(gathered[:, :, :, :tile], q, 0, keepdims=False)
        tiles = lax.dynamic_index_in_dim(tiles, node, 1, keepdims=False)
        return jnp.transpose(tiles, (1, 0, 2)).reshape(tile, -1)

    def diag_row(gathered, node, m):
        pieces = lax.dynamic_slice_in_dim(gathered[:, :, :, tile:], m * bands_per_tile, bands_per_tile, 0)
        pieces = lax.dynamic_index_in_dim(pieces, node, 2, keepdims=False)
        return jnp.transpose(pieces, (0, 2, 1, 3)).reshape(tile, -1)

    def diag_col(gathered, m, offset):
        pieces = lax.dynamic_index_in_dim(gathered[:, :, :, offset:offset + band], m, 1, keepdims=False)
        return jnp.transpose(pieces, (1, 0, 2, 3)).reshape(pieces.shape[1], -1, tile)

    own_row = jnp.minimum(r, own_tiles - 1)
    upper = r < own_tiles

    product_0 = mm(sigma_rows, factor_cols[0])
    lifted = [
        mm(sigma_rows, scatter_factor(factor_cols[node], picks_all[node - 1], slot_count, tile))[None]
        for node in (1, 2)
    ]
    tied_out = []
    gathered_0 = reduce_and_gather(0, product_0[None], product_0[None], [], jnp.concatenate(lifted, axis=0))
    lifted_cols = axis_gather(tied_out[0], "row", row_count, 4)

    info_1 = jnp.concatenate(
        [r.astype(jnp.int32)[None], picks_all[0:2].reshape(-1), jnp.zeros((2,), jnp.int32), c.astype(jnp.int32)[None]]
    )
    halves = row_count // own_tiles
    product_1, upper_half = level_products(
        info_1, gathered_0, lifted_cols, factor_cols[1:3], 1, tile, band, own_tiles, slot_count,
        tile, tile, halves,
    )
    gathered_1 = reduce_and_gather(1, product_1, upper_half, [])

    info_2 = jnp.concatenate(
        [r.astype(jnp.int32)[None], picks_all[2:nodes - 1].reshape(-1), (parents - 1).astype(jnp.int32),
         c.astype(jnp.int32)[None]]
    )
    (product_2,) = level_products(
        info_2, gathered_1, gathered_0, factor_cols[3:nodes], 2, tile, band, own_tiles, slot_count,
        tile // halves, tile, 0,
    )
    first_2 = 3
    count_2 = product_2.shape[0]
    gram_rows = jnp.zeros((count_2, width, tile), jnp.float32)
    gram_rows = lax.dynamic_update_slice_in_dim(gram_rows, gram_piece[first_2:first_2 + count_2], r * band, 1)
    diag_2 = axis_reduce(diag_partial(first_2, product_2) + gram_rows, "row", row_count, True, 2)

    products = jnp.concatenate([product_0[None], product_1, product_2], axis=0)
    diag_cols = jnp.concatenate(
        [diag_col(gathered_0, c, tile), diag_col(gathered_1, c, tile // halves), diag_2], axis=0
    )
    return (-products)[None], diag_cols[None]


def solution(mesh):
    return jax.shard_map(
        body,
        mesh=mesh,
        in_specs=(
            P(("leaf", "row"), "col"),
            P("leaf", None, "row", "col"),
            P("leaf", None, "col", None),
            P("leaf", None, None),
            P("leaf", None),
        ),
        out_specs=(P("leaf", None, "row", "col"), P("leaf", None, None, "col")),
        check_vma=False,
    )
```

```python
import functools

import jax
import jax.numpy as jnp
from jax import lax
from jax.experimental import pallas as pl
from jax.experimental.pallas import tpu as pltpu
from jax.sharding import PartitionSpec as P

TILE = 128
HIGHEST = lax.Precision.HIGHEST


def mm(a, b):
    return jnp.matmul(a, b, precision=HIGHEST, preferred_element_type=jnp.float32)


def tile_rows(matrix, index, tile):
    return lax.dynamic_slice_in_dim(matrix, index * tile, tile, 0)


def tile_cols(matrix, index, tile):
    return lax.dynamic_slice_in_dim(matrix, index * tile, tile, 1)


def scatter_factor(factor_col, slots, positions, tile):
    tiles = factor_col.reshape(slots.shape[0], tile, factor_col.shape[1])
    hits = slots[:, None] == jnp.arange(positions, dtype=slots.dtype)[None, :]
    present = jnp.any(hits, axis=0)
    source = jnp.argmax(hits, axis=0)
    moved = jnp.take(tiles, source, axis=0)
    moved = jnp.where(present[:, None, None], moved, 0.0)
    return moved.reshape(positions * tile, factor_col.shape[1])


def dot_hi(a, b):
    return jnp.dot(a, b, precision=HIGHEST, preferred_element_type=jnp.float32)


def dot_t_hi(a, b):
    return lax.dot_general(
        a, b, (((0,), (0,)), ((), ())), precision=HIGHEST, preferred_element_type=jnp.float32
    )


def level_kernel(info_ref, par_ref, low_ref, fac_ref, out_ref, *rest, level, tile, band, own_tiles, slot_count,
                 par_prow, low_prow, halves):
    count = out_ref.shape[0]
    split = tile // band
    r = info_ref[0]
    col = info_ref[1 + count * slot_count + count]
    own = lax.rem(r, own_tiles)

    def p_tile(ref, prow, node, q, m):
        if prow == tile:
            return ref[q, m, node, 0:tile, :]
        parts = tile // prow
        return jnp.concatenate([ref[q + j * own_tiles, m, node, 0:prow, :] for j in range(parts)], axis=0)

    def d_tile(ref, prow, node, a, m):
        return jnp.concatenate([ref[a * split + h, m, node, prow:prow + band, :] for h in range(split)], axis=0)

    for i in range(count):
        base = 1 + i * slot_count
        parent = info_ref[1 + count * slot_count + i]
        factor = [fac_ref[i, k * tile:(k + 1) * tile, :] for k in range(slot_count)]
        picks = [jnp.clip(info_ref[base + k], 0, slot_count - 1) for k in range(slot_count)]
        source = info_ref[base + jnp.maximum(r, own_tiles)]

        upper = dot_hi(d_tile(par_ref, par_prow, parent, own, 0), factor[0])
        for k in range(1, own_tiles):
            upper += dot_hi(d_tile(par_ref, par_prow, parent, own, k), factor[k])
        for k in range(own_tiles, slot_count):
            pick = picks[k] if par_prow == tile else jnp.minimum(picks[k], own_tiles - 1)
            upper -= dot_t_hi(p_tile(par_ref, par_prow, parent, pick, own), factor[k])

        if halves:
            half_ref = rest[0]
            rows = tile // halves
            which = r // own_tiles
            half = upper[0:rows]
            for j in range(1, halves):
                half = jnp.where(which == j, upper[j * rows:(j + 1) * rows], half)
            half_ref[i] = half

        @pl.when(r < own_tiles)
        def _():
            out_ref[i] = upper

        @pl.when(jnp.logical_and(r >= own_tiles, source >= 0))
        def _():
            if level == 1:
                s = jnp.clip(source, 0, slot_count - 1)
                acc = low_ref[i, pl.ds(pl.multiple_of(s * tile, tile), tile), :]
                for k in range(own_tiles):
                    acc -= dot_hi(p_tile(par_ref, par_prow, parent, s, k), factor[k])
            else:
                s = jnp.clip(source, 0, own_tiles - 1)
                acc = -dot_hi(p_tile(par_ref, par_prow, parent, s, 0), factor[0])
                for k in range(1, own_tiles):
                    acc -= dot_hi(p_tile(par_ref, par_prow, parent, s, k), factor[k])
                for k in range(own_tiles, slot_count):
                    q = jnp.minimum(picks[k], own_tiles - 1)
                    acc += dot_hi(d_tile(low_ref, low_prow, 0, s, q), factor[k])
            out_ref[i] = acc

        @pl.when(jnp.logical_and(r >= own_tiles, source < 0))
        def _():
            out_ref[i] = jnp.zeros((tile, tile), jnp.float32)


def level_products(info, parent_data, low_data, factors, level, tile, band, own_tiles, slot_count,
                   par_prow, low_prow, halves):
    kernel = functools.partial(
        level_kernel, level=level, tile=tile, band=band, own_tiles=own_tiles, slot_count=slot_count,
        par_prow=par_prow, low_prow=low_prow, halves=halves,
    )
    vmem = pl.BlockSpec(memory_space=pltpu.VMEM)
    count = factors.shape[0]
    shapes = [jax.ShapeDtypeStruct((count, tile, tile), jnp.float32)]
    if halves:
        shapes.append(jax.ShapeDtypeStruct((count, tile // halves, tile), jnp.float32))
    return pl.pallas_call(
        kernel,
        out_shape=tuple(shapes),
        in_specs=[pl.BlockSpec(memory_space=pltpu.SMEM), vmem, vmem, vmem],
        out_specs=tuple([vmem] * len(shapes)),
    )(info, parent_data, low_data, factors)


def reduce_kernel(x_ref, out_ref, recv_ref, send_sem, recv_sem, back_send, back_recv, *, axis, count, band, gather):
    me = lax.axis_index(axis)
    ids = {name: lax.axis_index(name) for name in ("leaf", "row", "col")}

    def device(peer):
        where = dict(ids)
        where[axis] = peer
        return (where["leaf"], where["row"], where["col"])

    mesh_ids = pl.DeviceIdType.MESH
    barrier = pltpu.get_barrier_semaphore()
    for d in range(1, count):
        pl.semaphore_signal(barrier, inc=1, device_id=device(lax.rem(me + d, count)), device_id_type=mesh_ids)
    pl.semaphore_wait(barrier, count - 1)

    sends = []
    for d in range(1, count):
        peer = lax.rem(me + d, count)
        copy = pltpu.make_async_remote_copy(
            src_ref=x_ref.at[:, pl.ds(pl.multiple_of(peer * band, band), band), :],
            dst_ref=recv_ref.at[d - 1],
            send_sem=send_sem.at[d - 1],
            recv_sem=recv_sem.at[d - 1],
            device_id=device(peer),
            device_id_type=mesh_ids,
        )
        copy.start()
        sends.append(copy)
    for copy in sends:
        copy.wait_recv()
    for copy in sends:
        copy.wait_send()
    own = pl.ds(pl.multiple_of(me * band, band), band)
    total = x_ref[:, own, :]
    for d in range(1, count):
        total = total + recv_ref[d - 1]
    if not gather:
        out_ref[...] = total
        return
    out_ref[:, own, :] = total
    backs = []
    for d in range(1, count):
        peer = lax.rem(me + d, count)
        copy = pltpu.make_async_remote_copy(
            src_ref=out_ref.at[:, own, :],
            dst_ref=out_ref.at[:, own, :],
            send_sem=back_send.at[d - 1],
            recv_sem=back_recv.at[d - 1],
            device_id=device(peer),
            device_id_type=mesh_ids,
        )
        copy.start()
        backs.append(copy)
    for d in range(1, count):
        source = lax.rem(me + count - d, count)
        part = pl.ds(pl.multiple_of(source * band, band), band)
        pltpu.make_async_remote_copy(
            src_ref=out_ref.at[:, part, :],
            dst_ref=out_ref.at[:, part, :],
            send_sem=back_send.at[d - 1],
            recv_sem=back_recv.at[d - 1],
            device_id=device(source),
            device_id_type=mesh_ids,
        ).wait_recv()
    for copy in backs:
        copy.wait_send()


def axis_reduce(x, axis, count, gather, collective_id):
    lead, rows, last = x.shape
    band = rows // count
    kernel = functools.partial(reduce_kernel, axis=axis, count=count, band=band, gather=gather)
    out_rows = rows if gather else band
    vmem = pl.BlockSpec(memory_space=pltpu.VMEM)
    return pl.pallas_call(
        kernel,
        out_shape=jax.ShapeDtypeStruct((lead, out_rows, last), x.dtype),
        in_specs=[vmem],
        out_specs=vmem,
        scratch_shapes=[
            pltpu.VMEM((count - 1, lead, band, last), x.dtype),
            pltpu.SemaphoreType.DMA((count - 1,)),
            pltpu.SemaphoreType.DMA((count - 1,)),
            pltpu.SemaphoreType.DMA((count - 1,)),
            pltpu.SemaphoreType.DMA((count - 1,)),
        ],
        compiler_params=pltpu.CompilerParams(collective_id=collective_id, has_side_effects=True),
    )(x)


def gather_kernel(x_ref, out_ref, send_sem, recv_sem, *, axis, count, band):
    me = lax.axis_index(axis)
    ids = {name: lax.axis_index(name) for name in ("leaf", "row", "col")}

    def device(peer):
        where = dict(ids)
        where[axis] = peer
        return (where["leaf"], where["row"], where["col"])

    mesh_ids = pl.DeviceIdType.MESH
    barrier = pltpu.get_barrier_semaphore()
    for d in range(1, count):
        pl.semaphore_signal(barrier, inc=1, device_id=device(lax.rem(me + d, count)), device_id_type=mesh_ids)
    pl.semaphore_wait(barrier, count - 1)
    own = pl.ds(pl.multiple_of(me * band, band), band)
    sends = []
    for d in range(1, count):
        peer = lax.rem(me + d, count)
        copy = pltpu.make_async_remote_copy(
            src_ref=x_ref,
            dst_ref=out_ref.at[:, own, :],
            send_sem=send_sem.at[d - 1],
            recv_sem=recv_sem.at[d - 1],
            device_id=device(peer),
            device_id_type=mesh_ids,
        )
        copy.start()
        sends.append(copy)
    out_ref[:, own, :] = x_ref[...]
    for d in range(1, count):
        source = lax.rem(me + count - d, count)
        part = pl.ds(pl.multiple_of(source * band, band), band)
        pltpu.make_async_remote_copy(
            src_ref=x_ref,
            dst_ref=out_ref.at[:, part, :],
            send_sem=send_sem.at[d - 1],
            recv_sem=recv_sem.at[d - 1],
            device_id=device(source),
            device_id_type=mesh_ids,
        ).wait_recv()
    for copy in sends:
        copy.wait_send()


def axis_gather(x, axis, count, collective_id):
    lead, band, last = x.shape
    vmem = pl.BlockSpec(memory_space=pltpu.VMEM)
    return pl.pallas_call(
        functools.partial(gather_kernel, axis=axis, count=count, band=band),
        out_shape=jax.ShapeDtypeStruct((lead, band * count, last), x.dtype),
        in_specs=[vmem],
        out_specs=vmem,
        scratch_shapes=[pltpu.SemaphoreType.DMA((count - 1,)), pltpu.SemaphoreType.DMA((count - 1,))],
        compiler_params=pltpu.CompilerParams(collective_id=collective_id, has_side_effects=True),
    )(x)


def body(sigma_top, panels, inverse_diag, slot_lists, parent_links):
    tile = TILE
    row_count = lax.axis_size("row")
    col_count = lax.axis_size("col")
    leaf_count = lax.axis_size("leaf")
    r = lax.axis_index("row")
    c = lax.axis_index("col")
    panel = panels[0]
    inverse = inverse_diag[0]
    picks_all = slot_lists[0]
    parents = parent_links[0]
    nodes = panel.shape[0]
    width = inverse.shape[2]
    own_tiles = width // tile
    slot_count = picks_all.shape[1]
    positions = slot_count + own_tiles
    band = width // row_count

    partial_factor = mm(panel, inverse)
    factor_rows = axis_reduce(partial_factor, "col", col_count, True, 3)
    living = jnp.concatenate([jnp.ones((1, slot_count), jnp.bool_), picks_all >= 0], axis=0)
    live_here = jnp.take(living, r, axis=1).astype(jnp.float32)
    factor_rows = factor_rows * live_here[:, None, None]
    factor_tile = lax.dynamic_slice_in_dim(factor_rows, c * tile, tile, 2)
    factor_cols = jnp.concatenate(
        [
            lax.all_gather(factor_tile[0:1], "row", axis=1, tiled=True),
            lax.all_gather(factor_tile[1:], "row", axis=1, tiled=True),
        ],
        axis=0,
    )

    inverse_band = lax.dynamic_slice_in_dim(inverse, r * band, band, 2)
    partial_gram = mm(jnp.transpose(inverse_band, (0, 2, 1)), inverse)
    gram_piece = lax.psum_scatter(partial_gram, "col", scatter_dimension=2, tiled=True)

    leaf = lax.axis_index("leaf")
    local_rows = sigma_top.shape[0]
    chunk_rows = lax.all_gather(sigma_top, "col", axis=1, tiled=True)
    chunks_per_tile = tile // local_rows
    rounds = []
    for t in range(chunks_per_tile):
        pairs = []
        for src_leaf in range(leaf_count):
            for src_row in range(row_count):
                q = src_leaf * row_count + src_row
                dst_leaf = (q % chunks_per_tile + t) % leaf_count
                dst_row = q // chunks_per_tile
                for col in range(col_count):
                    pairs.append(
                        ((src_leaf * row_count + src_row) * col_count + col,
                         (dst_leaf * row_count + dst_row) * col_count + col)
                    )
        rounds.append(lax.ppermute(chunk_rows, ("leaf", "row", "col"), pairs))
    order = lax.rem(leaf - jnp.arange(chunks_per_tile, dtype=jnp.int32) + 4 * leaf_count, leaf_count)
    sigma_rows = jnp.take(jnp.stack(rounds), order, axis=0).reshape(tile, -1)

    def diag_partial(first, products):
        rows = factor_rows[first:first + products.shape[0]]
        return mm(jnp.transpose(rows, (0, 2, 1)), products)

    def reduce_and_gather(first, products, sent, extra, tied=None):
        count = products.shape[0]
        piece = axis_reduce(diag_partial(first, products), "row", row_count, False, first)
        piece = piece + gram_piece[first:first + count]
        if tied is not None:
            piece, tied = lax.optimization_barrier((piece, tied))
            tied_out.append(tied)
        both = jnp.concatenate([sent, piece] + extra, axis=1)
        everything = lax.all_gather(both, ("row", "col"), axis=0)
        return everything.reshape(row_count, col_count, count, both.shape[1], tile)

    bands_per_tile = tile // band

    def product_col_t(gathered, node, m):
        tiles = lax.dynamic_index_in_dim(gathered[:, :, :, :tile], m, 1, keepdims=False)
        tiles = lax.dynamic_index_in_dim(tiles, node, 1, keepdims=False)
        return jnp.transpose(tiles, (2, 0, 1)).reshape(tile, -1)

    def product_row(gathered, node, q):
        tiles = lax.dynamic_index_in_dim(gathered[:, :, :, :tile], q, 0, keepdims=False)
        tiles = lax.dynamic_index_in_dim(tiles, node, 1, keepdims=False)
        return jnp.transpose(tiles, (1, 0, 2)).reshape(tile, -1)

    def diag_row(gathered, node, m):
        pieces = lax.dynamic_slice_in_dim(gathered[:, :, :, tile:], m * bands_per_tile, bands_per_tile, 0)
        pieces = lax.dynamic_index_in_dim(pieces, node, 2, keepdims=False)
        return jnp.transpose(pieces, (0, 2, 1, 3)).reshape(tile, -1)

    def diag_col(gathered, m, offset):
        pieces = lax.dynamic_index_in_dim(gathered[:, :, :, offset:offset + band], m, 1, keepdims=False)
        return jnp.transpose(pieces, (1, 0, 2, 3)).reshape(pieces.shape[1], -1, tile)

    own_row = jnp.minimum(r, own_tiles - 1)
    upper = r < own_tiles

    product_0 = mm(sigma_rows, factor_cols[0])
    lifted = [
        mm(sigma_rows, scatter_factor(factor_cols[node], picks_all[node - 1], slot_count, tile))[None]
        for node in (1, 2)
    ]
    tied_out = []
    gathered_0 = reduce_and_gather(0, product_0[None], product_0[None], [], jnp.concatenate(lifted, axis=0))
    lifted_cols = axis_gather(tied_out[0], "row", row_count, 4)

    info_1 = jnp.concatenate(
        [r.astype(jnp.int32)[None], picks_all[0:2].reshape(-1), jnp.zeros((2,), jnp.int32), c.astype(jnp.int32)[None]]
    )
    halves = row_count // own_tiles
    product_1, upper_half = level_products(
        info_1, gathered_0, lifted_cols, factor_cols[1:3], 1, tile, band, own_tiles, slot_count,
        tile, tile, halves,
    )
    gathered_1 = reduce_and_gather(1, product_1, upper_half, [])

    info_2 = jnp.concatenate(
        [r.astype(jnp.int32)[None], picks_all[2:nodes - 1].reshape(-1), (parents - 1).astype(jnp.int32),
         c.astype(jnp.int32)[None]]
    )
    (product_2,) = level_products(
        info_2, gathered_1, gathered_0, factor_cols[3:nodes], 2, tile, band, own_tiles, slot_count,
        tile // halves, tile, 0,
    )
    first_2 = 3
    count_2 = product_2.shape[0]
    gram_rows = jnp.zeros((count_2, width, tile), jnp.float32)
    gram_rows = lax.dynamic_update_slice_in_dim(gram_rows, gram_piece[first_2:first_2 + count_2], r * band, 1)
    diag_2 = axis_reduce(diag_partial(first_2, product_2) + gram_rows, "row", row_count, True, 2)

    products = jnp.concatenate([product_0[None], product_1, product_2], axis=0)
    diag_cols = jnp.concatenate(
        [diag_col(gathered_0, c, tile), diag_col(gathered_1, c, tile // halves), diag_2], axis=0
    )
    return (-products)[None], diag_cols[None]


def solution(mesh):
    return jax.shard_map(
        body,
        mesh=mesh,
        in_specs=(
            P(("leaf", "row"), "col"),
            P("leaf", None, "row", "col"),
            P("leaf", None, "col", None),
            P("leaf", None, None),
            P("leaf", None),
        ),
        out_specs=(P("leaf", None, "row", "col"), P("leaf", None, None, "col")),
        check_vma=False,
    )
```

```python
import functools

import jax
import jax.numpy as jnp
from jax import lax
from jax.experimental import pallas as pl
from jax.experimental.pallas import tpu as pltpu
from jax.sharding import PartitionSpec as P

TILE = 128
HIGHEST = lax.Precision.HIGHEST


def mm(a, b):
    return jnp.matmul(a, b, precision=HIGHEST, preferred_element_type=jnp.float32)


def tile_rows(matrix, index, tile):
    return lax.dynamic_slice_in_dim(matrix, index * tile, tile, 0)


def tile_cols(matrix, index, tile):
    return lax.dynamic_slice_in_dim(matrix, index * tile, tile, 1)


def scatter_factor(factor_col, slots, positions, tile):
    tiles = factor_col.reshape(slots.shape[0], tile, factor_col.shape[1])
    hits = slots[:, None] == jnp.arange(positions, dtype=slots.dtype)[None, :]
    present = jnp.any(hits, axis=0)
    source = jnp.argmax(hits, axis=0)
    moved = jnp.take(tiles, source, axis=0)
    moved = jnp.where(present[:, None, None], moved, 0.0)
    return moved.reshape(positions * tile, factor_col.shape[1])


def dot_hi(a, b):
    return jnp.dot(a, b, precision=HIGHEST, preferred_element_type=jnp.float32)


def dot_t_hi(a, b):
    return lax.dot_general(
        a, b, (((0,), (0,)), ((), ())), precision=HIGHEST, preferred_element_type=jnp.float32
    )


def level_kernel(info_ref, par_ref, low_ref, fac_ref, out_ref, *rest, level, tile, band, own_tiles, slot_count,
                 par_prow, low_prow, halves):
    count = out_ref.shape[0]
    split = tile // band
    r = info_ref[0]
    col = info_ref[1 + count * slot_count + count]
    own = lax.rem(r, own_tiles)

    def p_tile(ref, prow, node, q, m):
        if prow == tile:
            return ref[q, m, node, 0:tile, :]
        parts = tile // prow
        return jnp.concatenate([ref[q + j * own_tiles, m, node, 0:prow, :] for j in range(parts)], axis=0)

    def d_tile(ref, prow, node, a, m):
        return jnp.concatenate([ref[a * split + h, m, node, prow:prow + band, :] for h in range(split)], axis=0)

    for i in range(count):
        base = 1 + i * slot_count
        parent = info_ref[1 + count * slot_count + i]
        factor = [fac_ref[i, k * tile:(k + 1) * tile, :] for k in range(slot_count)]
        picks = [jnp.clip(info_ref[base + k], 0, slot_count - 1) for k in range(slot_count)]
        source = info_ref[base + jnp.maximum(r, own_tiles)]

        upper = dot_hi(d_tile(par_ref, par_prow, parent, own, 0), factor[0])
        for k in range(1, own_tiles):
            upper += dot_hi(d_tile(par_ref, par_prow, parent, own, k), factor[k])
        for k in range(own_tiles, slot_count):
            pick = picks[k] if par_prow == tile else jnp.minimum(picks[k], own_tiles - 1)
            upper -= dot_t_hi(p_tile(par_ref, par_prow, parent, pick, own), factor[k])

        if halves:
            half_ref = rest[0]
            rows = tile // halves
            which = r // own_tiles
            half = upper[0:rows]
            for j in range(1, halves):
                half = jnp.where(which == j, upper[j * rows:(j + 1) * rows], half)
            half_ref[i] = half

        @pl.when(r < own_tiles)
        def _():
            out_ref[i] = upper

        @pl.when(jnp.logical_and(r >= own_tiles, source >= 0))
        def _():
            if level == 1:
                s = jnp.clip(source, 0, slot_count - 1)
                acc = low_ref[i, pl.ds(pl.multiple_of(s * tile, tile), tile), :]
                for k in range(own_tiles):
                    acc -= dot_hi(p_tile(par_ref, par_prow, parent, s, k), factor[k])
            else:
                s = jnp.clip(source, 0, own_tiles - 1)
                acc = -dot_hi(p_tile(par_ref, par_prow, parent, s, 0), factor[0])
                for k in range(1, own_tiles):
                    acc -= dot_hi(p_tile(par_ref, par_prow, parent, s, k), factor[k])
                for k in range(own_tiles, slot_count):
                    q = jnp.minimum(picks[k], own_tiles - 1)
                    acc += dot_hi(d_tile(low_ref, low_prow, 0, s, q), factor[k])
            out_ref[i] = acc

        @pl.when(jnp.logical_and(r >= own_tiles, source < 0))
        def _():
            out_ref[i] = jnp.zeros((tile, tile), jnp.float32)


def level_products(info, parent_data, low_data, factors, level, tile, band, own_tiles, slot_count,
                   par_prow, low_prow, halves):
    kernel = functools.partial(
        level_kernel, level=level, tile=tile, band=band, own_tiles=own_tiles, slot_count=slot_count,
        par_prow=par_prow, low_prow=low_prow, halves=halves,
    )
    vmem = pl.BlockSpec(memory_space=pltpu.VMEM)
    count = factors.shape[0]
    shapes = [jax.ShapeDtypeStruct((count, tile, tile), jnp.float32)]
    if halves:
        shapes.append(jax.ShapeDtypeStruct((count, tile // halves, tile), jnp.float32))
    return pl.pallas_call(
        kernel,
        out_shape=tuple(shapes),
        in_specs=[pl.BlockSpec(memory_space=pltpu.SMEM), vmem, vmem, vmem],
        out_specs=tuple([vmem] * len(shapes)),
    )(info, parent_data, low_data, factors)


def reduce_kernel(x_ref, out_ref, recv_ref, send_sem, recv_sem, back_send, back_recv, *, axis, count, band, gather):
    me = lax.axis_index(axis)
    ids = {name: lax.axis_index(name) for name in ("leaf", "row", "col")}

    def device(peer):
        where = dict(ids)
        where[axis] = peer
        return (where["leaf"], where["row"], where["col"])

    mesh_ids = pl.DeviceIdType.MESH
    barrier = pltpu.get_barrier_semaphore()
    for d in range(1, count):
        pl.semaphore_signal(barrier, inc=1, device_id=device(lax.rem(me + d, count)), device_id_type=mesh_ids)
    pl.semaphore_wait(barrier, count - 1)

    sends = []
    for d in range(1, count):
        peer = lax.rem(me + d, count)
        copy = pltpu.make_async_remote_copy(
            src_ref=x_ref.at[:, pl.ds(pl.multiple_of(peer * band, band), band), :],
            dst_ref=recv_ref.at[d - 1],
            send_sem=send_sem.at[d - 1],
            recv_sem=recv_sem.at[d - 1],
            device_id=device(peer),
            device_id_type=mesh_ids,
        )
        copy.start()
        sends.append(copy)
    for copy in sends:
        copy.wait_recv()
    for copy in sends:
        copy.wait_send()
    own = pl.ds(pl.multiple_of(me * band, band), band)
    total = x_ref[:, own, :]
    for d in range(1, count):
        total = total + recv_ref[d - 1]
    if not gather:
        out_ref[...] = total
        return
    out_ref[:, own, :] = total
    backs = []
    for d in range(1, count):
        peer = lax.rem(me + d, count)
        copy = pltpu.make_async_remote_copy(
            src_ref=out_ref.at[:, own, :],
            dst_ref=out_ref.at[:, own, :],
            send_sem=back_send.at[d - 1],
            recv_sem=back_recv.at[d - 1],
            device_id=device(peer),
            device_id_type=mesh_ids,
        )
        copy.start()
        backs.append(copy)
    for d in range(1, count):
        source = lax.rem(me + count - d, count)
        part = pl.ds(pl.multiple_of(source * band, band), band)
        pltpu.make_async_remote_copy(
            src_ref=out_ref.at[:, part, :],
            dst_ref=out_ref.at[:, part, :],
            send_sem=back_send.at[d - 1],
            recv_sem=back_recv.at[d - 1],
            device_id=device(source),
            device_id_type=mesh_ids,
        ).wait_recv()
    for copy in backs:
        copy.wait_send()


def axis_reduce(x, axis, count, gather, collective_id):
    lead, rows, last = x.shape
    band = rows // count
    kernel = functools.partial(reduce_kernel, axis=axis, count=count, band=band, gather=gather)
    out_rows = rows if gather else band
    vmem = pl.BlockSpec(memory_space=pltpu.VMEM)
    return pl.pallas_call(
        kernel,
        out_shape=jax.ShapeDtypeStruct((lead, out_rows, last), x.dtype),
        in_specs=[vmem],
        out_specs=vmem,
        scratch_shapes=[
            pltpu.VMEM((count - 1, lead, band, last), x.dtype),
            pltpu.SemaphoreType.DMA((count - 1,)),
            pltpu.SemaphoreType.DMA((count - 1,)),
            pltpu.SemaphoreType.DMA((count - 1,)),
            pltpu.SemaphoreType.DMA((count - 1,)),
        ],
        compiler_params=pltpu.CompilerParams(collective_id=collective_id, has_side_effects=True),
    )(x)


def gather_kernel(x_ref, out_ref, send_sem, recv_sem, *, axis, count, band):
    me = lax.axis_index(axis)
    ids = {name: lax.axis_index(name) for name in ("leaf", "row", "col")}

    def device(peer):
        where = dict(ids)
        where[axis] = peer
        return (where["leaf"], where["row"], where["col"])

    mesh_ids = pl.DeviceIdType.MESH
    barrier = pltpu.get_barrier_semaphore()
    for d in range(1, count):
        pl.semaphore_signal(barrier, inc=1, device_id=device(lax.rem(me + d, count)), device_id_type=mesh_ids)
    pl.semaphore_wait(barrier, count - 1)
    own = pl.ds(pl.multiple_of(me * band, band), band)
    sends = []
    for d in range(1, count):
        peer = lax.rem(me + d, count)
        copy = pltpu.make_async_remote_copy(
            src_ref=x_ref,
            dst_ref=out_ref.at[:, own, :],
            send_sem=send_sem.at[d - 1],
            recv_sem=recv_sem.at[d - 1],
            device_id=device(peer),
            device_id_type=mesh_ids,
        )
        copy.start()
        sends.append(copy)
    out_ref[:, own, :] = x_ref[...]
    for d in range(1, count):
        source = lax.rem(me + count - d, count)
        part = pl.ds(pl.multiple_of(source * band, band), band)
        pltpu.make_async_remote_copy(
            src_ref=x_ref,
            dst_ref=out_ref.at[:, part, :],
            send_sem=send_sem.at[d - 1],
            recv_sem=recv_sem.at[d - 1],
            device_id=device(source),
            device_id_type=mesh_ids,
        ).wait_recv()
    for copy in sends:
        copy.wait_send()


def axis_gather(x, axis, count, collective_id):
    lead, band, last = x.shape
    vmem = pl.BlockSpec(memory_space=pltpu.VMEM)
    return pl.pallas_call(
        functools.partial(gather_kernel, axis=axis, count=count, band=band),
        out_shape=jax.ShapeDtypeStruct((lead, band * count, last), x.dtype),
        in_specs=[vmem],
        out_specs=vmem,
        scratch_shapes=[pltpu.SemaphoreType.DMA((count - 1,)), pltpu.SemaphoreType.DMA((count - 1,))],
        compiler_params=pltpu.CompilerParams(collective_id=collective_id, has_side_effects=True),
    )(x)


def pair_reduce_kernel(x_ref, out_ref, recv_a, recv_b, sems, *, band, chips):
    r = lax.axis_index("row")
    leaf = lax.axis_index("leaf")
    c = lax.axis_index("col")
    core = lax.rem(r, 2)
    chip = r // 2
    partner = r + 1 - 2 * core
    half = band * chips
    mesh_ids = pl.DeviceIdType.MESH
    peers = [2 * lax.rem(chip + d, chips) + core for d in range(1, chips)]

    barrier = pltpu.get_barrier_semaphore()
    for peer in [partner] + peers:
        pl.semaphore_signal(barrier, inc=1, device_id=(leaf, peer, c), device_id_type=mesh_ids)
    pl.semaphore_wait(barrier, chips)

    def rows(start, size):
        return pl.ds(pl.multiple_of(start, band), size)

    mine = rows(core * half, half)
    theirs = rows((1 - core) * half, half)
    copy = pltpu.make_async_remote_copy(
        src_ref=x_ref.at[:, theirs, :], dst_ref=recv_a, send_sem=sems.at[0, 0], recv_sem=sems.at[1, 0],
        device_id=(leaf, partner, c), device_id_type=mesh_ids,
    )
    copy.start()
    copy.wait_recv()
    copy.wait_send()
    recv_a[...] = recv_a[...] + x_ref[:, mine, :]

    sends = []
    for d in range(1, chips):
        target = lax.rem(chip + d, chips)
        copy = pltpu.make_async_remote_copy(
            src_ref=recv_a.at[:, rows(target * band, band), :], dst_ref=recv_b.at[d - 1],
            send_sem=sems.at[0, d], recv_sem=sems.at[1, d],
            device_id=(leaf, 2 * target + core, c), device_id_type=mesh_ids,
        )
        copy.start()
        sends.append(copy)
    for copy in sends:
        copy.wait_recv()
    for copy in sends:
        copy.wait_send()
    total = recv_a[:, rows(chip * band, band), :]
    for d in range(1, chips):
        total = total + recv_b[d - 1]
    own = rows(core * half + chip * band, band)
    out_ref[:, own, :] = total

    sends = []
    for d in range(1, chips):
        target = lax.rem(chip + d, chips)
        copy = pltpu.make_async_remote_copy(
            src_ref=out_ref.at[:, own, :], dst_ref=out_ref.at[:, own, :],
            send_sem=sems.at[2, d - 1], recv_sem=sems.at[3, d - 1],
            device_id=(leaf, 2 * target + core, c), device_id_type=mesh_ids,
        )
        copy.start()
        sends.append(copy)
    for d in range(1, chips):
        source = lax.rem(chip + chips - d, chips)
        part = rows(core * half + source * band, band)
        pltpu.make_async_remote_copy(
            src_ref=out_ref.at[:, part, :], dst_ref=out_ref.at[:, part, :],
            send_sem=sems.at[2, d - 1], recv_sem=sems.at[3, d - 1],
            device_id=(leaf, 2 * source + core, c), device_id_type=mesh_ids,
        ).wait_recv()
    for copy in sends:
        copy.wait_send()

    copy = pltpu.make_async_remote_copy(
        src_ref=out_ref.at[:, mine, :], dst_ref=out_ref.at[:, mine, :],
        send_sem=sems.at[2, chips - 1], recv_sem=sems.at[3, chips - 1],
        device_id=(leaf, partner, c), device_id_type=mesh_ids,
    )
    copy.start()
    pltpu.make_async_remote_copy(
        src_ref=out_ref.at[:, theirs, :], dst_ref=out_ref.at[:, theirs, :],
        send_sem=sems.at[2, chips - 1], recv_sem=sems.at[3, chips - 1],
        device_id=(leaf, partner, c), device_id_type=mesh_ids,
    ).wait_recv()
    copy.wait_send()


def pair_reduce(x, row_count, collective_id):
    lead, total_rows, last = x.shape
    chips = row_count // 2
    band = total_rows // row_count
    vmem = pl.BlockSpec(memory_space=pltpu.VMEM)
    return pl.pallas_call(
        functools.partial(pair_reduce_kernel, band=band, chips=chips),
        out_shape=jax.ShapeDtypeStruct(x.shape, x.dtype),
        in_specs=[vmem],
        out_specs=vmem,
        scratch_shapes=[
            pltpu.VMEM((lead, band * chips, last), x.dtype),
            pltpu.VMEM((chips - 1, lead, band, last), x.dtype),
            pltpu.SemaphoreType.DMA((4, chips)),
        ],
        compiler_params=pltpu.CompilerParams(collective_id=collective_id, has_side_effects=True),
    )(x)


def body(sigma_top, panels, inverse_diag, slot_lists, parent_links):
    tile = TILE
    row_count = lax.axis_size("row")
    col_count = lax.axis_size("col")
    leaf_count = lax.axis_size("leaf")
    r = lax.axis_index("row")
    c = lax.axis_index("col")
    panel = panels[0]
    inverse = inverse_diag[0]
    picks_all = slot_lists[0]
    parents = parent_links[0]
    nodes = panel.shape[0]
    width = inverse.shape[2]
    own_tiles = width // tile
    slot_count = picks_all.shape[1]
    positions = slot_count + own_tiles
    band = width // row_count

    partial_factor = mm(panel, inverse)
    factor_rows = axis_reduce(partial_factor, "col", col_count, True, 3)
    living = jnp.concatenate([jnp.ones((1, slot_count), jnp.bool_), picks_all >= 0], axis=0)
    live_here = jnp.take(living, r, axis=1).astype(jnp.float32)
    factor_rows = factor_rows * live_here[:, None, None]
    factor_tile = lax.dynamic_slice_in_dim(factor_rows, c * tile, tile, 2)
    factor_cols = lax.all_gather(factor_tile, "row", axis=1, tiled=True)

    inverse_band = lax.dynamic_slice_in_dim(inverse, r * band, band, 2)
    partial_gram = mm(jnp.transpose(inverse_band, (0, 2, 1)), inverse)
    gram_piece = lax.psum_scatter(partial_gram, "col", scatter_dimension=2, tiled=True)

    leaf = lax.axis_index("leaf")
    local_rows = sigma_top.shape[0]
    chunk_rows = lax.all_gather(sigma_top, "col", axis=1, tiled=True)
    chunks_per_tile = tile // local_rows
    rounds = []
    for t in range(chunks_per_tile):
        pairs = []
        for src_leaf in range(leaf_count):
            for src_row in range(row_count):
                q = src_leaf * row_count + src_row
                dst_leaf = (q % chunks_per_tile + t) % leaf_count
                dst_row = q // chunks_per_tile
                for col in range(col_count):
                    pairs.append(
                        ((src_leaf * row_count + src_row) * col_count + col,
                         (dst_leaf * row_count + dst_row) * col_count + col)
                    )
        rounds.append(lax.ppermute(chunk_rows, ("leaf", "row", "col"), pairs))
    order = lax.rem(leaf - jnp.arange(chunks_per_tile, dtype=jnp.int32) + 4 * leaf_count, leaf_count)
    sigma_rows = jnp.take(jnp.stack(rounds), order, axis=0).reshape(tile, -1)

    def diag_partial(first, products):
        rows = factor_rows[first:first + products.shape[0]]
        return mm(jnp.transpose(rows, (0, 2, 1)), products)

    def reduce_and_gather(first, products, sent, extra, tied=None):
        count = products.shape[0]
        piece = axis_reduce(diag_partial(first, products), "row", row_count, False, first)
        piece = piece + gram_piece[first:first + count]
        if tied is not None:
            piece, tied = lax.optimization_barrier((piece, tied))
            tied_out.append(tied)
        both = jnp.concatenate([sent, piece] + extra, axis=1)
        everything = lax.all_gather(both, ("row", "col"), axis=0)
        return everything.reshape(row_count, col_count, count, both.shape[1], tile)

    bands_per_tile = tile // band

    def product_col_t(gathered, node, m):
        tiles = lax.dynamic_index_in_dim(gathered[:, :, :, :tile], m, 1, keepdims=False)
        tiles = lax.dynamic_index_in_dim(tiles, node, 1, keepdims=False)
        return jnp.transpose(tiles, (2, 0, 1)).reshape(tile, -1)

    def product_row(gathered, node, q):
        tiles = lax.dynamic_index_in_dim(gathered[:, :, :, :tile], q, 0, keepdims=False)
        tiles = lax.dynamic_index_in_dim(tiles, node, 1, keepdims=False)
        return jnp.transpose(tiles, (1, 0, 2)).reshape(tile, -1)

    def diag_row(gathered, node, m):
        pieces = lax.dynamic_slice_in_dim(gathered[:, :, :, tile:], m * bands_per_tile, bands_per_tile, 0)
        pieces = lax.dynamic_index_in_dim(pieces, node, 2, keepdims=False)
        return jnp.transpose(pieces, (0, 2, 1, 3)).reshape(tile, -1)

    def diag_col(gathered, m, offset):
        pieces = lax.dynamic_index_in_dim(gathered[:, :, :, offset:offset + band], m, 1, keepdims=False)
        return jnp.transpose(pieces, (1, 0, 2, 3)).reshape(pieces.shape[1], -1, tile)

    own_row = jnp.minimum(r, own_tiles - 1)
    upper = r < own_tiles

    product_0 = mm(sigma_rows, factor_cols[0])
    lifted = [
        mm(sigma_rows, scatter_factor(factor_cols[node], picks_all[node - 1], slot_count, tile))[None]
        for node in (1, 2)
    ]
    tied_out = []
    gathered_0 = reduce_and_gather(0, product_0[None], product_0[None], [], jnp.concatenate(lifted, axis=0))
    lifted_cols = axis_gather(tied_out[0], "row", row_count, 4)

    info_1 = jnp.concatenate(
        [r.astype(jnp.int32)[None], picks_all[0:2].reshape(-1), jnp.zeros((2,), jnp.int32), c.astype(jnp.int32)[None]]
    )
    halves = row_count // own_tiles
    product_1, upper_half = level_products(
        info_1, gathered_0, lifted_cols, factor_cols[1:3], 1, tile, band, own_tiles, slot_count,
        tile, tile, halves,
    )
    gathered_1 = reduce_and_gather(1, product_1, upper_half, [])

    info_2 = jnp.concatenate(
        [r.astype(jnp.int32)[None], picks_all[2:nodes - 1].reshape(-1), (parents - 1).astype(jnp.int32),
         c.astype(jnp.int32)[None]]
    )
    (product_2,) = level_products(
        info_2, gathered_1, gathered_0, factor_cols[3:nodes], 2, tile, band, own_tiles, slot_count,
        tile // halves, tile, 0,
    )
    first_2 = 3
    count_2 = product_2.shape[0]
    gram_rows = jnp.zeros((count_2, width, tile), jnp.float32)
    gram_rows = lax.dynamic_update_slice_in_dim(gram_rows, gram_piece[first_2:first_2 + count_2], r * band, 1)
    diag_2 = pair_reduce(diag_partial(first_2, product_2) + gram_rows, row_count, 2)

    products = jnp.concatenate([product_0[None], product_1, product_2], axis=0)
    diag_cols = jnp.concatenate(
        [diag_col(gathered_0, c, tile), diag_col(gathered_1, c, tile // halves), diag_2], axis=0
    )
    return (-products)[None], diag_cols[None]


def solution(mesh):
    return jax.shard_map(
        body,
        mesh=mesh,
        in_specs=(
            P(("leaf", "row"), "col"),
            P("leaf", None, "row", "col"),
            P("leaf", None, "col", None),
            P("leaf", None, None),
            P("leaf", None),
        ),
        out_specs=(P("leaf", None, "row", "col"), P("leaf", None, None, "col")),
        check_vma=False,
    )
```

```python
import functools

import jax
import jax.numpy as jnp
from jax import lax
from jax.experimental import pallas as pl
from jax.experimental.pallas import tpu as pltpu
from jax.sharding import PartitionSpec as P

TILE = 128
HIGHEST = lax.Precision.HIGHEST


def mm(a, b):
    return jnp.matmul(a, b, precision=HIGHEST, preferred_element_type=jnp.float32)


def tile_rows(matrix, index, tile):
    return lax.dynamic_slice_in_dim(matrix, index * tile, tile, 0)


def tile_cols(matrix, index, tile):
    return lax.dynamic_slice_in_dim(matrix, index * tile, tile, 1)


def scatter_factor(factor_col, slots, positions, tile):
    tiles = factor_col.reshape(slots.shape[0], tile, factor_col.shape[1])
    hits = slots[:, None] == jnp.arange(positions, dtype=slots.dtype)[None, :]
    present = jnp.any(hits, axis=0)
    source = jnp.argmax(hits, axis=0)
    moved = jnp.take(tiles, source, axis=0)
    moved = jnp.where(present[:, None, None], moved, 0.0)
    return moved.reshape(positions * tile, factor_col.shape[1])


def dot_hi(a, b):
    return jnp.dot(a, b, precision=HIGHEST, preferred_element_type=jnp.float32)


def dot_t_hi(a, b):
    return lax.dot_general(
        a, b, (((0,), (0,)), ((), ())), precision=HIGHEST, preferred_element_type=jnp.float32
    )


def level_kernel(info_ref, par_ref, low_ref, fac_ref, out_ref, *rest, level, tile, band, own_tiles, slot_count,
                 par_prow, low_prow, halves):
    count = out_ref.shape[0]
    split = tile // band
    r = info_ref[0]
    col = info_ref[1 + count * slot_count + count]
    own = lax.rem(r, own_tiles)

    def p_tile(ref, prow, node, q, m):
        if prow == tile:
            return ref[q, m, node, 0:tile, :]
        parts = tile // prow
        return jnp.concatenate([ref[q + j * own_tiles, m, node, 0:prow, :] for j in range(parts)], axis=0)

    def d_tile(ref, prow, node, a, m):
        return jnp.concatenate([ref[a * split + h, m, node, prow:prow + band, :] for h in range(split)], axis=0)

    for i in range(count):
        base = 1 + i * slot_count
        parent = info_ref[1 + count * slot_count + i]
        factor = [fac_ref[i, k * tile:(k + 1) * tile, :] for k in range(slot_count)]
        picks = [jnp.clip(info_ref[base + k], 0, slot_count - 1) for k in range(slot_count)]
        source = info_ref[base + jnp.maximum(r, own_tiles)]

        upper = dot_hi(d_tile(par_ref, par_prow, parent, own, 0), factor[0])
        for k in range(1, own_tiles):
            upper += dot_hi(d_tile(par_ref, par_prow, parent, own, k), factor[k])
        for k in range(own_tiles, slot_count):
            pick = picks[k] if par_prow == tile else jnp.minimum(picks[k], own_tiles - 1)
            upper -= dot_t_hi(p_tile(par_ref, par_prow, parent, pick, own), factor[k])

        if halves:
            half_ref = rest[0]
            rows = tile // halves
            which = r // own_tiles
            half = upper[0:rows]
            for j in range(1, halves):
                half = jnp.where(which == j, upper[j * rows:(j + 1) * rows], half)
            half_ref[i] = half

        @pl.when(r < own_tiles)
        def _():
            out_ref[i] = upper

        @pl.when(jnp.logical_and(r >= own_tiles, source >= 0))
        def _():
            if level == 1:
                s = jnp.clip(source, 0, slot_count - 1)
                acc = low_ref[i, pl.ds(pl.multiple_of(s * tile, tile), tile), :]
                for k in range(own_tiles):
                    acc -= dot_hi(p_tile(par_ref, par_prow, parent, s, k), factor[k])
            else:
                s = jnp.clip(source, 0, own_tiles - 1)
                acc = -dot_hi(p_tile(par_ref, par_prow, parent, s, 0), factor[0])
                for k in range(1, own_tiles):
                    acc -= dot_hi(p_tile(par_ref, par_prow, parent, s, k), factor[k])
                for k in range(own_tiles, slot_count):
                    q = jnp.minimum(picks[k], own_tiles - 1)
                    acc += dot_hi(d_tile(low_ref, low_prow, 0, s, q), factor[k])
            out_ref[i] = acc

        @pl.when(jnp.logical_and(r >= own_tiles, source < 0))
        def _():
            out_ref[i] = jnp.zeros((tile, tile), jnp.float32)


def level_products(info, parent_data, low_data, factors, level, tile, band, own_tiles, slot_count,
                   par_prow, low_prow, halves):
    kernel = functools.partial(
        level_kernel, level=level, tile=tile, band=band, own_tiles=own_tiles, slot_count=slot_count,
        par_prow=par_prow, low_prow=low_prow, halves=halves,
    )
    vmem = pl.BlockSpec(memory_space=pltpu.VMEM)
    count = factors.shape[0]
    shapes = [jax.ShapeDtypeStruct((count, tile, tile), jnp.float32)]
    if halves:
        shapes.append(jax.ShapeDtypeStruct((count, tile // halves, tile), jnp.float32))
    return pl.pallas_call(
        kernel,
        out_shape=tuple(shapes),
        in_specs=[pl.BlockSpec(memory_space=pltpu.SMEM), vmem, vmem, vmem],
        out_specs=tuple([vmem] * len(shapes)),
    )(info, parent_data, low_data, factors)


def reduce_kernel(x_ref, out_ref, recv_ref, send_sem, recv_sem, back_send, back_recv, *, axis, count, band, gather):
    me = lax.axis_index(axis)
    ids = {name: lax.axis_index(name) for name in ("leaf", "row", "col")}

    def device(peer):
        where = dict(ids)
        where[axis] = peer
        return (where["leaf"], where["row"], where["col"])

    mesh_ids = pl.DeviceIdType.MESH
    barrier = pltpu.get_barrier_semaphore()
    for d in range(1, count):
        pl.semaphore_signal(barrier, inc=1, device_id=device(lax.rem(me + d, count)), device_id_type=mesh_ids)
    pl.semaphore_wait(barrier, count - 1)

    sends = []
    for d in range(1, count):
        peer = lax.rem(me + d, count)
        copy = pltpu.make_async_remote_copy(
            src_ref=x_ref.at[:, pl.ds(pl.multiple_of(peer * band, band), band), :],
            dst_ref=recv_ref.at[d - 1],
            send_sem=send_sem.at[d - 1],
            recv_sem=recv_sem.at[d - 1],
            device_id=device(peer),
            device_id_type=mesh_ids,
        )
        copy.start()
        sends.append(copy)
    for copy in sends:
        copy.wait_recv()
    for copy in sends:
        copy.wait_send()
    own = pl.ds(pl.multiple_of(me * band, band), band)
    total = x_ref[:, own, :]
    for d in range(1, count):
        total = total + recv_ref[d - 1]
    if not gather:
        out_ref[...] = total
        return
    out_ref[:, own, :] = total
    backs = []
    for d in range(1, count):
        peer = lax.rem(me + d, count)
        copy = pltpu.make_async_remote_copy(
            src_ref=out_ref.at[:, own, :],
            dst_ref=out_ref.at[:, own, :],
            send_sem=back_send.at[d - 1],
            recv_sem=back_recv.at[d - 1],
            device_id=device(peer),
            device_id_type=mesh_ids,
        )
        copy.start()
        backs.append(copy)
    for d in range(1, count):
        source = lax.rem(me + count - d, count)
        part = pl.ds(pl.multiple_of(source * band, band), band)
        pltpu.make_async_remote_copy(
            src_ref=out_ref.at[:, part, :],
            dst_ref=out_ref.at[:, part, :],
            send_sem=back_send.at[d - 1],
            recv_sem=back_recv.at[d - 1],
            device_id=device(source),
            device_id_type=mesh_ids,
        ).wait_recv()
    for copy in backs:
        copy.wait_send()


def axis_reduce(x, axis, count, gather, collective_id):
    lead, rows, last = x.shape
    band = rows // count
    kernel = functools.partial(reduce_kernel, axis=axis, count=count, band=band, gather=gather)
    out_rows = rows if gather else band
    vmem = pl.BlockSpec(memory_space=pltpu.VMEM)
    return pl.pallas_call(
        kernel,
        out_shape=jax.ShapeDtypeStruct((lead, out_rows, last), x.dtype),
        in_specs=[vmem],
        out_specs=vmem,
        scratch_shapes=[
            pltpu.VMEM((count - 1, lead, band, last), x.dtype),
            pltpu.SemaphoreType.DMA((count - 1,)),
            pltpu.SemaphoreType.DMA((count - 1,)),
            pltpu.SemaphoreType.DMA((count - 1,)),
            pltpu.SemaphoreType.DMA((count - 1,)),
        ],
        compiler_params=pltpu.CompilerParams(collective_id=collective_id, has_side_effects=True),
    )(x)


def gather_kernel(x_ref, out_ref, send_sem, recv_sem, *, axis, count, band):
    me = lax.axis_index(axis)
    ids = {name: lax.axis_index(name) for name in ("leaf", "row", "col")}

    def device(peer):
        where = dict(ids)
        where[axis] = peer
        return (where["leaf"], where["row"], where["col"])

    mesh_ids = pl.DeviceIdType.MESH
    barrier = pltpu.get_barrier_semaphore()
    for d in range(1, count):
        pl.semaphore_signal(barrier, inc=1, device_id=device(lax.rem(me + d, count)), device_id_type=mesh_ids)
    pl.semaphore_wait(barrier, count - 1)
    own = pl.ds(pl.multiple_of(me * band, band), band)
    sends = []
    for d in range(1, count):
        peer = lax.rem(me + d, count)
        copy = pltpu.make_async_remote_copy(
            src_ref=x_ref,
            dst_ref=out_ref.at[:, own, :],
            send_sem=send_sem.at[d - 1],
            recv_sem=recv_sem.at[d - 1],
            device_id=device(peer),
            device_id_type=mesh_ids,
        )
        copy.start()
        sends.append(copy)
    out_ref[:, own, :] = x_ref[...]
    for d in range(1, count):
        source = lax.rem(me + count - d, count)
        part = pl.ds(pl.multiple_of(source * band, band), band)
        pltpu.make_async_remote_copy(
            src_ref=x_ref,
            dst_ref=out_ref.at[:, part, :],
            send_sem=send_sem.at[d - 1],
            recv_sem=recv_sem.at[d - 1],
            device_id=device(source),
            device_id_type=mesh_ids,
        ).wait_recv()
    for copy in sends:
        copy.wait_send()


def axis_gather(x, axis, count, collective_id):
    lead, band, last = x.shape
    vmem = pl.BlockSpec(memory_space=pltpu.VMEM)
    return pl.pallas_call(
        functools.partial(gather_kernel, axis=axis, count=count, band=band),
        out_shape=jax.ShapeDtypeStruct((lead, band * count, last), x.dtype),
        in_specs=[vmem],
        out_specs=vmem,
        scratch_shapes=[pltpu.SemaphoreType.DMA((count - 1,)), pltpu.SemaphoreType.DMA((count - 1,))],
        compiler_params=pltpu.CompilerParams(collective_id=collective_id, has_side_effects=True),
    )(x)


def pair_reduce_kernel(x_ref, out_ref, recv_a, recv_b, sems, *, band, chips):
    r = lax.axis_index("row")
    leaf = lax.axis_index("leaf")
    c = lax.axis_index("col")
    core = lax.rem(r, 2)
    chip = r // 2
    partner = r + 1 - 2 * core
    half = band * chips
    mesh_ids = pl.DeviceIdType.MESH
    peers = [2 * lax.rem(chip + d, chips) + core for d in range(1, chips)]

    barrier = pltpu.get_barrier_semaphore()
    for peer in [partner] + peers:
        pl.semaphore_signal(barrier, inc=1, device_id=(leaf, peer, c), device_id_type=mesh_ids)
    pl.semaphore_wait(barrier, chips)

    def rows(start, size):
        return pl.ds(pl.multiple_of(start, band), size)

    mine = rows(core * half, half)
    theirs = rows((1 - core) * half, half)
    copy = pltpu.make_async_remote_copy(
        src_ref=x_ref.at[:, theirs, :], dst_ref=recv_a, send_sem=sems.at[0, 0], recv_sem=sems.at[1, 0],
        device_id=(leaf, partner, c), device_id_type=mesh_ids,
    )
    copy.start()
    copy.wait_recv()
    copy.wait_send()
    recv_a[...] = recv_a[...] + x_ref[:, mine, :]

    sends = []
    for d in range(1, chips):
        target = lax.rem(chip + d, chips)
        copy = pltpu.make_async_remote_copy(
            src_ref=recv_a.at[:, rows(target * band, band), :], dst_ref=recv_b.at[d - 1],
            send_sem=sems.at[0, d], recv_sem=sems.at[1, d],
            device_id=(leaf, 2 * target + core, c), device_id_type=mesh_ids,
        )
        copy.start()
        sends.append(copy)
    for copy in sends:
        copy.wait_recv()
    for copy in sends:
        copy.wait_send()
    total = recv_a[:, rows(chip * band, band), :]
    for d in range(1, chips):
        total = total + recv_b[d - 1]
    own = rows(core * half + chip * band, band)
    out_ref[:, own, :] = total

    sends = []
    for d in range(1, chips):
        target = lax.rem(chip + d, chips)
        copy = pltpu.make_async_remote_copy(
            src_ref=out_ref.at[:, own, :], dst_ref=out_ref.at[:, own, :],
            send_sem=sems.at[2, d - 1], recv_sem=sems.at[3, d - 1],
            device_id=(leaf, 2 * target + core, c), device_id_type=mesh_ids,
        )
        copy.start()
        sends.append(copy)
    for d in range(1, chips):
        source = lax.rem(chip + chips - d, chips)
        part = rows(core * half + source * band, band)
        pltpu.make_async_remote_copy(
            src_ref=out_ref.at[:, part, :], dst_ref=out_ref.at[:, part, :],
            send_sem=sems.at[2, d - 1], recv_sem=sems.at[3, d - 1],
            device_id=(leaf, 2 * source + core, c), device_id_type=mesh_ids,
        ).wait_recv()
    for copy in sends:
        copy.wait_send()

    copy = pltpu.make_async_remote_copy(
        src_ref=out_ref.at[:, mine, :], dst_ref=out_ref.at[:, mine, :],
        send_sem=sems.at[2, chips - 1], recv_sem=sems.at[3, chips - 1],
        device_id=(leaf, partner, c), device_id_type=mesh_ids,
    )
    copy.start()
    pltpu.make_async_remote_copy(
        src_ref=out_ref.at[:, theirs, :], dst_ref=out_ref.at[:, theirs, :],
        send_sem=sems.at[2, chips - 1], recv_sem=sems.at[3, chips - 1],
        device_id=(leaf, partner, c), device_id_type=mesh_ids,
    ).wait_recv()
    copy.wait_send()


def pair_reduce(x, row_count, collective_id):
    lead, total_rows, last = x.shape
    chips = row_count // 2
    band = total_rows // row_count
    vmem = pl.BlockSpec(memory_space=pltpu.VMEM)
    return pl.pallas_call(
        functools.partial(pair_reduce_kernel, band=band, chips=chips),
        out_shape=jax.ShapeDtypeStruct(x.shape, x.dtype),
        in_specs=[vmem],
        out_specs=vmem,
        scratch_shapes=[
            pltpu.VMEM((lead, band * chips, last), x.dtype),
            pltpu.VMEM((chips - 1, lead, band, last), x.dtype),
            pltpu.SemaphoreType.DMA((4, chips)),
        ],
        compiler_params=pltpu.CompilerParams(collective_id=collective_id, has_side_effects=True),
    )(x)


def pair_scatter_kernel(x_ref, out_ref, recv_a, recv_b, sems, *, chips):
    r = lax.axis_index("row")
    leaf = lax.axis_index("leaf")
    c = lax.axis_index("col")
    core = lax.rem(r, 2)
    chip = r // 2
    partner = r + 1 - 2 * core
    mesh_ids = pl.DeviceIdType.MESH
    peers = [2 * lax.rem(chip + d, chips) + core for d in range(1, chips)]

    barrier = pltpu.get_barrier_semaphore()
    for peer in [partner] + peers:
        pl.semaphore_signal(barrier, inc=1, device_id=(leaf, peer, c), device_id_type=mesh_ids)
    pl.semaphore_wait(barrier, chips)

    copy = pltpu.make_async_remote_copy(
        src_ref=x_ref.at[:, :, 1 - core], dst_ref=recv_a, send_sem=sems.at[0, 0], recv_sem=sems.at[1, 0],
        device_id=(leaf, partner, c), device_id_type=mesh_ids,
    )
    copy.start()
    copy.wait_recv()
    copy.wait_send()
    recv_a[...] = recv_a[...] + x_ref[:, :, core]

    sends = []
    for d in range(1, chips):
        target = lax.rem(chip + d, chips)
        copy = pltpu.make_async_remote_copy(
            src_ref=recv_a.at[:, target], dst_ref=recv_b.at[d - 1],
            send_sem=sems.at[0, d], recv_sem=sems.at[1, d],
            device_id=(leaf, 2 * target + core, c), device_id_type=mesh_ids,
        )
        copy.start()
        sends.append(copy)
    for copy in sends:
        copy.wait_recv()
    for copy in sends:
        copy.wait_send()
    total = recv_a[:, chip]
    for d in range(1, chips):
        total = total + recv_b[d - 1]
    out_ref[...] = total


def pair_scatter(x, row_count, collective_id):
    lead, total_rows, last = x.shape
    chips = row_count // 2
    band = total_rows // row_count
    vmem = pl.BlockSpec(memory_space=pltpu.VMEM)
    return pl.pallas_call(
        functools.partial(pair_scatter_kernel, chips=chips),
        out_shape=jax.ShapeDtypeStruct((lead, band, last), x.dtype),
        in_specs=[vmem],
        out_specs=vmem,
        scratch_shapes=[
            pltpu.VMEM((lead, chips, band, last), x.dtype),
            pltpu.VMEM((chips - 1, lead, band, last), x.dtype),
            pltpu.SemaphoreType.DMA((2, chips)),
        ],
        compiler_params=pltpu.CompilerParams(collective_id=collective_id, has_side_effects=True),
    )(x.reshape(lead, chips, 2, band, last))


def body(sigma_top, panels, inverse_diag, slot_lists, parent_links):
    tile = TILE
    row_count = lax.axis_size("row")
    col_count = lax.axis_size("col")
    leaf_count = lax.axis_size("leaf")
    r = lax.axis_index("row")
    c = lax.axis_index("col")
    panel = panels[0]
    inverse = inverse_diag[0]
    picks_all = slot_lists[0]
    parents = parent_links[0]
    nodes = panel.shape[0]
    width = inverse.shape[2]
    own_tiles = width // tile
    slot_count = picks_all.shape[1]
    positions = slot_count + own_tiles
    band = width // row_count

    partial_factor = mm(panel, inverse)
    factor_rows = axis_reduce(partial_factor, "col", col_count, True, 3)
    living = jnp.concatenate([jnp.ones((1, slot_count), jnp.bool_), picks_all >= 0], axis=0)
    live_here = jnp.take(living, r, axis=1).astype(jnp.float32)
    factor_rows = factor_rows * live_here[:, None, None]
    factor_tile = lax.dynamic_slice_in_dim(factor_rows, c * tile, tile, 2)
    factor_cols = lax.all_gather(factor_tile, "row", axis=1, tiled=True)

    inverse_band = lax.dynamic_slice_in_dim(inverse, r * band, band, 2)
    partial_gram = mm(jnp.transpose(inverse_band, (0, 2, 1)), inverse)
    gram_piece = lax.psum_scatter(partial_gram, "col", scatter_dimension=2, tiled=True)

    leaf = lax.axis_index("leaf")
    local_rows = sigma_top.shape[0]
    chunk_rows = lax.all_gather(sigma_top, "col", axis=1, tiled=True)
    chunks_per_tile = tile // local_rows
    rounds = []
    for t in range(chunks_per_tile):
        pairs = []
        for src_leaf in range(leaf_count):
            for src_row in range(row_count):
                q = src_leaf * row_count + src_row
                dst_leaf = (q % chunks_per_tile + t) % leaf_count
                dst_row = q // chunks_per_tile
                for col in range(col_count):
                    pairs.append(
                        ((src_leaf * row_count + src_row) * col_count + col,
                         (dst_leaf * row_count + dst_row) * col_count + col)
                    )
        rounds.append(lax.ppermute(chunk_rows, ("leaf", "row", "col"), pairs))
    order = lax.rem(leaf - jnp.arange(chunks_per_tile, dtype=jnp.int32) + 4 * leaf_count, leaf_count)
    sigma_rows = jnp.take(jnp.stack(rounds), order, axis=0).reshape(tile, -1)

    def diag_partial(first, products):
        rows = factor_rows[first:first + products.shape[0]]
        return mm(jnp.transpose(rows, (0, 2, 1)), products)

    def reduce_and_gather(first, products, sent, extra, tied=None):
        count = products.shape[0]
        piece = pair_scatter(diag_partial(first, products), row_count, first)
        piece = piece + gram_piece[first:first + count]
        if tied is not None:
            piece, tied = lax.optimization_barrier((piece, tied))
            tied_out.append(tied)
        both = jnp.concatenate([sent, piece] + extra, axis=1)
        everything = lax.all_gather(both, ("row", "col"), axis=0)
        return everything.reshape(row_count, col_count, count, both.shape[1], tile)

    bands_per_tile = tile // band

    def product_col_t(gathered, node, m):
        tiles = lax.dynamic_index_in_dim(gathered[:, :, :, :tile], m, 1, keepdims=False)
        tiles = lax.dynamic_index_in_dim(tiles, node, 1, keepdims=False)
        return jnp.transpose(tiles, (2, 0, 1)).reshape(tile, -1)

    def product_row(gathered, node, q):
        tiles = lax.dynamic_index_in_dim(gathered[:, :, :, :tile], q, 0, keepdims=False)
        tiles = lax.dynamic_index_in_dim(tiles, node, 1, keepdims=False)
        return jnp.transpose(tiles, (1, 0, 2)).reshape(tile, -1)

    def diag_row(gathered, node, m):
        pieces = lax.dynamic_slice_in_dim(gathered[:, :, :, tile:], m * bands_per_tile, bands_per_tile, 0)
        pieces = lax.dynamic_index_in_dim(pieces, node, 2, keepdims=False)
        return jnp.transpose(pieces, (0, 2, 1, 3)).reshape(tile, -1)

    def diag_col(gathered, m, offset):
        pieces = lax.dynamic_index_in_dim(gathered[:, :, :, offset:offset + band], m, 1, keepdims=False)
        return jnp.transpose(pieces, (1, 0, 2, 3)).reshape(pieces.shape[1], -1, tile)

    own_row = jnp.minimum(r, own_tiles - 1)
    upper = r < own_tiles

    product_0 = mm(sigma_rows, factor_cols[0])
    lifted = [
        mm(sigma_rows, scatter_factor(factor_cols[node], picks_all[node - 1], slot_count, tile))[None]
        for node in (1, 2)
    ]
    tied_out = []
    gathered_0 = reduce_and_gather(0, product_0[None], product_0[None], [], jnp.concatenate(lifted, axis=0))
    lifted_cols = axis_gather(tied_out[0], "row", row_count, 4)

    info_1 = jnp.concatenate(
        [r.astype(jnp.int32)[None], picks_all[0:2].reshape(-1), jnp.zeros((2,), jnp.int32), c.astype(jnp.int32)[None]]
    )
    halves = row_count // own_tiles
    product_1, upper_half = level_products(
        info_1, gathered_0, lifted_cols, factor_cols[1:3], 1, tile, band, own_tiles, slot_count,
        tile, tile, halves,
    )
    gathered_1 = reduce_and_gather(1, product_1, upper_half, [])

    info_2 = jnp.concatenate(
        [r.astype(jnp.int32)[None], picks_all[2:nodes - 1].reshape(-1), (parents - 1).astype(jnp.int32),
         c.astype(jnp.int32)[None]]
    )
    (product_2,) = level_products(
        info_2, gathered_1, gathered_0, factor_cols[3:nodes], 2, tile, band, own_tiles, slot_count,
        tile // halves, tile, 0,
    )
    first_2 = 3
    count_2 = product_2.shape[0]
    gram_rows = jnp.zeros((count_2, width, tile), jnp.float32)
    gram_rows = lax.dynamic_update_slice_in_dim(gram_rows, gram_piece[first_2:first_2 + count_2], r * band, 1)
    diag_2 = pair_reduce(diag_partial(first_2, product_2) + gram_rows, row_count, 2)

    products = jnp.concatenate([product_0[None], product_1, product_2], axis=0)
    diag_cols = jnp.concatenate(
        [diag_col(gathered_0, c, tile), diag_col(gathered_1, c, tile // halves), diag_2], axis=0
    )
    return (-products)[None], diag_cols[None]


def solution(mesh):
    return jax.shard_map(
        body,
        mesh=mesh,
        in_specs=(
            P(("leaf", "row"), "col"),
            P("leaf", None, "row", "col"),
            P("leaf", None, "col", None),
            P("leaf", None, None),
            P("leaf", None),
        ),
        out_specs=(P("leaf", None, "row", "col"), P("leaf", None, None, "col")),
        check_vma=False,
    )
```

```python
import functools

import jax
import jax.numpy as jnp
from jax import lax
from jax.experimental import pallas as pl
from jax.experimental.pallas import tpu as pltpu
from jax.sharding import PartitionSpec as P

TILE = 128
HIGHEST = lax.Precision.HIGHEST


def mm(a, b):
    return jnp.matmul(a, b, precision=HIGHEST, preferred_element_type=jnp.float32)


def tile_rows(matrix, index, tile):
    return lax.dynamic_slice_in_dim(matrix, index * tile, tile, 0)


def tile_cols(matrix, index, tile):
    return lax.dynamic_slice_in_dim(matrix, index * tile, tile, 1)


def scatter_factor(factor_col, slots, positions, tile):
    tiles = factor_col.reshape(slots.shape[0], tile, factor_col.shape[1])
    hits = slots[:, None] == jnp.arange(positions, dtype=slots.dtype)[None, :]
    present = jnp.any(hits, axis=0)
    source = jnp.argmax(hits, axis=0)
    moved = jnp.take(tiles, source, axis=0)
    moved = jnp.where(present[:, None, None], moved, 0.0)
    return moved.reshape(positions * tile, factor_col.shape[1])


def dot_hi(a, b):
    return jnp.dot(a, b, precision=HIGHEST, preferred_element_type=jnp.float32)


def dot_t_hi(a, b):
    return lax.dot_general(
        a, b, (((0,), (0,)), ((), ())), precision=HIGHEST, preferred_element_type=jnp.float32
    )


def level_kernel(info_ref, par_ref, low_ref, fac_ref, out_ref, *rest, level, tile, band, own_tiles, slot_count,
                 par_prow, low_prow, halves):
    count = out_ref.shape[0]
    split = tile // band
    r = info_ref[0]
    col = info_ref[1 + count * slot_count + count]
    own = lax.rem(r, own_tiles)

    def p_tile(ref, prow, node, q, m):
        if prow == tile:
            return ref[q, m, node, 0:tile, :]
        parts = tile // prow
        return jnp.concatenate([ref[q + j * own_tiles, m, node, 0:prow, :] for j in range(parts)], axis=0)

    def d_tile(ref, prow, node, a, m):
        return jnp.concatenate([ref[a * split + h, m, node, prow:prow + band, :] for h in range(split)], axis=0)

    for i in range(count):
        base = 1 + i * slot_count
        parent = info_ref[1 + count * slot_count + i]
        factor = [fac_ref[i, k * tile:(k + 1) * tile, :] for k in range(slot_count)]
        picks = [jnp.clip(info_ref[base + k], 0, slot_count - 1) for k in range(slot_count)]
        source = info_ref[base + jnp.maximum(r, own_tiles)]

        upper = dot_hi(d_tile(par_ref, par_prow, parent, own, 0), factor[0])
        for k in range(1, own_tiles):
            upper += dot_hi(d_tile(par_ref, par_prow, parent, own, k), factor[k])
        for k in range(own_tiles, slot_count):
            pick = picks[k] if par_prow == tile else jnp.minimum(picks[k], own_tiles - 1)
            upper -= dot_t_hi(p_tile(par_ref, par_prow, parent, pick, own), factor[k])

        if halves:
            half_ref = rest[0]
            rows = tile // halves
            which = r // own_tiles
            half = upper[0:rows]
            for j in range(1, halves):
                half = jnp.where(which == j, upper[j * rows:(j + 1) * rows], half)
            half_ref[i] = half

        @pl.when(r < own_tiles)
        def _():
            out_ref[i] = upper

        @pl.when(jnp.logical_and(r >= own_tiles, source >= 0))
        def _():
            if level == 1:
                s = jnp.clip(source, 0, slot_count - 1)
                acc = low_ref[i, pl.ds(pl.multiple_of(s * tile, tile), tile), :]
                for k in range(own_tiles):
                    acc -= dot_hi(p_tile(par_ref, par_prow, parent, s, k), factor[k])
            else:
                s = jnp.clip(source, 0, own_tiles - 1)
                acc = -dot_hi(p_tile(par_ref, par_prow, parent, s, 0), factor[0])
                for k in range(1, own_tiles):
                    acc -= dot_hi(p_tile(par_ref, par_prow, parent, s, k), factor[k])
                for k in range(own_tiles, slot_count):
                    q = jnp.minimum(picks[k], own_tiles - 1)
                    acc += dot_hi(d_tile(low_ref, low_prow, 0, s, q), factor[k])
            out_ref[i] = acc

        @pl.when(jnp.logical_and(r >= own_tiles, source < 0))
        def _():
            out_ref[i] = jnp.zeros((tile, tile), jnp.float32)


def level_products(info, parent_data, low_data, factors, level, tile, band, own_tiles, slot_count,
                   par_prow, low_prow, halves):
    kernel = functools.partial(
        level_kernel, level=level, tile=tile, band=band, own_tiles=own_tiles, slot_count=slot_count,
        par_prow=par_prow, low_prow=low_prow, halves=halves,
    )
    vmem = pl.BlockSpec(memory_space=pltpu.VMEM)
    count = factors.shape[0]
    shapes = [jax.ShapeDtypeStruct((count, tile, tile), jnp.float32)]
    if halves:
        shapes.append(jax.ShapeDtypeStruct((count, tile // halves, tile), jnp.float32))
    return pl.pallas_call(
        kernel,
        out_shape=tuple(shapes),
        in_specs=[pl.BlockSpec(memory_space=pltpu.SMEM), vmem, vmem, vmem],
        out_specs=tuple([vmem] * len(shapes)),
    )(info, parent_data, low_data, factors)


def reduce_kernel(x_ref, out_ref, recv_ref, send_sem, recv_sem, back_send, back_recv, *, axis, count, band, gather):
    me = lax.axis_index(axis)
    ids = {name: lax.axis_index(name) for name in ("leaf", "row", "col")}

    def device(peer):
        where = dict(ids)
        where[axis] = peer
        return (where["leaf"], where["row"], where["col"])

    mesh_ids = pl.DeviceIdType.MESH
    barrier = pltpu.get_barrier_semaphore()
    for d in range(1, count):
        pl.semaphore_signal(barrier, inc=1, device_id=device(lax.rem(me + d, count)), device_id_type=mesh_ids)
    pl.semaphore_wait(barrier, count - 1)

    sends = []
    for d in range(1, count):
        peer = lax.rem(me + d, count)
        copy = pltpu.make_async_remote_copy(
            src_ref=x_ref.at[:, pl.ds(pl.multiple_of(peer * band, band), band), :],
            dst_ref=recv_ref.at[d - 1],
            send_sem=send_sem.at[d - 1],
            recv_sem=recv_sem.at[d - 1],
            device_id=device(peer),
            device_id_type=mesh_ids,
        )
        copy.start()
        sends.append(copy)
    for copy in sends:
        copy.wait_recv()
    for copy in sends:
        copy.wait_send()
    own = pl.ds(pl.multiple_of(me * band, band), band)
    total = x_ref[:, own, :]
    for d in range(1, count):
        total = total + recv_ref[d - 1]
    if not gather:
        out_ref[...] = total
        return
    out_ref[:, own, :] = total
    backs = []
    for d in range(1, count):
        peer = lax.rem(me + d, count)
        copy = pltpu.make_async_remote_copy(
            src_ref=out_ref.at[:, own, :],
            dst_ref=out_ref.at[:, own, :],
            send_sem=back_send.at[d - 1],
            recv_sem=back_recv.at[d - 1],
            device_id=device(peer),
            device_id_type=mesh_ids,
        )
        copy.start()
        backs.append(copy)
    for d in range(1, count):
        source = lax.rem(me + count - d, count)
        part = pl.ds(pl.multiple_of(source * band, band), band)
        pltpu.make_async_remote_copy(
            src_ref=out_ref.at[:, part, :],
            dst_ref=out_ref.at[:, part, :],
            send_sem=back_send.at[d - 1],
            recv_sem=back_recv.at[d - 1],
            device_id=device(source),
            device_id_type=mesh_ids,
        ).wait_recv()
    for copy in backs:
        copy.wait_send()


def axis_reduce(x, axis, count, gather, collective_id):
    lead, rows, last = x.shape
    band = rows // count
    kernel = functools.partial(reduce_kernel, axis=axis, count=count, band=band, gather=gather)
    out_rows = rows if gather else band
    vmem = pl.BlockSpec(memory_space=pltpu.VMEM)
    return pl.pallas_call(
        kernel,
        out_shape=jax.ShapeDtypeStruct((lead, out_rows, last), x.dtype),
        in_specs=[vmem],
        out_specs=vmem,
        scratch_shapes=[
            pltpu.VMEM((count - 1, lead, band, last), x.dtype),
            pltpu.SemaphoreType.DMA((count - 1,)),
            pltpu.SemaphoreType.DMA((count - 1,)),
            pltpu.SemaphoreType.DMA((count - 1,)),
            pltpu.SemaphoreType.DMA((count - 1,)),
        ],
        compiler_params=pltpu.CompilerParams(collective_id=collective_id, has_side_effects=True),
    )(x)


def gather_kernel(x_ref, out_ref, send_sem, recv_sem, *, axis, count, band):
    me = lax.axis_index(axis)
    ids = {name: lax.axis_index(name) for name in ("leaf", "row", "col")}

    def device(peer):
        where = dict(ids)
        where[axis] = peer
        return (where["leaf"], where["row"], where["col"])

    mesh_ids = pl.DeviceIdType.MESH
    barrier = pltpu.get_barrier_semaphore()
    for d in range(1, count):
        pl.semaphore_signal(barrier, inc=1, device_id=device(lax.rem(me + d, count)), device_id_type=mesh_ids)
    pl.semaphore_wait(barrier, count - 1)
    own = pl.ds(pl.multiple_of(me * band, band), band)
    sends = []
    for d in range(1, count):
        peer = lax.rem(me + d, count)
        copy = pltpu.make_async_remote_copy(
            src_ref=x_ref,
            dst_ref=out_ref.at[:, own, :],
            send_sem=send_sem.at[d - 1],
            recv_sem=recv_sem.at[d - 1],
            device_id=device(peer),
            device_id_type=mesh_ids,
        )
        copy.start()
        sends.append(copy)
    out_ref[:, own, :] = x_ref[...]
    for d in range(1, count):
        source = lax.rem(me + count - d, count)
        part = pl.ds(pl.multiple_of(source * band, band), band)
        pltpu.make_async_remote_copy(
            src_ref=x_ref,
            dst_ref=out_ref.at[:, part, :],
            send_sem=send_sem.at[d - 1],
            recv_sem=recv_sem.at[d - 1],
            device_id=device(source),
            device_id_type=mesh_ids,
        ).wait_recv()
    for copy in sends:
        copy.wait_send()


def axis_gather(x, axis, count, collective_id):
    lead, band, last = x.shape
    vmem = pl.BlockSpec(memory_space=pltpu.VMEM)
    return pl.pallas_call(
        functools.partial(gather_kernel, axis=axis, count=count, band=band),
        out_shape=jax.ShapeDtypeStruct((lead, band * count, last), x.dtype),
        in_specs=[vmem],
        out_specs=vmem,
        scratch_shapes=[pltpu.SemaphoreType.DMA((count - 1,)), pltpu.SemaphoreType.DMA((count - 1,))],
        compiler_params=pltpu.CompilerParams(collective_id=collective_id, has_side_effects=True),
    )(x)


def pair_reduce_kernel(x_ref, out_ref, recv_a, recv_b, sems, *, band, chips):
    r = lax.axis_index("row")
    leaf = lax.axis_index("leaf")
    c = lax.axis_index("col")
    core = lax.rem(r, 2)
    chip = r // 2
    partner = r + 1 - 2 * core
    half = band * chips
    mesh_ids = pl.DeviceIdType.MESH
    peers = [2 * lax.rem(chip + d, chips) + core for d in range(1, chips)]

    barrier = pltpu.get_barrier_semaphore()
    for peer in [partner] + peers:
        pl.semaphore_signal(barrier, inc=1, device_id=(leaf, peer, c), device_id_type=mesh_ids)
    pl.semaphore_wait(barrier, chips)

    def rows(start, size):
        return pl.ds(pl.multiple_of(start, band), size)

    mine = rows(core * half, half)
    theirs = rows((1 - core) * half, half)
    copy = pltpu.make_async_remote_copy(
        src_ref=x_ref.at[:, theirs, :], dst_ref=recv_a, send_sem=sems.at[0, 0], recv_sem=sems.at[1, 0],
        device_id=(leaf, partner, c), device_id_type=mesh_ids,
    )
    copy.start()
    copy.wait_recv()
    copy.wait_send()
    recv_a[...] = recv_a[...] + x_ref[:, mine, :]

    sends = []
    for d in range(1, chips):
        target = lax.rem(chip + d, chips)
        copy = pltpu.make_async_remote_copy(
            src_ref=recv_a.at[:, rows(target * band, band), :], dst_ref=recv_b.at[d - 1],
            send_sem=sems.at[0, d], recv_sem=sems.at[1, d],
            device_id=(leaf, 2 * target + core, c), device_id_type=mesh_ids,
        )
        copy.start()
        sends.append(copy)
    for copy in sends:
        copy.wait_recv()
    for copy in sends:
        copy.wait_send()
    total = recv_a[:, rows(chip * band, band), :]
    for d in range(1, chips):
        total = total + recv_b[d - 1]
    own = rows(core * half + chip * band, band)
    out_ref[:, own, :] = total

    sends = []
    for d in range(1, chips):
        target = lax.rem(chip + d, chips)
        copy = pltpu.make_async_remote_copy(
            src_ref=out_ref.at[:, own, :], dst_ref=out_ref.at[:, own, :],
            send_sem=sems.at[2, d - 1], recv_sem=sems.at[3, d - 1],
            device_id=(leaf, 2 * target + core, c), device_id_type=mesh_ids,
        )
        copy.start()
        sends.append(copy)
    for d in range(1, chips):
        source = lax.rem(chip + chips - d, chips)
        part = rows(core * half + source * band, band)
        pltpu.make_async_remote_copy(
            src_ref=out_ref.at[:, part, :], dst_ref=out_ref.at[:, part, :],
            send_sem=sems.at[2, d - 1], recv_sem=sems.at[3, d - 1],
            device_id=(leaf, 2 * source + core, c), device_id_type=mesh_ids,
        ).wait_recv()
    for copy in sends:
        copy.wait_send()

    copy = pltpu.make_async_remote_copy(
        src_ref=out_ref.at[:, mine, :], dst_ref=out_ref.at[:, mine, :],
        send_sem=sems.at[2, chips - 1], recv_sem=sems.at[3, chips - 1],
        device_id=(leaf, partner, c), device_id_type=mesh_ids,
    )
    copy.start()
    pltpu.make_async_remote_copy(
        src_ref=out_ref.at[:, theirs, :], dst_ref=out_ref.at[:, theirs, :],
        send_sem=sems.at[2, chips - 1], recv_sem=sems.at[3, chips - 1],
        device_id=(leaf, partner, c), device_id_type=mesh_ids,
    ).wait_recv()
    copy.wait_send()


def pair_reduce(x, row_count, collective_id):
    lead, total_rows, last = x.shape
    chips = row_count // 2
    band = total_rows // row_count
    vmem = pl.BlockSpec(memory_space=pltpu.VMEM)
    return pl.pallas_call(
        functools.partial(pair_reduce_kernel, band=band, chips=chips),
        out_shape=jax.ShapeDtypeStruct(x.shape, x.dtype),
        in_specs=[vmem],
        out_specs=vmem,
        scratch_shapes=[
            pltpu.VMEM((lead, band * chips, last), x.dtype),
            pltpu.VMEM((chips - 1, lead, band, last), x.dtype),
            pltpu.SemaphoreType.DMA((4, chips)),
        ],
        compiler_params=pltpu.CompilerParams(collective_id=collective_id, has_side_effects=True),
    )(x)


def pair_scatter_kernel(x_ref, out_ref, recv_a, recv_b, sems, *, chips):
    r = lax.axis_index("row")
    leaf = lax.axis_index("leaf")
    c = lax.axis_index("col")
    core = lax.rem(r, 2)
    chip = r // 2
    partner = r + 1 - 2 * core
    mesh_ids = pl.DeviceIdType.MESH
    peers = [2 * lax.rem(chip + d, chips) + core for d in range(1, chips)]

    barrier = pltpu.get_barrier_semaphore()
    for peer in [partner] + peers:
        pl.semaphore_signal(barrier, inc=1, device_id=(leaf, peer, c), device_id_type=mesh_ids)
    pl.semaphore_wait(barrier, chips)

    copy = pltpu.make_async_remote_copy(
        src_ref=x_ref.at[:, :, 1 - core], dst_ref=recv_a, send_sem=sems.at[0, 0], recv_sem=sems.at[1, 0],
        device_id=(leaf, partner, c), device_id_type=mesh_ids,
    )
    copy.start()
    copy.wait_recv()
    copy.wait_send()
    recv_a[...] = recv_a[...] + x_ref[:, :, core]

    sends = []
    for d in range(1, chips):
        target = lax.rem(chip + d, chips)
        copy = pltpu.make_async_remote_copy(
            src_ref=recv_a.at[:, target], dst_ref=recv_b.at[d - 1],
            send_sem=sems.at[0, d], recv_sem=sems.at[1, d],
            device_id=(leaf, 2 * target + core, c), device_id_type=mesh_ids,
        )
        copy.start()
        sends.append(copy)
    for copy in sends:
        copy.wait_recv()
    for copy in sends:
        copy.wait_send()
    total = recv_a[:, chip]
    for d in range(1, chips):
        total = total + recv_b[d - 1]
    out_ref[...] = total


def pair_scatter(x, row_count, collective_id):
    lead, total_rows, last = x.shape
    chips = row_count // 2
    band = total_rows // row_count
    vmem = pl.BlockSpec(memory_space=pltpu.VMEM)
    return pl.pallas_call(
        functools.partial(pair_scatter_kernel, chips=chips),
        out_shape=jax.ShapeDtypeStruct((lead, band, last), x.dtype),
        in_specs=[vmem],
        out_specs=vmem,
        scratch_shapes=[
            pltpu.VMEM((lead, chips, band, last), x.dtype),
            pltpu.VMEM((chips - 1, lead, band, last), x.dtype),
            pltpu.SemaphoreType.DMA((2, chips)),
        ],
        compiler_params=pltpu.CompilerParams(collective_id=collective_id, has_side_effects=True),
    )(x.reshape(lead, chips, 2, band, last))


def pair_gather_kernel(x_ref, out_ref, sems, *, chips, rows):
    r = lax.axis_index("row")
    leaf = lax.axis_index("leaf")
    c = lax.axis_index("col")
    core = lax.rem(r, 2)
    chip = r // 2
    partner = r + 1 - 2 * core
    mesh_ids = pl.DeviceIdType.MESH

    def at(index):
        return out_ref.at[:, pl.ds(pl.multiple_of(index * rows, rows), rows), :]

    barrier = pltpu.get_barrier_semaphore()
    pl.semaphore_signal(barrier, inc=1, device_id=(leaf, partner, c), device_id_type=mesh_ids)
    for d in range(1, chips):
        peer = 2 * lax.rem(chip + d, chips) + core
        pl.semaphore_signal(barrier, inc=1, device_id=(leaf, peer, c), device_id_type=mesh_ids)
    pl.semaphore_wait(barrier, chips)

    sends = []
    copy = pltpu.make_async_remote_copy(
        src_ref=x_ref, dst_ref=at(r), send_sem=sems.at[0, 0], recv_sem=sems.at[1, 0],
        device_id=(leaf, partner, c), device_id_type=mesh_ids,
    )
    copy.start()
    sends.append(copy)
    for d in range(1, chips):
        peer = 2 * lax.rem(chip + d, chips) + core
        copy = pltpu.make_async_remote_copy(
            src_ref=x_ref, dst_ref=at(r), send_sem=sems.at[0, d], recv_sem=sems.at[1, d],
            device_id=(leaf, peer, c), device_id_type=mesh_ids,
        )
        copy.start()
        sends.append(copy)
    out_ref[:, pl.ds(pl.multiple_of(r * rows, rows), rows), :] = x_ref[...]
    for d in range(1, chips):
        source = 2 * lax.rem(chip + chips - d, chips) + core
        pltpu.make_async_remote_copy(
            src_ref=x_ref, dst_ref=at(source), send_sem=sems.at[0, d], recv_sem=sems.at[1, d],
            device_id=(leaf, source, c), device_id_type=mesh_ids,
        ).wait_recv()
        copy = pltpu.make_async_remote_copy(
            src_ref=at(source), dst_ref=at(source), send_sem=sems.at[0, chips + d - 1],
            recv_sem=sems.at[1, chips + d - 1], device_id=(leaf, partner, c), device_id_type=mesh_ids,
        )
        copy.start()
        sends.append(copy)
    pltpu.make_async_remote_copy(
        src_ref=x_ref, dst_ref=at(partner), send_sem=sems.at[0, 0], recv_sem=sems.at[1, 0],
        device_id=(leaf, partner, c), device_id_type=mesh_ids,
    ).wait_recv()
    for d in range(1, chips):
        source = 2 * lax.rem(chip + chips - d, chips) + 1 - core
        pltpu.make_async_remote_copy(
            src_ref=at(source), dst_ref=at(source), send_sem=sems.at[0, chips + d - 1],
            recv_sem=sems.at[1, chips + d - 1], device_id=(leaf, partner, c), device_id_type=mesh_ids,
        ).wait_recv()
    for copy in sends:
        copy.wait_send()


def pair_gather(x, row_count, collective_id):
    lead, rows, last = x.shape
    chips = row_count // 2
    vmem = pl.BlockSpec(memory_space=pltpu.VMEM)
    return pl.pallas_call(
        functools.partial(pair_gather_kernel, chips=chips, rows=rows),
        out_shape=jax.ShapeDtypeStruct((lead, rows * row_count, last), x.dtype),
        in_specs=[vmem],
        out_specs=vmem,
        scratch_shapes=[pltpu.SemaphoreType.DMA((2, 2 * chips - 1))],
        compiler_params=pltpu.CompilerParams(collective_id=collective_id, has_side_effects=True),
    )(x)


def body(sigma_top, panels, inverse_diag, slot_lists, parent_links):
    tile = TILE
    row_count = lax.axis_size("row")
    col_count = lax.axis_size("col")
    leaf_count = lax.axis_size("leaf")
    r = lax.axis_index("row")
    c = lax.axis_index("col")
    panel = panels[0]
    inverse = inverse_diag[0]
    picks_all = slot_lists[0]
    parents = parent_links[0]
    nodes = panel.shape[0]
    width = inverse.shape[2]
    own_tiles = width // tile
    slot_count = picks_all.shape[1]
    positions = slot_count + own_tiles
    band = width // row_count

    partial_factor = mm(panel, inverse)
    factor_rows = axis_reduce(partial_factor, "col", col_count, True, 3)
    living = jnp.concatenate([jnp.ones((1, slot_count), jnp.bool_), picks_all >= 0], axis=0)
    live_here = jnp.take(living, r, axis=1).astype(jnp.float32)
    factor_rows = factor_rows * live_here[:, None, None]
    factor_tile = lax.dynamic_slice_in_dim(factor_rows, c * tile, tile, 2)
    factor_cols = pair_gather(factor_tile, row_count, 5)

    inverse_band = lax.dynamic_slice_in_dim(inverse, r * band, band, 2)
    partial_gram = mm(jnp.transpose(inverse_band, (0, 2, 1)), inverse)
    gram_piece = lax.psum_scatter(partial_gram, "col", scatter_dimension=2, tiled=True)

    leaf = lax.axis_index("leaf")
    local_rows = sigma_top.shape[0]
    chunk_rows = lax.all_gather(sigma_top, "col", axis=1, tiled=True)
    chunks_per_tile = tile // local_rows
    rounds = []
    for t in range(chunks_per_tile):
        pairs = []
        for src_leaf in range(leaf_count):
            for src_row in range(row_count):
                q = src_leaf * row_count + src_row
                dst_leaf = (q % chunks_per_tile + t) % leaf_count
                dst_row = q // chunks_per_tile
                for col in range(col_count):
                    pairs.append(
                        ((src_leaf * row_count + src_row) * col_count + col,
                         (dst_leaf * row_count + dst_row) * col_count + col)
                    )
        rounds.append(lax.ppermute(chunk_rows, ("leaf", "row", "col"), pairs))
    order = lax.rem(leaf - jnp.arange(chunks_per_tile, dtype=jnp.int32) + 4 * leaf_count, leaf_count)
    sigma_rows = jnp.take(jnp.stack(rounds), order, axis=0).reshape(tile, -1)

    def diag_partial(first, products):
        rows = factor_rows[first:first + products.shape[0]]
        return mm(jnp.transpose(rows, (0, 2, 1)), products)

    def reduce_and_gather(first, products, sent, extra, tied=None):
        count = products.shape[0]
        piece = pair_scatter(diag_partial(first, products), row_count, first)
        piece = piece + gram_piece[first:first + count]
        if tied is not None:
            piece, tied = lax.optimization_barrier((piece, tied))
            tied_out.append(tied)
        both = jnp.concatenate([sent, piece] + extra, axis=1)
        everything = lax.all_gather(both, ("row", "col"), axis=0)
        return everything.reshape(row_count, col_count, count, both.shape[1], tile)

    bands_per_tile = tile // band

    def product_col_t(gathered, node, m):
        tiles = lax.dynamic_index_in_dim(gathered[:, :, :, :tile], m, 1, keepdims=False)
        tiles = lax.dynamic_index_in_dim(tiles, node, 1, keepdims=False)
        return jnp.transpose(tiles, (2, 0, 1)).reshape(tile, -1)

    def product_row(gathered, node, q):
        tiles = lax.dynamic_index_in_dim(gathered[:, :, :, :tile], q, 0, keepdims=False)
        tiles = lax.dynamic_index_in_dim(tiles, node, 1, keepdims=False)
        return jnp.transpose(tiles, (1, 0, 2)).reshape(tile, -1)

    def diag_row(gathered, node, m):
        pieces = lax.dynamic_slice_in_dim(gathered[:, :, :, tile:], m * bands_per_tile, bands_per_tile, 0)
        pieces = lax.dynamic_index_in_dim(pieces, node, 2, keepdims=False)
        return jnp.transpose(pieces, (0, 2, 1, 3)).reshape(tile, -1)

    def diag_col(gathered, m, offset):
        pieces = lax.dynamic_index_in_dim(gathered[:, :, :, offset:offset + band], m, 1, keepdims=False)
        return jnp.transpose(pieces, (1, 0, 2, 3)).reshape(pieces.shape[1], -1, tile)

    own_row = jnp.minimum(r, own_tiles - 1)
    upper = r < own_tiles

    product_0 = mm(sigma_rows, factor_cols[0])
    lifted = [
        mm(sigma_rows, scatter_factor(factor_cols[node], picks_all[node - 1], slot_count, tile))[None]
        for node in (1, 2)
    ]
    tied_out = []
    gathered_0 = reduce_and_gather(0, product_0[None], product_0[None], [], jnp.concatenate(lifted, axis=0))
    lifted_cols = axis_gather(tied_out[0], "row", row_count, 4)

    info_1 = jnp.concatenate(
        [r.astype(jnp.int32)[None], picks_all[0:2].reshape(-1), jnp.zeros((2,), jnp.int32), c.astype(jnp.int32)[None]]
    )
    halves = row_count // own_tiles
    product_1, upper_half = level_products(
        info_1, gathered_0, lifted_cols, factor_cols[1:3], 1, tile, band, own_tiles, slot_count,
        tile, tile, halves,
    )
    gathered_1 = reduce_and_gather(1, product_1, upper_half, [])

    info_2 = jnp.concatenate(
        [r.astype(jnp.int32)[None], picks_all[2:nodes - 1].reshape(-1), (parents - 1).astype(jnp.int32),
         c.astype(jnp.int32)[None]]
    )
    (product_2,) = level_products(
        info_2, gathered_1, gathered_0, factor_cols[3:nodes], 2, tile, band, own_tiles, slot_count,
        tile // halves, tile, 0,
    )
    first_2 = 3
    count_2 = product_2.shape[0]
    gram_rows = jnp.zeros((count_2, width, tile), jnp.float32)
    gram_rows = lax.dynamic_update_slice_in_dim(gram_rows, gram_piece[first_2:first_2 + count_2], r * band, 1)
    diag_2 = pair_reduce(diag_partial(first_2, product_2) + gram_rows, row_count, 2)

    products = jnp.concatenate([product_0[None], product_1, product_2], axis=0)
    diag_cols = jnp.concatenate(
        [diag_col(gathered_0, c, tile), diag_col(gathered_1, c, tile // halves), diag_2], axis=0
    )
    return (-products)[None], diag_cols[None]


def solution(mesh):
    return jax.shard_map(
        body,
        mesh=mesh,
        in_specs=(
            P(("leaf", "row"), "col"),
            P("leaf", None, "row", "col"),
            P("leaf", None, "col", None),
            P("leaf", None, None),
            P("leaf", None),
        ),
        out_specs=(P("leaf", None, "row", "col"), P("leaf", None, None, "col")),
        check_vma=False,
    )
```

```python
import functools

import jax
import jax.numpy as jnp
from jax import lax
from jax.experimental import pallas as pl
from jax.experimental.pallas import tpu as pltpu
from jax.sharding import PartitionSpec as P

TILE = 128
HIGHEST = lax.Precision.HIGHEST


def mm(a, b):
    return jnp.matmul(a, b, precision=HIGHEST, preferred_element_type=jnp.float32)


def tile_rows(matrix, index, tile):
    return lax.dynamic_slice_in_dim(matrix, index * tile, tile, 0)


def tile_cols(matrix, index, tile):
    return lax.dynamic_slice_in_dim(matrix, index * tile, tile, 1)


def scatter_factor(factor_col, slots, positions, tile):
    tiles = factor_col.reshape(slots.shape[0], tile, factor_col.shape[1])
    hits = slots[:, None] == jnp.arange(positions, dtype=slots.dtype)[None, :]
    present = jnp.any(hits, axis=0)
    source = jnp.argmax(hits, axis=0)
    moved = jnp.take(tiles, source, axis=0)
    moved = jnp.where(present[:, None, None], moved, 0.0)
    return moved.reshape(positions * tile, factor_col.shape[1])


def dot_hi(a, b):
    return jnp.dot(a, b, precision=HIGHEST, preferred_element_type=jnp.float32)


def dot_t_hi(a, b):
    return lax.dot_general(
        a, b, (((0,), (0,)), ((), ())), precision=HIGHEST, preferred_element_type=jnp.float32
    )


def level_kernel(info_ref, par_ref, low_ref, fac_ref, *rest, level, tile, band, own_tiles, slot_count,
                 par_prow, low_prow, halves, with_diag):
    extra = ()
    if with_diag:
        extra = (rest[0], rest[1], rest[3])
        rest = (rest[2],) + rest[4:]
    out_ref = rest[0]
    rest = rest[1:]
    count = out_ref.shape[0]
    split = tile // band
    r = info_ref[0]
    col = info_ref[1 + count * slot_count + count]
    own = lax.rem(r, own_tiles)

    def p_tile(ref, prow, node, q, m):
        if prow == tile:
            return ref[q, m, node, 0:tile, :]
        parts = tile // prow
        return jnp.concatenate([ref[q + j * own_tiles, m, node, 0:prow, :] for j in range(parts)], axis=0)

    def d_tile(ref, prow, node, a, m):
        return jnp.concatenate([ref[a * split + h, m, node, prow:prow + band, :] for h in range(split)], axis=0)

    for i in range(count):
        base = 1 + i * slot_count
        parent = info_ref[1 + count * slot_count + i]
        factor = [fac_ref[i, k * tile:(k + 1) * tile, :] for k in range(slot_count)]
        picks = [jnp.clip(info_ref[base + k], 0, slot_count - 1) for k in range(slot_count)]
        source = info_ref[base + jnp.maximum(r, own_tiles)]

        upper = dot_hi(d_tile(par_ref, par_prow, parent, own, 0), factor[0])
        for k in range(1, own_tiles):
            upper += dot_hi(d_tile(par_ref, par_prow, parent, own, k), factor[k])
        for k in range(own_tiles, slot_count):
            pick = picks[k] if par_prow == tile else jnp.minimum(picks[k], own_tiles - 1)
            upper -= dot_t_hi(p_tile(par_ref, par_prow, parent, pick, own), factor[k])

        if halves:
            half_ref = rest[0]
            rows = tile // halves
            which = r // own_tiles
            half = upper[0:rows]
            for j in range(1, halves):
                half = jnp.where(which == j, upper[j * rows:(j + 1) * rows], half)
            half_ref[i] = half

        @pl.when(r < own_tiles)
        def _():
            out_ref[i] = upper

        @pl.when(jnp.logical_and(r >= own_tiles, source >= 0))
        def _():
            if level == 1:
                s = jnp.clip(source, 0, slot_count - 1)
                acc = low_ref[i, pl.ds(pl.multiple_of(s * tile, tile), tile), :]
                for k in range(own_tiles):
                    acc -= dot_hi(p_tile(par_ref, par_prow, parent, s, k), factor[k])
            else:
                s = jnp.clip(source, 0, own_tiles - 1)
                acc = -dot_hi(p_tile(par_ref, par_prow, parent, s, 0), factor[0])
                for k in range(1, own_tiles):
                    acc -= dot_hi(p_tile(par_ref, par_prow, parent, s, k), factor[k])
                for k in range(own_tiles, slot_count):
                    q = jnp.minimum(picks[k], own_tiles - 1)
                    acc += dot_hi(d_tile(low_ref, low_prow, 0, s, q), factor[k])
            out_ref[i] = acc

        @pl.when(jnp.logical_and(r >= own_tiles, source < 0))
        def _():
            out_ref[i] = jnp.zeros((tile, tile), jnp.float32)

        if extra:
            rows_ref, gram_ref, diag_ref = extra
            diag_ref[i] = dot_t_hi(rows_ref[i], out_ref[i])
            start = pl.multiple_of(r * band, band)
            diag_ref[i, pl.ds(start, band), :] = diag_ref[i, pl.ds(start, band), :] + gram_ref[i]


def level_products(info, parent_data, low_data, factors, level, tile, band, own_tiles, slot_count,
                   par_prow, low_prow, halves, diag_inputs=()):
    kernel = functools.partial(
        level_kernel, level=level, tile=tile, band=band, own_tiles=own_tiles, slot_count=slot_count,
        par_prow=par_prow, low_prow=low_prow, halves=halves, with_diag=bool(diag_inputs),
    )
    vmem = pl.BlockSpec(memory_space=pltpu.VMEM)
    count = factors.shape[0]
    shapes = [jax.ShapeDtypeStruct((count, tile, tile), jnp.float32)]
    if halves:
        shapes.append(jax.ShapeDtypeStruct((count, tile // halves, tile), jnp.float32))
    if diag_inputs:
        width = diag_inputs[0].shape[2]
        shapes.append(jax.ShapeDtypeStruct((count, width, tile), jnp.float32))
    return pl.pallas_call(
        kernel,
        out_shape=tuple(shapes),
        in_specs=[pl.BlockSpec(memory_space=pltpu.SMEM)] + [vmem] * (3 + len(diag_inputs)),
        out_specs=tuple([vmem] * len(shapes)),
    )(info, parent_data, low_data, factors, *diag_inputs)


def reduce_kernel(x_ref, out_ref, recv_ref, send_sem, recv_sem, back_send, back_recv, *, axis, count, band, gather):
    me = lax.axis_index(axis)
    ids = {name: lax.axis_index(name) for name in ("leaf", "row", "col")}

    def device(peer):
        where = dict(ids)
        where[axis] = peer
        return (where["leaf"], where["row"], where["col"])

    mesh_ids = pl.DeviceIdType.MESH
    barrier = pltpu.get_barrier_semaphore()
    for d in range(1, count):
        pl.semaphore_signal(barrier, inc=1, device_id=device(lax.rem(me + d, count)), device_id_type=mesh_ids)
    pl.semaphore_wait(barrier, count - 1)

    sends = []
    for d in range(1, count):
        peer = lax.rem(me + d, count)
        copy = pltpu.make_async_remote_copy(
            src_ref=x_ref.at[:, pl.ds(pl.multiple_of(peer * band, band), band), :],
            dst_ref=recv_ref.at[d - 1],
            send_sem=send_sem.at[d - 1],
            recv_sem=recv_sem.at[d - 1],
            device_id=device(peer),
            device_id_type=mesh_ids,
        )
        copy.start()
        sends.append(copy)
    for copy in sends:
        copy.wait_recv()
    for copy in sends:
        copy.wait_send()
    own = pl.ds(pl.multiple_of(me * band, band), band)
    total = x_ref[:, own, :]
    for d in range(1, count):
        total = total + recv_ref[d - 1]
    if not gather:
        out_ref[...] = total
        return
    out_ref[:, own, :] = total
    backs = []
    for d in range(1, count):
        peer = lax.rem(me + d, count)
        copy = pltpu.make_async_remote_copy(
            src_ref=out_ref.at[:, own, :],
            dst_ref=out_ref.at[:, own, :],
            send_sem=back_send.at[d - 1],
            recv_sem=back_recv.at[d - 1],
            device_id=device(peer),
            device_id_type=mesh_ids,
        )
        copy.start()
        backs.append(copy)
    for d in range(1, count):
        source = lax.rem(me + count - d, count)
        part = pl.ds(pl.multiple_of(source * band, band), band)
        pltpu.make_async_remote_copy(
            src_ref=out_ref.at[:, part, :],
            dst_ref=out_ref.at[:, part, :],
            send_sem=back_send.at[d - 1],
            recv_sem=back_recv.at[d - 1],
            device_id=device(source),
            device_id_type=mesh_ids,
        ).wait_recv()
    for copy in backs:
        copy.wait_send()


def axis_reduce(x, axis, count, gather, collective_id):
    lead, rows, last = x.shape
    band = rows // count
    kernel = functools.partial(reduce_kernel, axis=axis, count=count, band=band, gather=gather)
    out_rows = rows if gather else band
    vmem = pl.BlockSpec(memory_space=pltpu.VMEM)
    return pl.pallas_call(
        kernel,
        out_shape=jax.ShapeDtypeStruct((lead, out_rows, last), x.dtype),
        in_specs=[vmem],
        out_specs=vmem,
        scratch_shapes=[
            pltpu.VMEM((count - 1, lead, band, last), x.dtype),
            pltpu.SemaphoreType.DMA((count - 1,)),
            pltpu.SemaphoreType.DMA((count - 1,)),
            pltpu.SemaphoreType.DMA((count - 1,)),
            pltpu.SemaphoreType.DMA((count - 1,)),
        ],
        compiler_params=pltpu.CompilerParams(collective_id=collective_id, has_side_effects=True),
    )(x)


def gather_kernel(x_ref, out_ref, send_sem, recv_sem, *, axis, count, band):
    me = lax.axis_index(axis)
    ids = {name: lax.axis_index(name) for name in ("leaf", "row", "col")}

    def device(peer):
        where = dict(ids)
        where[axis] = peer
        return (where["leaf"], where["row"], where["col"])

    mesh_ids = pl.DeviceIdType.MESH
    barrier = pltpu.get_barrier_semaphore()
    for d in range(1, count):
        pl.semaphore_signal(barrier, inc=1, device_id=device(lax.rem(me + d, count)), device_id_type=mesh_ids)
    pl.semaphore_wait(barrier, count - 1)
    own = pl.ds(pl.multiple_of(me * band, band), band)
    sends = []
    for d in range(1, count):
        peer = lax.rem(me + d, count)
        copy = pltpu.make_async_remote_copy(
            src_ref=x_ref,
            dst_ref=out_ref.at[:, own, :],
            send_sem=send_sem.at[d - 1],
            recv_sem=recv_sem.at[d - 1],
            device_id=device(peer),
            device_id_type=mesh_ids,
        )
        copy.start()
        sends.append(copy)
    out_ref[:, own, :] = x_ref[...]
    for d in range(1, count):
        source = lax.rem(me + count - d, count)
        part = pl.ds(pl.multiple_of(source * band, band), band)
        pltpu.make_async_remote_copy(
            src_ref=x_ref,
            dst_ref=out_ref.at[:, part, :],
            send_sem=send_sem.at[d - 1],
            recv_sem=recv_sem.at[d - 1],
            device_id=device(source),
            device_id_type=mesh_ids,
        ).wait_recv()
    for copy in sends:
        copy.wait_send()


def axis_gather(x, axis, count, collective_id):
    lead, band, last = x.shape
    vmem = pl.BlockSpec(memory_space=pltpu.VMEM)
    return pl.pallas_call(
        functools.partial(gather_kernel, axis=axis, count=count, band=band),
        out_shape=jax.ShapeDtypeStruct((lead, band * count, last), x.dtype),
        in_specs=[vmem],
        out_specs=vmem,
        scratch_shapes=[pltpu.SemaphoreType.DMA((count - 1,)), pltpu.SemaphoreType.DMA((count - 1,))],
        compiler_params=pltpu.CompilerParams(collective_id=collective_id, has_side_effects=True),
    )(x)


def pair_reduce_kernel(x_ref, out_ref, recv_a, recv_b, sems, *, band, chips):
    r = lax.axis_index("row")
    leaf = lax.axis_index("leaf")
    c = lax.axis_index("col")
    core = lax.rem(r, 2)
    chip = r // 2
    partner = r + 1 - 2 * core
    half = band * chips
    mesh_ids = pl.DeviceIdType.MESH
    peers = [2 * lax.rem(chip + d, chips) + core for d in range(1, chips)]

    barrier = pltpu.get_barrier_semaphore()
    for peer in [partner] + peers:
        pl.semaphore_signal(barrier, inc=1, device_id=(leaf, peer, c), device_id_type=mesh_ids)
    pl.semaphore_wait(barrier, chips)

    def rows(start, size):
        return pl.ds(pl.multiple_of(start, band), size)

    mine = rows(core * half, half)
    theirs = rows((1 - core) * half, half)
    copy = pltpu.make_async_remote_copy(
        src_ref=x_ref.at[:, theirs, :], dst_ref=recv_a, send_sem=sems.at[0, 0], recv_sem=sems.at[1, 0],
        device_id=(leaf, partner, c), device_id_type=mesh_ids,
    )
    copy.start()
    copy.wait_recv()
    copy.wait_send()
    recv_a[...] = recv_a[...] + x_ref[:, mine, :]

    sends = []
    for d in range(1, chips):
        target = lax.rem(chip + d, chips)
        copy = pltpu.make_async_remote_copy(
            src_ref=recv_a.at[:, rows(target * band, band), :], dst_ref=recv_b.at[d - 1],
            send_sem=sems.at[0, d], recv_sem=sems.at[1, d],
            device_id=(leaf, 2 * target + core, c), device_id_type=mesh_ids,
        )
        copy.start()
        sends.append(copy)
    for copy in sends:
        copy.wait_recv()
    for copy in sends:
        copy.wait_send()
    total = recv_a[:, rows(chip * band, band), :]
    for d in range(1, chips):
        total = total + recv_b[d - 1]
    own = rows(core * half + chip * band, band)
    out_ref[:, own, :] = total

    sends = []
    for d in range(1, chips):
        target = lax.rem(chip + d, chips)
        copy = pltpu.make_async_remote_copy(
            src_ref=out_ref.at[:, own, :], dst_ref=out_ref.at[:, own, :],
            send_sem=sems.at[2, d - 1], recv_sem=sems.at[3, d - 1],
            device_id=(leaf, 2 * target + core, c), device_id_type=mesh_ids,
        )
        copy.start()
        sends.append(copy)
    for d in range(1, chips):
        source = lax.rem(chip + chips - d, chips)
        part = rows(core * half + source * band, band)
        pltpu.make_async_remote_copy(
            src_ref=out_ref.at[:, part, :], dst_ref=out_ref.at[:, part, :],
            send_sem=sems.at[2, d - 1], recv_sem=sems.at[3, d - 1],
            device_id=(leaf, 2 * source + core, c), device_id_type=mesh_ids,
        ).wait_recv()
    for copy in sends:
        copy.wait_send()

    copy = pltpu.make_async_remote_copy(
        src_ref=out_ref.at[:, mine, :], dst_ref=out_ref.at[:, mine, :],
        send_sem=sems.at[2, chips - 1], recv_sem=sems.at[3, chips - 1],
        device_id=(leaf, partner, c), device_id_type=mesh_ids,
    )
    copy.start()
    pltpu.make_async_remote_copy(
        src_ref=out_ref.at[:, theirs, :], dst_ref=out_ref.at[:, theirs, :],
        send_sem=sems.at[2, chips - 1], recv_sem=sems.at[3, chips - 1],
        device_id=(leaf, partner, c), device_id_type=mesh_ids,
    ).wait_recv()
    copy.wait_send()


def pair_reduce(x, row_count, collective_id):
    lead, total_rows, last = x.shape
    chips = row_count // 2
    band = total_rows // row_count
    vmem = pl.BlockSpec(memory_space=pltpu.VMEM)
    return pl.pallas_call(
        functools.partial(pair_reduce_kernel, band=band, chips=chips),
        out_shape=jax.ShapeDtypeStruct(x.shape, x.dtype),
        in_specs=[vmem],
        out_specs=vmem,
        scratch_shapes=[
            pltpu.VMEM((lead, band * chips, last), x.dtype),
            pltpu.VMEM((chips - 1, lead, band, last), x.dtype),
            pltpu.SemaphoreType.DMA((4, chips)),
        ],
        compiler_params=pltpu.CompilerParams(collective_id=collective_id, has_side_effects=True),
    )(x)


def pair_scatter_kernel(x_ref, out_ref, recv_a, recv_b, sems, *, chips):
    r = lax.axis_index("row")
    leaf = lax.axis_index("leaf")
    c = lax.axis_index("col")
    core = lax.rem(r, 2)
    chip = r // 2
    partner = r + 1 - 2 * core
    mesh_ids = pl.DeviceIdType.MESH
    peers = [2 * lax.rem(chip + d, chips) + core for d in range(1, chips)]

    barrier = pltpu.get_barrier_semaphore()
    for peer in [partner] + peers:
        pl.semaphore_signal(barrier, inc=1, device_id=(leaf, peer, c), device_id_type=mesh_ids)
    pl.semaphore_wait(barrier, chips)

    copy = pltpu.make_async_remote_copy(
        src_ref=x_ref.at[:, :, 1 - core], dst_ref=recv_a, send_sem=sems.at[0, 0], recv_sem=sems.at[1, 0],
        device_id=(leaf, partner, c), device_id_type=mesh_ids,
    )
    copy.start()
    copy.wait_recv()
    copy.wait_send()
    recv_a[...] = recv_a[...] + x_ref[:, :, core]

    sends = []
    for d in range(1, chips):
        target = lax.rem(chip + d, chips)
        copy = pltpu.make_async_remote_copy(
            src_ref=recv_a.at[:, target], dst_ref=recv_b.at[d - 1],
            send_sem=sems.at[0, d], recv_sem=sems.at[1, d],
            device_id=(leaf, 2 * target + core, c), device_id_type=mesh_ids,
        )
        copy.start()
        sends.append(copy)
    for copy in sends:
        copy.wait_recv()
    for copy in sends:
        copy.wait_send()
    total = recv_a[:, chip]
    for d in range(1, chips):
        total = total + recv_b[d - 1]
    out_ref[...] = total


def pair_scatter(x, row_count, collective_id):
    lead, total_rows, last = x.shape
    chips = row_count // 2
    band = total_rows // row_count
    vmem = pl.BlockSpec(memory_space=pltpu.VMEM)
    return pl.pallas_call(
        functools.partial(pair_scatter_kernel, chips=chips),
        out_shape=jax.ShapeDtypeStruct((lead, band, last), x.dtype),
        in_specs=[vmem],
        out_specs=vmem,
        scratch_shapes=[
            pltpu.VMEM((lead, chips, band, last), x.dtype),
            pltpu.VMEM((chips - 1, lead, band, last), x.dtype),
            pltpu.SemaphoreType.DMA((2, chips)),
        ],
        compiler_params=pltpu.CompilerParams(collective_id=collective_id, has_side_effects=True),
    )(x.reshape(lead, chips, 2, band, last))


def body(sigma_top, panels, inverse_diag, slot_lists, parent_links):
    tile = TILE
    row_count = lax.axis_size("row")
    col_count = lax.axis_size("col")
    leaf_count = lax.axis_size("leaf")
    r = lax.axis_index("row")
    c = lax.axis_index("col")
    panel = panels[0]
    inverse = inverse_diag[0]
    picks_all = slot_lists[0]
    parents = parent_links[0]
    nodes = panel.shape[0]
    width = inverse.shape[2]
    own_tiles = width // tile
    slot_count = picks_all.shape[1]
    positions = slot_count + own_tiles
    band = width // row_count

    partial_factor = mm(panel, inverse)
    factor_rows = axis_reduce(partial_factor, "col", col_count, True, 3)
    living = jnp.concatenate([jnp.ones((1, slot_count), jnp.bool_), picks_all >= 0], axis=0)
    live_here = jnp.take(living, r, axis=1).astype(jnp.float32)
    factor_rows = factor_rows * live_here[:, None, None]
    factor_tile = lax.dynamic_slice_in_dim(factor_rows, c * tile, tile, 2)
    factor_cols = lax.all_gather(factor_tile, "row", axis=1, tiled=True)

    inverse_band = lax.dynamic_slice_in_dim(inverse, r * band, band, 2)
    partial_gram = mm(jnp.transpose(inverse_band, (0, 2, 1)), inverse)
    gram_piece = lax.psum_scatter(partial_gram, "col", scatter_dimension=2, tiled=True)

    leaf = lax.axis_index("leaf")
    local_rows = sigma_top.shape[0]
    chunk_rows = lax.all_gather(sigma_top, "col", axis=1, tiled=True)
    chunks_per_tile = tile // local_rows
    rounds = []
    for t in range(chunks_per_tile):
        pairs = []
        for src_leaf in range(leaf_count):
            for src_row in range(row_count):
                q = src_leaf * row_count + src_row
                dst_leaf = (q % chunks_per_tile + t) % leaf_count
                dst_row = q // chunks_per_tile
                for col in range(col_count):
                    pairs.append(
                        ((src_leaf * row_count + src_row) * col_count + col,
                         (dst_leaf * row_count + dst_row) * col_count + col)
                    )
        rounds.append(lax.ppermute(chunk_rows, ("leaf", "row", "col"), pairs))
    order = lax.rem(leaf - jnp.arange(chunks_per_tile, dtype=jnp.int32) + 4 * leaf_count, leaf_count)
    sigma_rows = jnp.take(jnp.stack(rounds), order, axis=0).reshape(tile, -1)

    def diag_partial(first, products):
        rows = factor_rows[first:first + products.shape[0]]
        return mm(jnp.transpose(rows, (0, 2, 1)), products)

    def reduce_and_gather(first, products, sent, extra, tied=None):
        count = products.shape[0]
        piece = pair_scatter(diag_partial(first, products), row_count, first)
        piece = piece + gram_piece[first:first + count]
        if tied is not None:
            piece, tied = lax.optimization_barrier((piece, tied))
            tied_out.append(tied)
        both = jnp.concatenate([sent, piece] + extra, axis=1)
        everything = lax.all_gather(both, ("row", "col"), axis=0)
        return everything.reshape(row_count, col_count, count, both.shape[1], tile)

    bands_per_tile = tile // band

    def product_col_t(gathered, node, m):
        tiles = lax.dynamic_index_in_dim(gathered[:, :, :, :tile], m, 1, keepdims=False)
        tiles = lax.dynamic_index_in_dim(tiles, node, 1, keepdims=False)
        return jnp.transpose(tiles, (2, 0, 1)).reshape(tile, -1)

    def product_row(gathered, node, q):
        tiles = lax.dynamic_index_in_dim(gathered[:, :, :, :tile], q, 0, keepdims=False)
        tiles = lax.dynamic_index_in_dim(tiles, node, 1, keepdims=False)
        return jnp.transpose(tiles, (1, 0, 2)).reshape(tile, -1)

    def diag_row(gathered, node, m):
        pieces = lax.dynamic_slice_in_dim(gathered[:, :, :, tile:], m * bands_per_tile, bands_per_tile, 0)
        pieces = lax.dynamic_index_in_dim(pieces, node, 2, keepdims=False)
        return jnp.transpose(pieces, (0, 2, 1, 3)).reshape(tile, -1)

    def diag_col(gathered, m, offset):
        pieces = lax.dynamic_index_in_dim(gathered[:, :, :, offset:offset + band], m, 1, keepdims=False)
        return jnp.transpose(pieces, (1, 0, 2, 3)).reshape(pieces.shape[1], -1, tile)

    own_row = jnp.minimum(r, own_tiles - 1)
    upper = r < own_tiles

    product_0 = mm(sigma_rows, factor_cols[0])
    lifted = [
        mm(sigma_rows, scatter_factor(factor_cols[node], picks_all[node - 1], slot_count, tile))[None]
        for node in (1, 2)
    ]
    tied_out = []
    gathered_0 = reduce_and_gather(0, product_0[None], product_0[None], [], jnp.concatenate(lifted, axis=0))
    lifted_cols = axis_gather(tied_out[0], "row", row_count, 4)

    info_1 = jnp.concatenate(
        [r.astype(jnp.int32)[None], picks_all[0:2].reshape(-1), jnp.zeros((2,), jnp.int32), c.astype(jnp.int32)[None]]
    )
    halves = row_count // own_tiles
    product_1, upper_half = level_products(
        info_1, gathered_0, lifted_cols, factor_cols[1:3], 1, tile, band, own_tiles, slot_count,
        tile, tile, halves,
    )
    gathered_1 = reduce_and_gather(1, product_1, upper_half, [])

    info_2 = jnp.concatenate(
        [r.astype(jnp.int32)[None], picks_all[2:nodes - 1].reshape(-1), (parents - 1).astype(jnp.int32),
         c.astype(jnp.int32)[None]]
    )
    product_2, partial_2 = level_products(
        info_2, gathered_1, gathered_0, factor_cols[3:nodes], 2, tile, band, own_tiles, slot_count,
        tile // halves, tile, 0, (factor_rows[3:nodes], gram_piece[3:nodes]),
    )
    diag_2 = pair_reduce(partial_2, row_count, 2)

    products = jnp.concatenate([product_0[None], product_1, product_2], axis=0)
    diag_cols = jnp.concatenate(
        [diag_col(gathered_0, c, tile), diag_col(gathered_1, c, tile // halves), diag_2], axis=0
    )
    return (-products)[None], diag_cols[None]


def solution(mesh):
    return jax.shard_map(
        body,
        mesh=mesh,
        in_specs=(
            P(("leaf", "row"), "col"),
            P("leaf", None, "row", "col"),
            P("leaf", None, "col", None),
            P("leaf", None, None),
            P("leaf", None),
        ),
        out_specs=(P("leaf", None, "row", "col"), P("leaf", None, None, "col")),
        check_vma=False,
    )
```

```python
import functools

import jax
import jax.numpy as jnp
from jax import lax
from jax.experimental import pallas as pl
from jax.experimental.pallas import tpu as pltpu
from jax.sharding import PartitionSpec as P

TILE = 128
HIGHEST = lax.Precision.HIGHEST


def mm(a, b):
    return jnp.matmul(a, b, precision=HIGHEST, preferred_element_type=jnp.float32)


def tile_rows(matrix, index, tile):
    return lax.dynamic_slice_in_dim(matrix, index * tile, tile, 0)


def tile_cols(matrix, index, tile):
    return lax.dynamic_slice_in_dim(matrix, index * tile, tile, 1)


def scatter_factor(factor_col, slots, positions, tile):
    tiles = factor_col.reshape(slots.shape[0], tile, factor_col.shape[1])
    hits = slots[:, None] == jnp.arange(positions, dtype=slots.dtype)[None, :]
    present = jnp.any(hits, axis=0)
    source = jnp.argmax(hits, axis=0)
    moved = jnp.take(tiles, source, axis=0)
    moved = jnp.where(present[:, None, None], moved, 0.0)
    return moved.reshape(positions * tile, factor_col.shape[1])


def dot_hi(a, b):
    return jnp.dot(a, b, precision=HIGHEST, preferred_element_type=jnp.float32)


def dot_t_hi(a, b):
    return lax.dot_general(
        a, b, (((0,), (0,)), ((), ())), precision=HIGHEST, preferred_element_type=jnp.float32
    )


def level_kernel(info_ref, par_ref, low_ref, fac_ref, *rest, level, tile, band, own_tiles, slot_count,
                 par_prow, low_prow, halves, with_diag):
    extra = ()
    if with_diag:
        extra = (rest[0], rest[1], rest[-1])
        rest = rest[2:-1]
    out_ref = rest[0]
    rest = rest[1:]
    count = out_ref.shape[0]
    split = tile // band
    r = info_ref[0]
    col = info_ref[1 + count * slot_count + count]
    own = lax.rem(r, own_tiles)

    def p_tile(ref, prow, node, q, m):
        if prow == tile:
            return ref[q, m, node, 0:tile, :]
        parts = tile // prow
        return jnp.concatenate([ref[q + j * own_tiles, m, node, 0:prow, :] for j in range(parts)], axis=0)

    def d_tile(ref, prow, node, a, m):
        return jnp.concatenate([ref[a * split + h, m, node, prow:prow + band, :] for h in range(split)], axis=0)

    for i in range(count):
        base = 1 + i * slot_count
        parent = info_ref[1 + count * slot_count + i]
        factor = [fac_ref[i, k * tile:(k + 1) * tile, :] for k in range(slot_count)]
        picks = [jnp.clip(info_ref[base + k], 0, slot_count - 1) for k in range(slot_count)]
        source = info_ref[base + jnp.maximum(r, own_tiles)]

        upper = dot_hi(d_tile(par_ref, par_prow, parent, own, 0), factor[0])
        for k in range(1, own_tiles):
            upper += dot_hi(d_tile(par_ref, par_prow, parent, own, k), factor[k])
        for k in range(own_tiles, slot_count):
            pick = picks[k] if par_prow == tile else jnp.minimum(picks[k], own_tiles - 1)
            upper -= dot_t_hi(p_tile(par_ref, par_prow, parent, pick, own), factor[k])

        if halves:
            half_ref = rest[0]
            rows = tile // halves
            which = r // own_tiles
            half = upper[0:rows]
            for j in range(1, halves):
                half = jnp.where(which == j, upper[j * rows:(j + 1) * rows], half)
            half_ref[i] = half

        @pl.when(r < own_tiles)
        def _():
            out_ref[i] = upper

        @pl.when(jnp.logical_and(r >= own_tiles, source >= 0))
        def _():
            if level == 1:
                s = jnp.clip(source, 0, slot_count - 1)
                acc = low_ref[i, pl.ds(pl.multiple_of(s * tile, tile), tile), :]
                for k in range(own_tiles):
                    acc -= dot_hi(p_tile(par_ref, par_prow, parent, s, k), factor[k])
            else:
                s = jnp.clip(source, 0, own_tiles - 1)
                acc = -dot_hi(p_tile(par_ref, par_prow, parent, s, 0), factor[0])
                for k in range(1, own_tiles):
                    acc -= dot_hi(p_tile(par_ref, par_prow, parent, s, k), factor[k])
                for k in range(own_tiles, slot_count):
                    q = jnp.minimum(picks[k], own_tiles - 1)
                    acc += dot_hi(d_tile(low_ref, low_prow, 0, s, q), factor[k])
            out_ref[i] = acc

        @pl.when(jnp.logical_and(r >= own_tiles, source < 0))
        def _():
            out_ref[i] = jnp.zeros((tile, tile), jnp.float32)

        if extra:
            rows_ref, gram_ref, diag_ref = extra
            diag_ref[i] = dot_t_hi(rows_ref[i], out_ref[i])
            start = pl.multiple_of(r * band, band)
            diag_ref[i, pl.ds(start, band), :] = diag_ref[i, pl.ds(start, band), :] + gram_ref[i]


def level_products(info, parent_data, low_data, factors, level, tile, band, own_tiles, slot_count,
                   par_prow, low_prow, halves, diag_inputs=()):
    kernel = functools.partial(
        level_kernel, level=level, tile=tile, band=band, own_tiles=own_tiles, slot_count=slot_count,
        par_prow=par_prow, low_prow=low_prow, halves=halves, with_diag=bool(diag_inputs),
    )
    vmem = pl.BlockSpec(memory_space=pltpu.VMEM)
    count = factors.shape[0]
    shapes = [jax.ShapeDtypeStruct((count, tile, tile), jnp.float32)]
    if halves:
        shapes.append(jax.ShapeDtypeStruct((count, tile // halves, tile), jnp.float32))
    if diag_inputs:
        width = diag_inputs[0].shape[2]
        shapes.append(jax.ShapeDtypeStruct((count, width, tile), jnp.float32))
    return pl.pallas_call(
        kernel,
        out_shape=tuple(shapes),
        in_specs=[pl.BlockSpec(memory_space=pltpu.SMEM)] + [vmem] * (3 + len(diag_inputs)),
        out_specs=tuple([vmem] * len(shapes)),
    )(info, parent_data, low_data, factors, *diag_inputs)


def reduce_kernel(x_ref, out_ref, recv_ref, send_sem, recv_sem, back_send, back_recv, *, axis, count, band, gather):
    me = lax.axis_index(axis)
    ids = {name: lax.axis_index(name) for name in ("leaf", "row", "col")}

    def device(peer):
        where = dict(ids)
        where[axis] = peer
        return (where["leaf"], where["row"], where["col"])

    mesh_ids = pl.DeviceIdType.MESH
    barrier = pltpu.get_barrier_semaphore()
    for d in range(1, count):
        pl.semaphore_signal(barrier, inc=1, device_id=device(lax.rem(me + d, count)), device_id_type=mesh_ids)
    pl.semaphore_wait(barrier, count - 1)

    sends = []
    for d in range(1, count):
        peer = lax.rem(me + d, count)
        copy = pltpu.make_async_remote_copy(
            src_ref=x_ref.at[:, pl.ds(pl.multiple_of(peer * band, band), band), :],
            dst_ref=recv_ref.at[d - 1],
            send_sem=send_sem.at[d - 1],
            recv_sem=recv_sem.at[d - 1],
            device_id=device(peer),
            device_id_type=mesh_ids,
        )
        copy.start()
        sends.append(copy)
    for copy in sends:
        copy.wait_recv()
    for copy in sends:
        copy.wait_send()
    own = pl.ds(pl.multiple_of(me * band, band), band)
    total = x_ref[:, own, :]
    for d in range(1, count):
        total = total + recv_ref[d - 1]
    if not gather:
        out_ref[...] = total
        return
    out_ref[:, own, :] = total
    backs = []
    for d in range(1, count):
        peer = lax.rem(me + d, count)
        copy = pltpu.make_async_remote_copy(
            src_ref=out_ref.at[:, own, :],
            dst_ref=out_ref.at[:, own, :],
            send_sem=back_send.at[d - 1],
            recv_sem=back_recv.at[d - 1],
            device_id=device(peer),
            device_id_type=mesh_ids,
        )
        copy.start()
        backs.append(copy)
    for d in range(1, count):
        source = lax.rem(me + count - d, count)
        part = pl.ds(pl.multiple_of(source * band, band), band)
        pltpu.make_async_remote_copy(
            src_ref=out_ref.at[:, part, :],
            dst_ref=out_ref.at[:, part, :],
            send_sem=back_send.at[d - 1],
            recv_sem=back_recv.at[d - 1],
            device_id=device(source),
            device_id_type=mesh_ids,
        ).wait_recv()
    for copy in backs:
        copy.wait_send()


def axis_reduce(x, axis, count, gather, collective_id):
    lead, rows, last = x.shape
    band = rows // count
    kernel = functools.partial(reduce_kernel, axis=axis, count=count, band=band, gather=gather)
    out_rows = rows if gather else band
    vmem = pl.BlockSpec(memory_space=pltpu.VMEM)
    return pl.pallas_call(
        kernel,
        out_shape=jax.ShapeDtypeStruct((lead, out_rows, last), x.dtype),
        in_specs=[vmem],
        out_specs=vmem,
        scratch_shapes=[
            pltpu.VMEM((count - 1, lead, band, last), x.dtype),
            pltpu.SemaphoreType.DMA((count - 1,)),
            pltpu.SemaphoreType.DMA((count - 1,)),
            pltpu.SemaphoreType.DMA((count - 1,)),
            pltpu.SemaphoreType.DMA((count - 1,)),
        ],
        compiler_params=pltpu.CompilerParams(collective_id=collective_id, has_side_effects=True),
    )(x)


def gather_kernel(x_ref, out_ref, send_sem, recv_sem, *, axis, count, band):
    me = lax.axis_index(axis)
    ids = {name: lax.axis_index(name) for name in ("leaf", "row", "col")}

    def device(peer):
        where = dict(ids)
        where[axis] = peer
        return (where["leaf"], where["row"], where["col"])

    mesh_ids = pl.DeviceIdType.MESH
    barrier = pltpu.get_barrier_semaphore()
    for d in range(1, count):
        pl.semaphore_signal(barrier, inc=1, device_id=device(lax.rem(me + d, count)), device_id_type=mesh_ids)
    pl.semaphore_wait(barrier, count - 1)
    own = pl.ds(pl.multiple_of(me * band, band), band)
    sends = []
    for d in range(1, count):
        peer = lax.rem(me + d, count)
        copy = pltpu.make_async_remote_copy(
            src_ref=x_ref,
            dst_ref=out_ref.at[:, own, :],
            send_sem=send_sem.at[d - 1],
            recv_sem=recv_sem.at[d - 1],
            device_id=device(peer),
            device_id_type=mesh_ids,
        )
        copy.start()
        sends.append(copy)
    out_ref[:, own, :] = x_ref[...]
    for d in range(1, count):
        source = lax.rem(me + count - d, count)
        part = pl.ds(pl.multiple_of(source * band, band), band)
        pltpu.make_async_remote_copy(
            src_ref=x_ref,
            dst_ref=out_ref.at[:, part, :],
            send_sem=send_sem.at[d - 1],
            recv_sem=recv_sem.at[d - 1],
            device_id=device(source),
            device_id_type=mesh_ids,
        ).wait_recv()
    for copy in sends:
        copy.wait_send()


def axis_gather(x, axis, count, collective_id):
    lead, band, last = x.shape
    vmem = pl.BlockSpec(memory_space=pltpu.VMEM)
    return pl.pallas_call(
        functools.partial(gather_kernel, axis=axis, count=count, band=band),
        out_shape=jax.ShapeDtypeStruct((lead, band * count, last), x.dtype),
        in_specs=[vmem],
        out_specs=vmem,
        scratch_shapes=[pltpu.SemaphoreType.DMA((count - 1,)), pltpu.SemaphoreType.DMA((count - 1,))],
        compiler_params=pltpu.CompilerParams(collective_id=collective_id, has_side_effects=True),
    )(x)


def pair_reduce_kernel(x_ref, out_ref, recv_a, recv_b, sems, *, band, chips):
    r = lax.axis_index("row")
    leaf = lax.axis_index("leaf")
    c = lax.axis_index("col")
    core = lax.rem(r, 2)
    chip = r // 2
    partner = r + 1 - 2 * core
    half = band * chips
    mesh_ids = pl.DeviceIdType.MESH
    peers = [2 * lax.rem(chip + d, chips) + core for d in range(1, chips)]

    barrier = pltpu.get_barrier_semaphore()
    for peer in [partner] + peers:
        pl.semaphore_signal(barrier, inc=1, device_id=(leaf, peer, c), device_id_type=mesh_ids)
    pl.semaphore_wait(barrier, chips)

    def rows(start, size):
        return pl.ds(pl.multiple_of(start, band), size)

    mine = rows(core * half, half)
    theirs = rows((1 - core) * half, half)
    copy = pltpu.make_async_remote_copy(
        src_ref=x_ref.at[:, theirs, :], dst_ref=recv_a, send_sem=sems.at[0, 0], recv_sem=sems.at[1, 0],
        device_id=(leaf, partner, c), device_id_type=mesh_ids,
    )
    copy.start()
    copy.wait_recv()
    copy.wait_send()
    recv_a[...] = recv_a[...] + x_ref[:, mine, :]

    sends = []
    for d in range(1, chips):
        target = lax.rem(chip + d, chips)
        copy = pltpu.make_async_remote_copy(
            src_ref=recv_a.at[:, rows(target * band, band), :], dst_ref=recv_b.at[d - 1],
            send_sem=sems.at[0, d], recv_sem=sems.at[1, d],
            device_id=(leaf, 2 * target + core, c), device_id_type=mesh_ids,
        )
        copy.start()
        sends.append(copy)
    for copy in sends:
        copy.wait_recv()
    for copy in sends:
        copy.wait_send()
    total = recv_a[:, rows(chip * band, band), :]
    for d in range(1, chips):
        total = total + recv_b[d - 1]
    own = rows(core * half + chip * band, band)
    out_ref[:, own, :] = total

    sends = []
    for d in range(1, chips):
        target = lax.rem(chip + d, chips)
        copy = pltpu.make_async_remote_copy(
            src_ref=out_ref.at[:, own, :], dst_ref=out_ref.at[:, own, :],
            send_sem=sems.at[2, d - 1], recv_sem=sems.at[3, d - 1],
            device_id=(leaf, 2 * target + core, c), device_id_type=mesh_ids,
        )
        copy.start()
        sends.append(copy)
    for d in range(1, chips):
        source = lax.rem(chip + chips - d, chips)
        part = rows(core * half + source * band, band)
        pltpu.make_async_remote_copy(
            src_ref=out_ref.at[:, part, :], dst_ref=out_ref.at[:, part, :],
            send_sem=sems.at[2, d - 1], recv_sem=sems.at[3, d - 1],
            device_id=(leaf, 2 * source + core, c), device_id_type=mesh_ids,
        ).wait_recv()
    for copy in sends:
        copy.wait_send()

    copy = pltpu.make_async_remote_copy(
        src_ref=out_ref.at[:, mine, :], dst_ref=out_ref.at[:, mine, :],
        send_sem=sems.at[2, chips - 1], recv_sem=sems.at[3, chips - 1],
        device_id=(leaf, partner, c), device_id_type=mesh_ids,
    )
    copy.start()
    pltpu.make_async_remote_copy(
        src_ref=out_ref.at[:, theirs, :], dst_ref=out_ref.at[:, theirs, :],
        send_sem=sems.at[2, chips - 1], recv_sem=sems.at[3, chips - 1],
        device_id=(leaf, partner, c), device_id_type=mesh_ids,
    ).wait_recv()
    copy.wait_send()


def pair_reduce(x, row_count, collective_id):
    lead, total_rows, last = x.shape
    chips = row_count // 2
    band = total_rows // row_count
    vmem = pl.BlockSpec(memory_space=pltpu.VMEM)
    return pl.pallas_call(
        functools.partial(pair_reduce_kernel, band=band, chips=chips),
        out_shape=jax.ShapeDtypeStruct(x.shape, x.dtype),
        in_specs=[vmem],
        out_specs=vmem,
        scratch_shapes=[
            pltpu.VMEM((lead, band * chips, last), x.dtype),
            pltpu.VMEM((chips - 1, lead, band, last), x.dtype),
            pltpu.SemaphoreType.DMA((4, chips)),
        ],
        compiler_params=pltpu.CompilerParams(collective_id=collective_id, has_side_effects=True),
    )(x)


def pair_scatter_kernel(x_ref, out_ref, recv_a, recv_b, sems, *, chips):
    r = lax.axis_index("row")
    leaf = lax.axis_index("leaf")
    c = lax.axis_index("col")
    core = lax.rem(r, 2)
    chip = r // 2
    partner = r + 1 - 2 * core
    mesh_ids = pl.DeviceIdType.MESH
    peers = [2 * lax.rem(chip + d, chips) + core for d in range(1, chips)]

    barrier = pltpu.get_barrier_semaphore()
    for peer in [partner] + peers:
        pl.semaphore_signal(barrier, inc=1, device_id=(leaf, peer, c), device_id_type=mesh_ids)
    pl.semaphore_wait(barrier, chips)

    copy = pltpu.make_async_remote_copy(
        src_ref=x_ref.at[:, :, 1 - core], dst_ref=recv_a, send_sem=sems.at[0, 0], recv_sem=sems.at[1, 0],
        device_id=(leaf, partner, c), device_id_type=mesh_ids,
    )
    copy.start()
    copy.wait_recv()
    copy.wait_send()
    recv_a[...] = recv_a[...] + x_ref[:, :, core]

    sends = []
    for d in range(1, chips):
        target = lax.rem(chip + d, chips)
        copy = pltpu.make_async_remote_copy(
            src_ref=recv_a.at[:, target], dst_ref=recv_b.at[d - 1],
            send_sem=sems.at[0, d], recv_sem=sems.at[1, d],
            device_id=(leaf, 2 * target + core, c), device_id_type=mesh_ids,
        )
        copy.start()
        sends.append(copy)
    for copy in sends:
        copy.wait_recv()
    for copy in sends:
        copy.wait_send()
    total = recv_a[:, chip]
    for d in range(1, chips):
        total = total + recv_b[d - 1]
    out_ref[...] = total


def pair_scatter(x, row_count, collective_id):
    lead, total_rows, last = x.shape
    chips = row_count // 2
    band = total_rows // row_count
    vmem = pl.BlockSpec(memory_space=pltpu.VMEM)
    return pl.pallas_call(
        functools.partial(pair_scatter_kernel, chips=chips),
        out_shape=jax.ShapeDtypeStruct((lead, band, last), x.dtype),
        in_specs=[vmem],
        out_specs=vmem,
        scratch_shapes=[
            pltpu.VMEM((lead, chips, band, last), x.dtype),
            pltpu.VMEM((chips - 1, lead, band, last), x.dtype),
            pltpu.SemaphoreType.DMA((2, chips)),
        ],
        compiler_params=pltpu.CompilerParams(collective_id=collective_id, has_side_effects=True),
    )(x.reshape(lead, chips, 2, band, last))


def body(sigma_top, panels, inverse_diag, slot_lists, parent_links):
    tile = TILE
    row_count = lax.axis_size("row")
    col_count = lax.axis_size("col")
    leaf_count = lax.axis_size("leaf")
    r = lax.axis_index("row")
    c = lax.axis_index("col")
    panel = panels[0]
    inverse = inverse_diag[0]
    picks_all = slot_lists[0]
    parents = parent_links[0]
    nodes = panel.shape[0]
    width = inverse.shape[2]
    own_tiles = width // tile
    slot_count = picks_all.shape[1]
    positions = slot_count + own_tiles
    band = width // row_count

    partial_factor = mm(panel, inverse)
    factor_rows = axis_reduce(partial_factor, "col", col_count, True, 3)
    living = jnp.concatenate([jnp.ones((1, slot_count), jnp.bool_), picks_all >= 0], axis=0)
    live_here = jnp.take(living, r, axis=1).astype(jnp.float32)
    factor_rows = factor_rows * live_here[:, None, None]
    factor_tile = lax.dynamic_slice_in_dim(factor_rows, c * tile, tile, 2)
    factor_cols = lax.all_gather(factor_tile, "row", axis=1, tiled=True)

    inverse_band = lax.dynamic_slice_in_dim(inverse, r * band, band, 2)
    partial_gram = mm(jnp.transpose(inverse_band, (0, 2, 1)), inverse)
    gram_piece = lax.psum_scatter(partial_gram, "col", scatter_dimension=2, tiled=True)

    leaf = lax.axis_index("leaf")
    local_rows = sigma_top.shape[0]
    chunk_rows = lax.all_gather(sigma_top, "col", axis=1, tiled=True)
    chunks_per_tile = tile // local_rows
    rounds = []
    for t in range(chunks_per_tile):
        pairs = []
        for src_leaf in range(leaf_count):
            for src_row in range(row_count):
                q = src_leaf * row_count + src_row
                dst_leaf = (q % chunks_per_tile + t) % leaf_count
                dst_row = q // chunks_per_tile
                for col in range(col_count):
                    pairs.append(
                        ((src_leaf * row_count + src_row) * col_count + col,
                         (dst_leaf * row_count + dst_row) * col_count + col)
                    )
        rounds.append(lax.ppermute(chunk_rows, ("leaf", "row", "col"), pairs))
    order = lax.rem(leaf - jnp.arange(chunks_per_tile, dtype=jnp.int32) + 4 * leaf_count, leaf_count)
    sigma_rows = jnp.take(jnp.stack(rounds), order, axis=0).reshape(tile, -1)

    def diag_partial(first, products):
        rows = factor_rows[first:first + products.shape[0]]
        return mm(jnp.transpose(rows, (0, 2, 1)), products)

    def reduce_and_gather(first, products, sent, extra, tied=None, partial=None):
        count = products.shape[0]
        if partial is None:
            piece = pair_scatter(diag_partial(first, products), row_count, first)
            piece = piece + gram_piece[first:first + count]
        else:
            piece = pair_scatter(partial, row_count, first)
        if tied is not None:
            piece, tied = lax.optimization_barrier((piece, tied))
            tied_out.append(tied)
        both = jnp.concatenate([sent, piece] + extra, axis=1)
        everything = lax.all_gather(both, ("row", "col"), axis=0)
        return everything.reshape(row_count, col_count, count, both.shape[1], tile)

    bands_per_tile = tile // band

    def product_col_t(gathered, node, m):
        tiles = lax.dynamic_index_in_dim(gathered[:, :, :, :tile], m, 1, keepdims=False)
        tiles = lax.dynamic_index_in_dim(tiles, node, 1, keepdims=False)
        return jnp.transpose(tiles, (2, 0, 1)).reshape(tile, -1)

    def product_row(gathered, node, q):
        tiles = lax.dynamic_index_in_dim(gathered[:, :, :, :tile], q, 0, keepdims=False)
        tiles = lax.dynamic_index_in_dim(tiles, node, 1, keepdims=False)
        return jnp.transpose(tiles, (1, 0, 2)).reshape(tile, -1)

    def diag_row(gathered, node, m):
        pieces = lax.dynamic_slice_in_dim(gathered[:, :, :, tile:], m * bands_per_tile, bands_per_tile, 0)
        pieces = lax.dynamic_index_in_dim(pieces, node, 2, keepdims=False)
        return jnp.transpose(pieces, (0, 2, 1, 3)).reshape(tile, -1)

    def diag_col(gathered, m, offset):
        pieces = lax.dynamic_index_in_dim(gathered[:, :, :, offset:offset + band], m, 1, keepdims=False)
        return jnp.transpose(pieces, (1, 0, 2, 3)).reshape(pieces.shape[1], -1, tile)

    own_row = jnp.minimum(r, own_tiles - 1)
    upper = r < own_tiles

    product_0 = mm(sigma_rows, factor_cols[0])
    lifted = [
        mm(sigma_rows, scatter_factor(factor_cols[node], picks_all[node - 1], slot_count, tile))[None]
        for node in (1, 2)
    ]
    tied_out = []
    gathered_0 = reduce_and_gather(0, product_0[None], product_0[None], [], jnp.concatenate(lifted, axis=0))
    lifted_cols = axis_gather(tied_out[0], "row", row_count, 4)

    info_1 = jnp.concatenate(
        [r.astype(jnp.int32)[None], picks_all[0:2].reshape(-1), jnp.zeros((2,), jnp.int32), c.astype(jnp.int32)[None]]
    )
    halves = row_count // own_tiles
    product_1, upper_half, partial_1 = level_products(
        info_1, gathered_0, lifted_cols, factor_cols[1:3], 1, tile, band, own_tiles, slot_count,
        tile, tile, halves, (factor_rows[1:3], gram_piece[1:3]),
    )
    gathered_1 = reduce_and_gather(1, product_1, upper_half, [], partial=partial_1)

    info_2 = jnp.concatenate(
        [r.astype(jnp.int32)[None], picks_all[2:nodes - 1].reshape(-1), (parents - 1).astype(jnp.int32),
         c.astype(jnp.int32)[None]]
    )
    product_2, partial_2 = level_products(
        info_2, gathered_1, gathered_0, factor_cols[3:nodes], 2, tile, band, own_tiles, slot_count,
        tile // halves, tile, 0, (factor_rows[3:nodes], gram_piece[3:nodes]),
    )
    diag_2 = pair_reduce(partial_2, row_count, 2)

    products = jnp.concatenate([product_0[None], product_1, product_2], axis=0)
    diag_cols = jnp.concatenate(
        [diag_col(gathered_0, c, tile), diag_col(gathered_1, c, tile // halves), diag_2], axis=0
    )
    return (-products)[None], diag_cols[None]


def solution(mesh):
    return jax.shard_map(
        body,
        mesh=mesh,
        in_specs=(
            P(("leaf", "row"), "col"),
            P("leaf", None, "row", "col"),
            P("leaf", None, "col", None),
            P("leaf", None, None),
            P("leaf", None),
        ),
        out_specs=(P("leaf", None, "row", "col"), P("leaf", None, None, "col")),
        check_vma=False,
    )
```

```python
import functools

import jax
import jax.numpy as jnp
from jax import lax
from jax.experimental import pallas as pl
from jax.experimental.pallas import tpu as pltpu
from jax.sharding import PartitionSpec as P

TILE = 128
HIGHEST = lax.Precision.HIGHEST


def mm(a, b):
    return jnp.matmul(a, b, precision=HIGHEST, preferred_element_type=jnp.float32)


def tile_rows(matrix, index, tile):
    return lax.dynamic_slice_in_dim(matrix, index * tile, tile, 0)


def tile_cols(matrix, index, tile):
    return lax.dynamic_slice_in_dim(matrix, index * tile, tile, 1)


def scatter_factor(factor_col, slots, positions, tile):
    tiles = factor_col.reshape(slots.shape[0], tile, factor_col.shape[1])
    hits = slots[:, None] == jnp.arange(positions, dtype=slots.dtype)[None, :]
    present = jnp.any(hits, axis=0)
    source = jnp.argmax(hits, axis=0)
    moved = jnp.take(tiles, source, axis=0)
    moved = jnp.where(present[:, None, None], moved, 0.0)
    return moved.reshape(positions * tile, factor_col.shape[1])


def dot_hi(a, b):
    return jnp.dot(a, b, precision=HIGHEST, preferred_element_type=jnp.float32)


def dot_t_hi(a, b):
    return lax.dot_general(
        a, b, (((0,), (0,)), ((), ())), precision=HIGHEST, preferred_element_type=jnp.float32
    )


def level_kernel(info_ref, par_ref, low_ref, fac_ref, *rest, level, tile, band, own_tiles, slot_count,
                 par_prow, low_prow, halves, with_diag):
    extra = ()
    if with_diag:
        extra = (rest[0], rest[1], rest[3])
        rest = (rest[2],) + rest[4:]
    out_ref = rest[0]
    rest = rest[1:]
    count = out_ref.shape[0]
    split = tile // band
    r = info_ref[0]
    col = info_ref[1 + count * slot_count + count]
    own = lax.rem(r, own_tiles)

    def p_tile(ref, prow, node, q, m):
        if prow == tile:
            return ref[q, m, node, 0:tile, :]
        parts = tile // prow
        return jnp.concatenate([ref[q + j * own_tiles, m, node, 0:prow, :] for j in range(parts)], axis=0)

    def d_tile(ref, prow, node, a, m):
        return jnp.concatenate([ref[a * split + h, m, node, prow:prow + band, :] for h in range(split)], axis=0)

    for i in range(count):
        base = 1 + i * slot_count
        parent = info_ref[1 + count * slot_count + i]
        factor = [fac_ref[i, k * tile:(k + 1) * tile, :] for k in range(slot_count)]
        picks = [jnp.clip(info_ref[base + k], 0, slot_count - 1) for k in range(slot_count)]
        source = info_ref[base + jnp.maximum(r, own_tiles)]

        upper = dot_hi(d_tile(par_ref, par_prow, parent, own, 0), factor[0])
        for k in range(1, own_tiles):
            upper += dot_hi(d_tile(par_ref, par_prow, parent, own, k), factor[k])
        for k in range(own_tiles, slot_count):
            pick = picks[k] if par_prow == tile else jnp.minimum(picks[k], own_tiles - 1)
            upper -= dot_t_hi(p_tile(par_ref, par_prow, parent, pick, own), factor[k])

        if halves:
            half_ref = rest[0]
            rows = tile // halves
            which = r // own_tiles
            half = upper[0:rows]
            for j in range(1, halves):
                half = jnp.where(which == j, upper[j * rows:(j + 1) * rows], half)
            half_ref[i] = half

        @pl.when(r < own_tiles)
        def _():
            out_ref[i] = upper

        @pl.when(jnp.logical_and(r >= own_tiles, source >= 0))
        def _():
            if level == 1:
                s = jnp.clip(source, 0, slot_count - 1)
                acc = low_ref[i, pl.ds(pl.multiple_of(s * tile, tile), tile), :]
                for k in range(own_tiles):
                    acc -= dot_hi(p_tile(par_ref, par_prow, parent, s, k), factor[k])
            else:
                s = jnp.clip(source, 0, own_tiles - 1)
                acc = -dot_hi(p_tile(par_ref, par_prow, parent, s, 0), factor[0])
                for k in range(1, own_tiles):
                    acc -= dot_hi(p_tile(par_ref, par_prow, parent, s, k), factor[k])
                for k in range(own_tiles, slot_count):
                    q = jnp.minimum(picks[k], own_tiles - 1)
                    acc += dot_hi(d_tile(low_ref, low_prow, 0, s, q), factor[k])
            out_ref[i] = acc

        @pl.when(jnp.logical_and(r >= own_tiles, source < 0))
        def _():
            out_ref[i] = jnp.zeros((tile, tile), jnp.float32)

        if extra:
            rows_ref, gram_ref, diag_ref = extra
            diag_ref[i] = dot_t_hi(rows_ref[i], out_ref[i])
            start = pl.multiple_of(r * band, band)
            diag_ref[i, pl.ds(start, band), :] = diag_ref[i, pl.ds(start, band), :] + gram_ref[i]


def level_products(info, parent_data, low_data, factors, level, tile, band, own_tiles, slot_count,
                   par_prow, low_prow, halves, diag_inputs=()):
    kernel = functools.partial(
        level_kernel, level=level, tile=tile, band=band, own_tiles=own_tiles, slot_count=slot_count,
        par_prow=par_prow, low_prow=low_prow, halves=halves, with_diag=bool(diag_inputs),
    )
    vmem = pl.BlockSpec(memory_space=pltpu.VMEM)
    count = factors.shape[0]
    shapes = [jax.ShapeDtypeStruct((count, tile, tile), jnp.float32)]
    if halves:
        shapes.append(jax.ShapeDtypeStruct((count, tile // halves, tile), jnp.float32))
    if diag_inputs:
        width = diag_inputs[0].shape[2]
        shapes.append(jax.ShapeDtypeStruct((count, width, tile), jnp.float32))
    return pl.pallas_call(
        kernel,
        out_shape=tuple(shapes),
        in_specs=[pl.BlockSpec(memory_space=pltpu.SMEM)] + [vmem] * (3 + len(diag_inputs)),
        out_specs=tuple([vmem] * len(shapes)),
    )(info, parent_data, low_data, factors, *diag_inputs)


def reduce_kernel(x_ref, out_ref, recv_ref, send_sem, recv_sem, back_send, back_recv, *, axis, count, band, gather):
    me = lax.axis_index(axis)
    ids = {name: lax.axis_index(name) for name in ("leaf", "row", "col")}

    def device(peer):
        where = dict(ids)
        where[axis] = peer
        return (where["leaf"], where["row"], where["col"])

    mesh_ids = pl.DeviceIdType.MESH
    barrier = pltpu.get_barrier_semaphore()
    for d in range(1, count):
        pl.semaphore_signal(barrier, inc=1, device_id=device(lax.rem(me + d, count)), device_id_type=mesh_ids)
    pl.semaphore_wait(barrier, count - 1)

    sends = []
    for d in range(1, count):
        peer = lax.rem(me + d, count)
        copy = pltpu.make_async_remote_copy(
            src_ref=x_ref.at[:, pl.ds(pl.multiple_of(peer * band, band), band), :],
            dst_ref=recv_ref.at[d - 1],
            send_sem=send_sem.at[d - 1],
            recv_sem=recv_sem.at[d - 1],
            device_id=device(peer),
            device_id_type=mesh_ids,
        )
        copy.start()
        sends.append(copy)
    for copy in sends:
        copy.wait_recv()
    for copy in sends:
        copy.wait_send()
    own = pl.ds(pl.multiple_of(me * band, band), band)
    total = x_ref[:, own, :]
    for d in range(1, count):
        total = total + recv_ref[d - 1]
    if not gather:
        out_ref[...] = total
        return
    out_ref[:, own, :] = total
    backs = []
    for d in range(1, count):
        peer = lax.rem(me + d, count)
        copy = pltpu.make_async_remote_copy(
            src_ref=out_ref.at[:, own, :],
            dst_ref=out_ref.at[:, own, :],
            send_sem=back_send.at[d - 1],
            recv_sem=back_recv.at[d - 1],
            device_id=device(peer),
            device_id_type=mesh_ids,
        )
        copy.start()
        backs.append(copy)
    for d in range(1, count):
        source = lax.rem(me + count - d, count)
        part = pl.ds(pl.multiple_of(source * band, band), band)
        pltpu.make_async_remote_copy(
            src_ref=out_ref.at[:, part, :],
            dst_ref=out_ref.at[:, part, :],
            send_sem=back_send.at[d - 1],
            recv_sem=back_recv.at[d - 1],
            device_id=device(source),
            device_id_type=mesh_ids,
        ).wait_recv()
    for copy in backs:
        copy.wait_send()


def axis_reduce(x, axis, count, gather, collective_id):
    lead, rows, last = x.shape
    band = rows // count
    kernel = functools.partial(reduce_kernel, axis=axis, count=count, band=band, gather=gather)
    out_rows = rows if gather else band
    vmem = pl.BlockSpec(memory_space=pltpu.VMEM)
    return pl.pallas_call(
        kernel,
        out_shape=jax.ShapeDtypeStruct((lead, out_rows, last), x.dtype),
        in_specs=[vmem],
        out_specs=vmem,
        scratch_shapes=[
            pltpu.VMEM((count - 1, lead, band, last), x.dtype),
            pltpu.SemaphoreType.DMA((count - 1,)),
            pltpu.SemaphoreType.DMA((count - 1,)),
            pltpu.SemaphoreType.DMA((count - 1,)),
            pltpu.SemaphoreType.DMA((count - 1,)),
        ],
        compiler_params=pltpu.CompilerParams(collective_id=collective_id, has_side_effects=True),
    )(x)


def gather_kernel(x_ref, out_ref, send_sem, recv_sem, *, axis, count, band):
    me = lax.axis_index(axis)
    ids = {name: lax.axis_index(name) for name in ("leaf", "row", "col")}

    def device(peer):
        where = dict(ids)
        where[axis] = peer
        return (where["leaf"], where["row"], where["col"])

    mesh_ids = pl.DeviceIdType.MESH
    barrier = pltpu.get_barrier_semaphore()
    for d in range(1, count):
        pl.semaphore_signal(barrier, inc=1, device_id=device(lax.rem(me + d, count)), device_id_type=mesh_ids)
    pl.semaphore_wait(barrier, count - 1)
    own = pl.ds(pl.multiple_of(me * band, band), band)
    sends = []
    for d in range(1, count):
        peer = lax.rem(me + d, count)
        copy = pltpu.make_async_remote_copy(
            src_ref=x_ref,
            dst_ref=out_ref.at[:, own, :],
            send_sem=send_sem.at[d - 1],
            recv_sem=recv_sem.at[d - 1],
            device_id=device(peer),
            device_id_type=mesh_ids,
        )
        copy.start()
        sends.append(copy)
    out_ref[:, own, :] = x_ref[...]
    for d in range(1, count):
        source = lax.rem(me + count - d, count)
        part = pl.ds(pl.multiple_of(source * band, band), band)
        pltpu.make_async_remote_copy(
            src_ref=x_ref,
            dst_ref=out_ref.at[:, part, :],
            send_sem=send_sem.at[d - 1],
            recv_sem=recv_sem.at[d - 1],
            device_id=device(source),
            device_id_type=mesh_ids,
        ).wait_recv()
    for copy in sends:
        copy.wait_send()


def axis_gather(x, axis, count, collective_id):
    lead, band, last = x.shape
    vmem = pl.BlockSpec(memory_space=pltpu.VMEM)
    return pl.pallas_call(
        functools.partial(gather_kernel, axis=axis, count=count, band=band),
        out_shape=jax.ShapeDtypeStruct((lead, band * count, last), x.dtype),
        in_specs=[vmem],
        out_specs=vmem,
        scratch_shapes=[pltpu.SemaphoreType.DMA((count - 1,)), pltpu.SemaphoreType.DMA((count - 1,))],
        compiler_params=pltpu.CompilerParams(collective_id=collective_id, has_side_effects=True),
    )(x)


def pair_reduce_kernel(x_ref, out_ref, recv_a, recv_b, sems, *, band, chips):
    r = lax.axis_index("row")
    leaf = lax.axis_index("leaf")
    c = lax.axis_index("col")
    core = lax.rem(r, 2)
    chip = r // 2
    partner = r + 1 - 2 * core
    half = band * chips
    mesh_ids = pl.DeviceIdType.MESH
    peers = [2 * lax.rem(chip + d, chips) + core for d in range(1, chips)]

    barrier = pltpu.get_barrier_semaphore()
    for peer in [partner] + peers:
        pl.semaphore_signal(barrier, inc=1, device_id=(leaf, peer, c), device_id_type=mesh_ids)
    pl.semaphore_wait(barrier, chips)

    def rows(start, size):
        return pl.ds(pl.multiple_of(start, band), size)

    mine = rows(core * half, half)
    theirs = rows((1 - core) * half, half)
    copy = pltpu.make_async_remote_copy(
        src_ref=x_ref.at[:, theirs, :], dst_ref=recv_a, send_sem=sems.at[0, 0], recv_sem=sems.at[1, 0],
        device_id=(leaf, partner, c), device_id_type=mesh_ids,
    )
    copy.start()
    copy.wait_recv()
    copy.wait_send()
    recv_a[...] = recv_a[...] + x_ref[:, mine, :]

    sends = []
    for d in range(1, chips):
        target = lax.rem(chip + d, chips)
        copy = pltpu.make_async_remote_copy(
            src_ref=recv_a.at[:, rows(target * band, band), :], dst_ref=recv_b.at[d - 1],
            send_sem=sems.at[0, d], recv_sem=sems.at[1, d],
            device_id=(leaf, 2 * target + core, c), device_id_type=mesh_ids,
        )
        copy.start()
        sends.append(copy)
    for copy in sends:
        copy.wait_recv()
    for copy in sends:
        copy.wait_send()
    total = recv_a[:, rows(chip * band, band), :]
    for d in range(1, chips):
        total = total + recv_b[d - 1]
    own = rows(core * half + chip * band, band)
    out_ref[:, own, :] = total

    sends = []
    for d in range(1, chips):
        target = lax.rem(chip + d, chips)
        copy = pltpu.make_async_remote_copy(
            src_ref=out_ref.at[:, own, :], dst_ref=out_ref.at[:, own, :],
            send_sem=sems.at[2, d - 1], recv_sem=sems.at[3, d - 1],
            device_id=(leaf, 2 * target + core, c), device_id_type=mesh_ids,
        )
        copy.start()
        sends.append(copy)
    for d in range(1, chips):
        source = lax.rem(chip + chips - d, chips)
        part = rows(core * half + source * band, band)
        pltpu.make_async_remote_copy(
            src_ref=out_ref.at[:, part, :], dst_ref=out_ref.at[:, part, :],
            send_sem=sems.at[2, d - 1], recv_sem=sems.at[3, d - 1],
            device_id=(leaf, 2 * source + core, c), device_id_type=mesh_ids,
        ).wait_recv()
    for copy in sends:
        copy.wait_send()

    copy = pltpu.make_async_remote_copy(
        src_ref=out_ref.at[:, mine, :], dst_ref=out_ref.at[:, mine, :],
        send_sem=sems.at[2, chips - 1], recv_sem=sems.at[3, chips - 1],
        device_id=(leaf, partner, c), device_id_type=mesh_ids,
    )
    copy.start()
    pltpu.make_async_remote_copy(
        src_ref=out_ref.at[:, theirs, :], dst_ref=out_ref.at[:, theirs, :],
        send_sem=sems.at[2, chips - 1], recv_sem=sems.at[3, chips - 1],
        device_id=(leaf, partner, c), device_id_type=mesh_ids,
    ).wait_recv()
    copy.wait_send()


def pair_reduce(x, row_count, collective_id):
    lead, total_rows, last = x.shape
    chips = row_count // 2
    band = total_rows // row_count
    vmem = pl.BlockSpec(memory_space=pltpu.VMEM)
    return pl.pallas_call(
        functools.partial(pair_reduce_kernel, band=band, chips=chips),
        out_shape=jax.ShapeDtypeStruct(x.shape, x.dtype),
        in_specs=[vmem],
        out_specs=vmem,
        scratch_shapes=[
            pltpu.VMEM((lead, band * chips, last), x.dtype),
            pltpu.VMEM((chips - 1, lead, band, last), x.dtype),
            pltpu.SemaphoreType.DMA((4, chips)),
        ],
        compiler_params=pltpu.CompilerParams(collective_id=collective_id, has_side_effects=True),
    )(x)


def pair_scatter_kernel(x_ref, out_ref, recv_a, recv_b, sems, *, chips):
    r = lax.axis_index("row")
    leaf = lax.axis_index("leaf")
    c = lax.axis_index("col")
    core = lax.rem(r, 2)
    chip = r // 2
    partner = r + 1 - 2 * core
    mesh_ids = pl.DeviceIdType.MESH
    peers = [2 * lax.rem(chip + d, chips) + core for d in range(1, chips)]

    barrier = pltpu.get_barrier_semaphore()
    for peer in [partner] + peers:
        pl.semaphore_signal(barrier, inc=1, device_id=(leaf, peer, c), device_id_type=mesh_ids)
    pl.semaphore_wait(barrier, chips)

    copy = pltpu.make_async_remote_copy(
        src_ref=x_ref.at[:, :, 1 - core], dst_ref=recv_a, send_sem=sems.at[0, 0], recv_sem=sems.at[1, 0],
        device_id=(leaf, partner, c), device_id_type=mesh_ids,
    )
    copy.start()
    copy.wait_recv()
    copy.wait_send()
    recv_a[...] = recv_a[...] + x_ref[:, :, core]

    sends = []
    for d in range(1, chips):
        target = lax.rem(chip + d, chips)
        copy = pltpu.make_async_remote_copy(
            src_ref=recv_a.at[:, target], dst_ref=recv_b.at[d - 1],
            send_sem=sems.at[0, d], recv_sem=sems.at[1, d],
            device_id=(leaf, 2 * target + core, c), device_id_type=mesh_ids,
        )
        copy.start()
        sends.append(copy)
    for copy in sends:
        copy.wait_recv()
    for copy in sends:
        copy.wait_send()
    total = recv_a[:, chip]
    for d in range(1, chips):
        total = total + recv_b[d - 1]
    out_ref[...] = total


def pair_scatter(x, row_count, collective_id):
    lead, total_rows, last = x.shape
    chips = row_count // 2
    band = total_rows // row_count
    vmem = pl.BlockSpec(memory_space=pltpu.VMEM)
    return pl.pallas_call(
        functools.partial(pair_scatter_kernel, chips=chips),
        out_shape=jax.ShapeDtypeStruct((lead, band, last), x.dtype),
        in_specs=[vmem],
        out_specs=vmem,
        scratch_shapes=[
            pltpu.VMEM((lead, chips, band, last), x.dtype),
            pltpu.VMEM((chips - 1, lead, band, last), x.dtype),
            pltpu.SemaphoreType.DMA((2, chips)),
        ],
        compiler_params=pltpu.CompilerParams(collective_id=collective_id, has_side_effects=True),
    )(x.reshape(lead, chips, 2, band, last))


def pair_gather_kernel(x_ref, out_ref, sems, *, chips, rows):
    r = lax.axis_index("row")
    leaf = lax.axis_index("leaf")
    c = lax.axis_index("col")
    core = lax.rem(r, 2)
    chip = r // 2
    partner = r + 1 - 2 * core
    mesh_ids = pl.DeviceIdType.MESH

    def at(index):
        return out_ref.at[:, pl.ds(pl.multiple_of(index * rows, rows), rows), :]

    barrier = pltpu.get_barrier_semaphore()
    pl.semaphore_signal(barrier, inc=1, device_id=(leaf, partner, c), device_id_type=mesh_ids)
    for d in range(1, chips):
        peer = 2 * lax.rem(chip + d, chips) + core
        pl.semaphore_signal(barrier, inc=1, device_id=(leaf, peer, c), device_id_type=mesh_ids)
    pl.semaphore_wait(barrier, chips)

    sends = []
    copy = pltpu.make_async_remote_copy(
        src_ref=x_ref, dst_ref=at(r), send_sem=sems.at[0, 0], recv_sem=sems.at[1, 0],
        device_id=(leaf, partner, c), device_id_type=mesh_ids,
    )
    copy.start()
    sends.append(copy)
    for d in range(1, chips):
        peer = 2 * lax.rem(chip + d, chips) + core
        copy = pltpu.make_async_remote_copy(
            src_ref=x_ref, dst_ref=at(r), send_sem=sems.at[0, d], recv_sem=sems.at[1, d],
            device_id=(leaf, peer, c), device_id_type=mesh_ids,
        )
        copy.start()
        sends.append(copy)
    out_ref[:, pl.ds(pl.multiple_of(r * rows, rows), rows), :] = x_ref[...]
    for d in range(1, chips):
        source = 2 * lax.rem(chip + chips - d, chips) + core
        pltpu.make_async_remote_copy(
            src_ref=x_ref, dst_ref=at(source), send_sem=sems.at[0, d], recv_sem=sems.at[1, d],
            device_id=(leaf, source, c), device_id_type=mesh_ids,
        ).wait_recv()
        copy = pltpu.make_async_remote_copy(
            src_ref=at(source), dst_ref=at(source), send_sem=sems.at[0, chips + d - 1],
            recv_sem=sems.at[1, chips + d - 1], device_id=(leaf, partner, c), device_id_type=mesh_ids,
        )
        copy.start()
        sends.append(copy)
    pltpu.make_async_remote_copy(
        src_ref=x_ref, dst_ref=at(partner), send_sem=sems.at[0, 0], recv_sem=sems.at[1, 0],
        device_id=(leaf, partner, c), device_id_type=mesh_ids,
    ).wait_recv()
    for d in range(1, chips):
        source = 2 * lax.rem(chip + chips - d, chips) + 1 - core
        pltpu.make_async_remote_copy(
            src_ref=at(source), dst_ref=at(source), send_sem=sems.at[0, chips + d - 1],
            recv_sem=sems.at[1, chips + d - 1], device_id=(leaf, partner, c), device_id_type=mesh_ids,
        ).wait_recv()
    for copy in sends:
        copy.wait_send()


def pair_gather(x, row_count, collective_id):
    lead, rows, last = x.shape
    chips = row_count // 2
    vmem = pl.BlockSpec(memory_space=pltpu.VMEM)
    return pl.pallas_call(
        functools.partial(pair_gather_kernel, chips=chips, rows=rows),
        out_shape=jax.ShapeDtypeStruct((lead, rows * row_count, last), x.dtype),
        in_specs=[vmem],
        out_specs=vmem,
        scratch_shapes=[pltpu.SemaphoreType.DMA((2, 2 * chips - 1))],
        compiler_params=pltpu.CompilerParams(collective_id=collective_id, has_side_effects=True),
    )(x)


def body(sigma_top, panels, inverse_diag, slot_lists, parent_links):
    tile = TILE
    row_count = lax.axis_size("row")
    col_count = lax.axis_size("col")
    leaf_count = lax.axis_size("leaf")
    r = lax.axis_index("row")
    c = lax.axis_index("col")
    panel = panels[0]
    inverse = inverse_diag[0]
    picks_all = slot_lists[0]
    parents = parent_links[0]
    nodes = panel.shape[0]
    width = inverse.shape[2]
    own_tiles = width // tile
    slot_count = picks_all.shape[1]
    positions = slot_count + own_tiles
    band = width // row_count

    partial_factor = mm(panel, inverse)
    factor_rows = axis_reduce(partial_factor, "col", col_count, True, 3)
    living = jnp.concatenate([jnp.ones((1, slot_count), jnp.bool_), picks_all >= 0], axis=0)
    live_here = jnp.take(living, r, axis=1).astype(jnp.float32)
    factor_rows = factor_rows * live_here[:, None, None]
    factor_tile = lax.dynamic_slice_in_dim(factor_rows, c * tile, tile, 2)
    factor_cols = lax.all_gather(factor_tile, "row", axis=1, tiled=True)

    inverse_band = lax.dynamic_slice_in_dim(inverse, r * band, band, 2)
    partial_gram = mm(jnp.transpose(inverse_band, (0, 2, 1)), inverse)
    gram_piece = lax.psum_scatter(partial_gram, "col", scatter_dimension=2, tiled=True)

    leaf = lax.axis_index("leaf")
    local_rows = sigma_top.shape[0]
    chunk_rows = lax.all_gather(sigma_top, "col", axis=1, tiled=True)
    chunks_per_tile = tile // local_rows
    rounds = []
    for t in range(chunks_per_tile):
        pairs = []
        for src_leaf in range(leaf_count):
            for src_row in range(row_count):
                q = src_leaf * row_count + src_row
                dst_leaf = (q % chunks_per_tile + t) % leaf_count
                dst_row = q // chunks_per_tile
                for col in range(col_count):
                    pairs.append(
                        ((src_leaf * row_count + src_row) * col_count + col,
                         (dst_leaf * row_count + dst_row) * col_count + col)
                    )
        rounds.append(lax.ppermute(chunk_rows, ("leaf", "row", "col"), pairs))
    order = lax.rem(leaf - jnp.arange(chunks_per_tile, dtype=jnp.int32) + 4 * leaf_count, leaf_count)
    sigma_rows = jnp.take(jnp.stack(rounds), order, axis=0).reshape(tile, -1)

    def diag_partial(first, products):
        rows = factor_rows[first:first + products.shape[0]]
        return mm(jnp.transpose(rows, (0, 2, 1)), products)

    def reduce_and_gather(first, products, sent, extra, tied=None):
        count = products.shape[0]
        piece = pair_scatter(diag_partial(first, products), row_count, first)
        piece = piece + gram_piece[first:first + count]
        if tied is not None:
            piece, tied = lax.optimization_barrier((piece, tied))
            tied_out.append(tied)
        both = jnp.concatenate([sent, piece] + extra, axis=1)
        everything = lax.all_gather(both, ("row", "col"), axis=0)
        return everything.reshape(row_count, col_count, count, both.shape[1], tile)

    bands_per_tile = tile // band

    def product_col_t(gathered, node, m):
        tiles = lax.dynamic_index_in_dim(gathered[:, :, :, :tile], m, 1, keepdims=False)
        tiles = lax.dynamic_index_in_dim(tiles, node, 1, keepdims=False)
        return jnp.transpose(tiles, (2, 0, 1)).reshape(tile, -1)

    def product_row(gathered, node, q):
        tiles = lax.dynamic_index_in_dim(gathered[:, :, :, :tile], q, 0, keepdims=False)
        tiles = lax.dynamic_index_in_dim(tiles, node, 1, keepdims=False)
        return jnp.transpose(tiles, (1, 0, 2)).reshape(tile, -1)

    def diag_row(gathered, node, m):
        pieces = lax.dynamic_slice_in_dim(gathered[:, :, :, tile:], m * bands_per_tile, bands_per_tile, 0)
        pieces = lax.dynamic_index_in_dim(pieces, node, 2, keepdims=False)
        return jnp.transpose(pieces, (0, 2, 1, 3)).reshape(tile, -1)

    def diag_col(gathered, m, offset):
        pieces = lax.dynamic_index_in_dim(gathered[:, :, :, offset:offset + band], m, 1, keepdims=False)
        return jnp.transpose(pieces, (1, 0, 2, 3)).reshape(pieces.shape[1], -1, tile)

    own_row = jnp.minimum(r, own_tiles - 1)
    upper = r < own_tiles

    product_0 = mm(sigma_rows, factor_cols[0])
    lifted = [
        mm(sigma_rows, scatter_factor(factor_cols[node], picks_all[node - 1], slot_count, tile))[None]
        for node in (1, 2)
    ]
    tied_out = []
    gathered_0 = reduce_and_gather(0, product_0[None], product_0[None], [], jnp.concatenate(lifted, axis=0))
    lifted_cols = pair_gather(tied_out[0], row_count, 4)

    info_1 = jnp.concatenate(
        [r.astype(jnp.int32)[None], picks_all[0:2].reshape(-1), jnp.zeros((2,), jnp.int32), c.astype(jnp.int32)[None]]
    )
    halves = row_count // own_tiles
    product_1, upper_half = level_products(
        info_1, gathered_0, lifted_cols, factor_cols[1:3], 1, tile, band, own_tiles, slot_count,
        tile, tile, halves,
    )
    gathered_1 = reduce_and_gather(1, product_1, upper_half, [])

    info_2 = jnp.concatenate(
        [r.astype(jnp.int32)[None], picks_all[2:nodes - 1].reshape(-1), (parents - 1).astype(jnp.int32),
         c.astype(jnp.int32)[None]]
    )
    product_2, partial_2 = level_products(
        info_2, gathered_1, gathered_0, factor_cols[3:nodes], 2, tile, band, own_tiles, slot_count,
        tile // halves, tile, 0, (factor_rows[3:nodes], gram_piece[3:nodes]),
    )
    diag_2 = pair_reduce(partial_2, row_count, 2)

    products = jnp.concatenate([product_0[None], product_1, product_2], axis=0)
    diag_cols = jnp.concatenate(
        [diag_col(gathered_0, c, tile), diag_col(gathered_1, c, tile // halves), diag_2], axis=0
    )
    return (-products)[None], diag_cols[None]


def solution(mesh):
    return jax.shard_map(
        body,
        mesh=mesh,
        in_specs=(
            P(("leaf", "row"), "col"),
            P("leaf", None, "row", "col"),
            P("leaf", None, "col", None),
            P("leaf", None, None),
            P("leaf", None),
        ),
        out_specs=(P("leaf", None, "row", "col"), P("leaf", None, None, "col")),
        check_vma=False,
    )
```
